256 devices in a mesh: tile: 256 (over z, y, x, core).
Axes of the slice: x: 4, y: 4, z: 8, core: 2. Of those that a mesh axis runs over, the one named last changes fastest.
Arguments:
- adjoint_zonal: bfloat16 [32, 8, 4096, 128], P(None, None, 'tile'), may hold values from -70 to 70
- adjoint_meridional: bfloat16 [32, 8, 4096, 128], P(None, None, 'tile'), may hold values from -70 to 70
- cell_fraction: bfloat16 [8, 4096, 128], P(None, 'tile'), may hold values from 0.19921875 to 1
- level_thickness: float32 [8], replicated, may hold values from 0.5 to 2
- land_mask: int32 [4096, 128], P('tile'), may hold values 0 or 1
- edge_codes: int32 [256, 4], P('tile'), may hold values from 0 to 1, as said below
Outputs:
- surface_adjoint: float32 [32, 4096, 128], P(None, 'tile')
- residual: float32 [32, 4096, 128], P(None, 'tile')
The draws below stay inside these ranges and needn't reach their ends.
Inputs may be any that keep to these rules, and one draw needn't show every extreme that they name: edge_codes[t, 1] equals edge_codes[t - 1, 0] and edge_codes[t, 3] equals edge_codes[t - 16, 2], tile numbers taken modulo 256.
All inputs are finite; a program needn't handle non-finite values. No bound on the sum of `land_mask` on one device may be relied on, other than what follows from the above.
Results may differ from the reference program's by a relative error of at most 0.0003.
Values may be sent and summed in bfloat16 or wider, within the bound.
A program may use at most 64 MiB of HBM per device.

```python
import math
from functools import partial
import jax
import jax.numpy as jnp
from jax import lax

TY = 16
TX = 128
MEMB = 32
LEV = 8
NTX = 16
ITERS = 4
ROWS = 4096
N_TILE = 256


def adjoint_field(key, salt):
    folded = jax.random.fold_in(key, salt)
    key_set = jax.random.split(folded, 3)
    row_scale = jnp.exp(jax.random.uniform(key_set[0], (ROWS,), jnp.float32, 0.0, math.log(3.2)))
    col_scale = jnp.exp(jax.random.uniform(key_set[1], (TX,), jnp.float32, 0.0, math.log(3.2)))
    tile_of_row = (jnp.arange(ROWS) // TY).astype(jnp.float32)
    tile_factor = 3.0 ** (tile_of_row / max(N_TILE - 1, 1))
    scaling = 0.25 * (row_scale * tile_factor)[:, None] * col_scale[None, :]
    jitter = jnp.clip(jax.random.normal(key_set[2], (MEMB, LEV, ROWS, TX), jnp.float32), -6.0, 6.0)
    values = jitter * scaling
    return values.astype(jnp.bfloat16)


def draw_adjoint_zonal(key, part):
    return adjoint_field(key, 11)


def draw_adjoint_meridional(key, part):
    return adjoint_field(key, 23)


def draw_edge_codes(key, part):
    key_pair = jax.random.split(jax.random.fold_in(key, 37), 2)
    east_flip = jax.random.randint(key_pair[0], (N_TILE,), 0, 2).astype(jnp.int32)
    north_flip = jax.random.randint(key_pair[1], (N_TILE,), 0, 2).astype(jnp.int32)
    return jnp.stack([east_flip, jnp.roll(east_flip, 1), north_flip, jnp.roll(north_flip, NTX)], axis=1).astype(jnp.int32)


def touch_ends(result, key, least, largest):
    dims = result.shape
    place = [jax.random.randint(jax.random.fold_in(key, axis), (), 0, dims[axis]) for axis in range(len(dims))]
    result = result.at[tuple(place)].set(least)
    longest = dims.index(max(dims))
    place[longest] = (place[longest] + 1) % dims[longest]
    return result.at[tuple(place)].set(largest)


def steps_of(stream_key, extent, shards, least, largest):
    def one(position, blocks):
        steps = jax.random.uniform(jax.random.fold_in(jax.random.fold_in(stream_key, 6), position), (blocks,), jnp.float32, least / len(shards), largest / len(shards))
        return jnp.repeat(jnp.exp(steps), extent[position] // blocks).reshape((-1,) + (1,) * (len(extent) - position - 1))

    factor_of = one(*shards[0])
    for cut in shards[1:]:
        factor_of = factor_of * one(*cut)
    return factor_of


def setup_inputs(seed: int = 0) -> dict:
    arg_keys = jax.random.split(jax.random.key(seed), 7)
    return {
        "adjoint_zonal": draw_adjoint_zonal(jax.random.fold_in(arg_keys[6], 71), 0),
        "adjoint_meridional": draw_adjoint_meridional(jax.random.fold_in(arg_keys[6], 71), 0),
        "cell_fraction": jnp.clip(0.19921875 + 0.80078125 * jax.random.uniform(arg_keys[2], (LEV, ROWS, TX), jnp.float32) ** steps_of(arg_keys[2], (LEV, ROWS, TX), ((1, 256),), -0.2, 0.2), 0.19921875, 1.0).astype(jnp.bfloat16),
        "level_thickness": jnp.clip(jnp.exp(jax.random.uniform(arg_keys[3], (LEV,), jnp.float32, math.log(0.5), math.log(2.0))), 0.5, 2.0),
        "land_mask": touch_ends((jax.random.randint(arg_keys[4], (ROWS, TX), 0, 5) < 4).astype(jnp.int32), jax.random.fold_in(arg_keys[4], 1), 0, 1),
        "edge_codes": draw_edge_codes(jax.random.fold_in(arg_keys[6], 71), 0),
    }


storage_coef = 1.0
coupling_coef = 0.25

def reverse_where(edge_values, reverse_flag):
    return jnp.where(reverse_flag == 1, jnp.flip(edge_values, -1), edge_values)

def attach(field_now, east_edge, west_edge, north_edge, south_edge):
    east_full = jnp.concatenate([field_now[..., 1:], east_edge[..., None]], axis=-1)
    west_full = jnp.concatenate([west_edge[..., None], field_now[..., :-1]], axis=-1)
    north_full = jnp.concatenate([field_now[..., 1:, :], north_edge[..., None, :]], axis=-2)
    south_full = jnp.concatenate([south_edge[..., None, :], field_now[..., :-1, :]], axis=-2)
    return (east_full, west_full, north_full, south_full)

def neighbour_fields(field_now, link_codes):
    east_edge = reverse_where(jnp.roll(field_now[..., :, 0], -1, axis=-2), link_codes[:, 0:1])
    west_edge = reverse_where(jnp.roll(field_now[..., :, -1], 1, axis=-2), link_codes[:, 1:2])
    north_edge = reverse_where(jnp.roll(field_now[..., 0, :], -NTX, axis=-2), link_codes[:, 2:3])
    south_edge = reverse_where(jnp.roll(field_now[..., -1, :], NTX, axis=-2), link_codes[:, 3:4])
    return attach(field_now, east_edge, west_edge, north_edge, south_edge)

def column_sum(values, fraction, thickness):
    running = thickness[0] * fraction[0].astype(jnp.float32) * values[:, 0].astype(jnp.float32)
    for level_index in range(1, values.shape[1]):
        running = running + thickness[level_index] * fraction[level_index].astype(jnp.float32) * values[:, level_index].astype(jnp.float32)
    return running

def column_depth(fraction, thickness, wet_cells):
    running = thickness[0] * fraction[0].astype(jnp.float32)
    for level_index in range(1, fraction.shape[0]):
        running = running + thickness[level_index] * fraction[level_index].astype(jnp.float32)
    return wet_cells * running

def apply_operator(field_now, diagonal, weights, neighbours):
    east_full, west_full, north_full, south_full = neighbours(field_now)
    return diagonal * field_now + weights[0] * (field_now - east_full) + weights[1] * (field_now - west_full) + weights[2] * (field_now - north_full) + weights[3] * (field_now - south_full)

def member_sum(first_field, second_field):
    return lax.optimization_barrier(jnp.sum(first_field * second_field, axis=(1, 2, 3)))

def widen(member_values):
    return member_values[:, None, None, None]

def reference(adjoint_zonal, adjoint_meridional, cell_fraction, level_thickness, land_mask, edge_codes):
    members = adjoint_zonal.shape[0]
    levels = adjoint_zonal.shape[1]
    zonal_tiles = adjoint_zonal.reshape(members, levels, N_TILE, TY, TX)
    meridional_tiles = adjoint_meridional.reshape(members, levels, N_TILE, TY, TX)
    fraction_tiles = cell_fraction.reshape(levels, N_TILE, TY, TX)
    wet_cells = land_mask.astype(jnp.float32).reshape(N_TILE, TY, TX)
    neighbours = partial(neighbour_fields, link_codes=edge_codes)
    water_depth = column_depth(fraction_tiles, level_thickness, wet_cells)
    transport_u = column_sum(zonal_tiles, fraction_tiles, level_thickness)
    transport_v = column_sum(meridional_tiles, fraction_tiles, level_thickness)
    east_transport = neighbours(transport_u)[0]
    north_transport = neighbours(transport_v)[2]
    right_side = wet_cells * (transport_u - east_transport + transport_v - north_transport)
    depth_east, depth_west, depth_north, depth_south = neighbours(water_depth)
    weights = (coupling_coef * jnp.sqrt(water_depth * depth_east), coupling_coef * jnp.sqrt(water_depth * depth_west), coupling_coef * jnp.sqrt(water_depth * depth_north), coupling_coef * jnp.sqrt(water_depth * depth_south))
    diagonal = storage_coef * wet_cells + (1.0 - wet_cells)
    solution = jnp.zeros_like(right_side)
    residual = right_side
    direction = right_side
    norm_now = member_sum(residual, residual)
    for step_index in range(ITERS):
        applied = apply_operator(direction, diagonal, weights, neighbours)
        step_size = norm_now / member_sum(direction, applied)
        solution = solution + widen(step_size) * direction
        residual = residual - widen(step_size) * applied
        norm_next = member_sum(residual, residual)
        direction = residual + widen(norm_next / norm_now) * direction
        norm_now = norm_next
    return (solution.reshape(members, N_TILE * TY, TX), residual.reshape(members, N_TILE * TY, TX))
```

```python
import functools

import jax
import jax.numpy as jnp
from jax import lax
from jax.experimental import pallas as pl
from jax.experimental.pallas import tpu as pltpu
from jax.sharding import PartitionSpec as P

MESH = pl.DeviceIdType.MESH
F32 = jnp.float32
MEMB, LEV, TY, TX = 32, 8, 16, 128
NTX = 16
PLANE, DEPTH = 32, 8
N_TILE = PLANE * DEPTH
PITCH = 48
UNROLL = 4
CHUNKS = 4


def lanes(shape):
    return lax.broadcasted_iota(jnp.int32, shape, len(shape) - 1)


def roll_lanes(x, shift):
    return pltpu.roll(x, shift % 128, axis=x.ndim - 1)


def exchange_groups(a):
    lane = lanes(a[0].shape)
    low = lane < 64
    even = (lane // 32) % 2 == 0
    b0 = jnp.where(low, a[0], roll_lanes(a[2], 64))
    b2 = jnp.where(low, roll_lanes(a[0], 64), a[2])
    b1 = jnp.where(low, a[1], roll_lanes(a[3], 64))
    b3 = jnp.where(low, roll_lanes(a[1], 64), a[3])
    return (
        jnp.where(even, b0, roll_lanes(b1, 32)),
        jnp.where(even, roll_lanes(b0, 96), b1),
        jnp.where(even, b2, roll_lanes(b3, 32)),
        jnp.where(even, roll_lanes(b2, 96), b3),
    )


def reverse8(x):
    place = lax.broadcasted_iota(jnp.int32, x.shape, 0)
    x = pltpu.roll(x, 4, axis=0)
    x = jnp.where(place % 4 < 2, pltpu.roll(x, 6, axis=0), pltpu.roll(x, 2, axis=0))
    return jnp.where(place % 2 < 1, pltpu.roll(x, 7, axis=0), pltpu.roll(x, 1, axis=0))


def reverse_rows(x):
    blocks = x.shape[0] // 8
    return jnp.concatenate(
        [reverse8(x[8 * k : 8 * k + 8]) for k in range(blocks - 1, -1, -1)], axis=0
    )


def reverse_columns(x):
    even = (lanes(x.shape) // 32) % 2 == 0
    return reverse_rows(jnp.where(even, roll_lanes(x, 32), roll_lanes(x, 96)))


def pack_sums(p):
    p = [x[0:8] + x[8:16] + (x[16:24] + x[24:32]) for x in p]
    lane = lanes(p[0].shape)
    low = lane < 64
    even = (lane // 32) % 2 == 0
    x = jnp.where(low, p[0] + roll_lanes(p[0], 64), p[2] + roll_lanes(p[2], 64))
    y = jnp.where(low, p[1] + roll_lanes(p[1], 64), p[3] + roll_lanes(p[3], 64))
    z = jnp.where(even, x + roll_lanes(x, 96), y + roll_lanes(y, 32))
    return jnp.sum(z, axis=0, keepdims=True)


def spread(row):
    lane = lanes(row.shape)
    out = []
    for k in range(4):
        x = jnp.where(lane // 32 == k, row, 0.0)
        x = x + roll_lanes(x, 64)
        out.append(x + roll_lanes(x, 32))
    return out


def kernel(
    u_hbm, v_hbm, fraction, thickness, land, codes, x_out, r_out,
    u_buf, v_buf, tu1, tv1, weight, tu2, tv2, field, g_buf, q_buf, qsum, stage,
    edge_send, edge_recv, tu_send, tu_recv, tv_send, tv_recv, a1, b1, a2, b2,
    load_sem, send_sem, recv_sem, ar_send, ar_recv,
):
    me = lax.axis_index("tile")
    east, west = lax.rem(me + 1, N_TILE), lax.rem(me + N_TILE - 1, N_TILE)
    north, south = lax.rem(me + NTX, N_TILE), lax.rem(me + N_TILE - NTX, N_TILE)
    level, place = me // PLANE, lax.rem(me, PLANE)
    plane_peers = [level * PLANE + lax.rem(place + d, PLANE) for d in range(1, PLANE)]
    level_peers = [lax.rem(level + d, DEPTH) * PLANE + place for d in range(1, DEPTH)]

    part = MEMB // CHUNKS
    loads = []
    for c in range(CHUNKS):
        for n, (src, dst) in enumerate(((u_hbm, u_buf), (v_hbm, v_buf))):
            at = pl.ds(c * part, part)
            copy = pltpu.make_async_copy(src.at[at], dst.at[at], load_sem.at[n, c])
            copy.start()
            loads.append(copy)

    barrier = pltpu.get_barrier_semaphore()
    greeted = [east, west, north, south] + plane_peers + level_peers
    for peer in greeted:
        pl.semaphore_signal(barrier, inc=1, device_id=(peer,), device_id_type=MESH)

    flip = [codes[0, k] == 1 for k in range(4)]

    depth = None
    for k in range(LEV):
        w = thickness[k] * fraction[k].astype(F32)
        weight[k] = w
        depth = w if depth is None else depth + w
    root = 0.5 * jnp.sqrt(land[...].astype(F32) * depth)
    stage[...] = root

    def to_groups(rows_of, store):
        for block in range(4):
            z = jnp.concatenate([rows_of(4 * block + k) for k in range(4)], axis=0)
            t = jnp.transpose(z)
            out = exchange_groups([t[32 * g : 32 * g + 32] for g in range(4)])
            for k in range(4):
                store(4 * block + k, out[k])

    def inner(i):
        start = (i + 1) * PITCH + 8
        if not isinstance(i, int):
            start = pl.multiple_of(start, 8)
        return pl.ds(start, 32)

    def column(s):
        return pl.ds(PITCH + 8 + s, TY, stride=PITCH)

    def store_q(i, value):
        q_buf[i] = value
        g_buf[0, inner(i), :] = value

    to_groups(lambda i: jnp.broadcast_to(stage[pl.ds(i, 1), :], (MEMB, TX)), store_q)

    def column_sums(src, dst, n):
        for c in range(CHUNKS):
            loads[2 * c + n].wait()

            def member(m, carry):
                total = weight[0] * src[m, 0].astype(F32)
                for k in range(1, LEV):
                    total = total + weight[k] * src[m, k].astype(F32)
                dst[pl.ds(pl.multiple_of(m * TY, TY), TY), :] = total
                return carry

            lax.fori_loop(c * part, (c + 1) * part, member, 0, unroll=2)

    def remote(src, dst, index, direction, peer):
        return pltpu.make_async_remote_copy(
            src_ref=src, dst_ref=dst,
            send_sem=send_sem.at[index, direction], recv_sem=recv_sem.at[index, direction],
            device_id=(peer,), device_id_type=MESH,
        )

    def edges(k):
        return [
            remote(edge_send.at[k, 2], g_buf.at[k, pl.ds(17 * PITCH + 8, 32)], k, 2, south),
            remote(edge_send.at[k, 3], g_buf.at[k, pl.ds(8, 32)], k, 3, north),
            remote(edge_send.at[k, 0, pl.ds(0, TY)], edge_recv.at[k, 0], k, 0, west),
            remote(edge_send.at[k, 1, pl.ds(0, TY)], edge_recv.at[k, 1], k, 1, east),
        ]

    def put_rows(k):
        low, high = g_buf[k, inner(0), :], g_buf[k, inner(TY - 1), :]
        edge_send[k, 2] = jnp.where(flip[3], reverse_columns(low), low)
        edge_send[k, 3] = jnp.where(flip[2], reverse_columns(high), high)

    def put_columns(k):
        first, last = g_buf[k, column(0), :], g_buf[k, column(31), :]
        to_west = roll_lanes(first, 96)
        to_east = roll_lanes(last, 32)
        edge_send[k, 0, pl.ds(0, TY)] = jnp.where(flip[1], reverse_rows(to_west), to_west)
        edge_send[k, 1, pl.ds(0, TY)] = jnp.where(flip[0], reverse_rows(to_east), to_east)
        return to_west, to_east

    def take_columns(k, to_west, to_east):
        lane = lanes(to_west.shape)
        g_buf[k, column(32), :] = jnp.where(lane < 96, to_west, edge_recv[k, 0])
        g_buf[k, column(-1), :] = jnp.where(lane >= 32, to_east, edge_recv[k, 1])

    sent = []

    def send_edges(k):
        put_rows(k)
        copies = edges(k)
        copies[0].start()
        copies[1].start()
        own = put_columns(k)
        copies[2].start()
        copies[3].start()
        sent.extend(copies)
        return copies, own

    def take_edges(k, copies, own):
        copies[2].wait_recv()
        copies[3].wait_recv()
        take_columns(k, *own)
        copies[0].wait_recv()
        copies[1].wait_recv()

    def around(k, i):
        here = inner(i)
        base = here.start
        return (g_buf[k, pl.ds(base + 1, 32), :] + g_buf[k, pl.ds(base - 1, 32), :]) + (
            g_buf[k, inner(i + 1), :] + g_buf[k, inner(i - 1), :]
        )

    column_sums(u_buf, tu1, 0)
    column_sums(v_buf, tv1, 1)

    def store_tu(i, value):
        tu2[inner(i), :] = value

    def store_tv(i, value):
        tv2[pl.ds(i * 32, 32), :] = value

    to_groups(lambda i: tv1[pl.ds(i, MEMB, stride=TY), :], store_tv)
    to_groups(lambda i: tu1[pl.ds(i, MEMB, stride=TY), :], store_tu)

    row = tv2[pl.ds(0, 32), :]
    tv_send[...] = jnp.where(flip[3], reverse_columns(row), row)
    own_tu = roll_lanes(tu2[column(0), :], 96)
    tu_send[...] = jnp.where(flip[1], reverse_rows(own_tu), own_tu)

    pl.semaphore_wait(barrier, len(greeted))
    tv_copy = remote(tv_send, tv2.at[pl.ds(TY * 32, 32)], 5, 2, south)
    tv_copy.start()
    tu_copy = remote(tu_send, tu_recv, 5, 0, west)
    tu_copy.start()
    copies, own = send_edges(0)
    tu_copy.wait_recv()
    tu2[column(32), :] = jnp.where(lanes(own_tu.shape) < 96, own_tu, tu_recv[...])
    tv_copy.wait_recv()
    take_edges(0, copies, own)

    zero = jnp.zeros((32, 128), F32)

    def first(i, total):
        q = q_buf[i]
        here = inner(i)
        below = pl.multiple_of(i * 32, 32)
        value = (
            tu2[here, :] - tu2[pl.ds(here.start + 1, 32), :]
            + tv2[pl.ds(below, 32), :] - tv2[pl.ds(below + 32, 32), :]
        )
        value = jnp.where(q > 0.0, value, 0.0)
        qsum[i] = around(0, i)
        field[0, i] = value
        g_buf[1, here, :] = q * value
        return total + value * value

    n0 = lax.fori_loop(0, TY, first, zero, unroll=UNROLL)

    def image(k, square):
        copies, own = send_edges(k)
        yield
        take_edges(k, copies, own)

        def step(i, totals):
            q, old = q_buf[i], field[k - 1, i]
            value = q * (qsum[i] * old - around(k, i))
            field[k, i] = value
            if k < 4:
                g_buf[k + 1, inner(i), :] = q * value
            if square is None:
                return totals
            cross, own_square = totals
            return cross + old * value, own_square + value * value if square else own_square

        yield lax.fori_loop(0, TY, step, (zero, zero), unroll=UNROLL)

    def make_image(k, square, between=None):
        steps = image(k, square)
        next(steps)
        if between is not None:
            between()
        return next(steps)

    def fan(buf, slot, peers, phase, which):
        def copy_to(peer):
            return pltpu.make_async_remote_copy(
                src_ref=buf.at[slot], dst_ref=buf.at[slot],
                send_sem=ar_send.at[which, phase], recv_sem=ar_recv.at[which, phase],
                device_id=(peer,), device_id_type=MESH,
            )

        for peer in peers:
            copy_to(peer).start()

    def fan_wait(buf, count, sem):
        pltpu.make_async_copy(buf.at[pl.ds(0, count)], buf.at[pl.ds(0, count)], sem).wait()

    def start_level(values, buf, which):
        buf[place] = values
        fan(buf, place, plane_peers, 0, which)

    def cross_levels(buf_a, buf_b, which):
        fan_wait(buf_a, PLANE - 1, ar_recv.at[which, 0])
        buf_b[level] = jnp.sum(buf_a[...], axis=0)
        fan(buf_b, level, level_peers, 1, which)

    def finish(buf_b, which):
        fan_wait(buf_b, DEPTH - 1, ar_recv.at[which, 1])
        return jnp.sum(buf_b[...], axis=0)

    n1, n2 = make_image(1, True)
    n3, _ = make_image(2, False)
    make_image(3, None, lambda: start_level(pack_sums([n0, n1, n2, n3]), a1, 0))
    make_image(4, None, lambda: cross_levels(a1, b1, 0))
    s0, s1, s2, s3 = spread(finish(b1, 0))

    m0, m1, m2, m3 = s0, s0 + s1, s0 + 2.0 * s1 + s2, s0 + 3.0 * (s1 + s2) + s3
    alpha0 = m0 / m1
    rr1 = m0 - alpha0 * (2.0 * m1 - alpha0 * m2)
    gain = 1.0 + rr1 / m0
    alpha1 = rr1 / (gain * gain * m1 - alpha0 * (2.0 * gain * m2 - alpha0 * m3))
    lead = alpha0 * alpha1
    lin = -(alpha0 + alpha1 * gain)
    c0, c1, c2 = 1.0 + lin + lead, lin + 2.0 * lead, lead
    e0, e1 = gain - alpha0, -alpha0
    x0, x1 = -lin - lead, -lead

    def rows(*values):
        return [jnp.broadcast_to(v, (32, 128)) for v in values]

    c0b, c1b, c2b, e0b, e1b = rows(c0, c1, c2, e0, e1)

    def second(i, totals):
        v = [field[k, i] for k in range(5)]
        r = [c0b * v[k] + c1b * v[k + 1] + c2b * v[k + 2] for k in range(3)]
        d = [e0b * v[k] + e1b * v[k + 1] for k in range(3)]
        here = inner(i)
        for k in range(3):
            g_buf[k, here, :] = r[k]
        g_buf[3, here, :] = d[0]
        g_buf[4, here, :] = d[1]
        tu2[here, :] = d[2]
        pairs = (
            (r[0], r[0]), (r[0], d[0]), (d[0], d[0]), (r[0], r[1]),
            (r[0], d[1]), (d[0], d[1]), (r[1], r[1]), (r[1], d[1]),
            (d[1], d[1]), (r[1], r[2]), (r[1], d[2]), (d[1], d[2]),
        )
        out = []
        for t, (x, y) in zip(totals, pairs):
            p = x * y
            out.append(t + (p[0:8] + p[8:16] + (p[16:24] + p[24:32])))
        return tuple(out)

    small = jnp.zeros((8, 128), F32)
    totals = lax.fori_loop(0, TY, second, (small,) * 12, unroll=2)
    wide = [jnp.concatenate([t, jnp.zeros((24, 128), F32)], axis=0) for t in totals]
    packed = [pack_sums(wide[4 * k : 4 * k + 4]) for k in range(3)]
    start_level(jnp.concatenate(packed + [packed[0] * 0.0], axis=0), a2, 1)
    cross_levels(a2, b2, 1)
    sums = finish(b2, 1)
    rr, rd, dd, rr_1 = spread(sums[0:1])
    rd_1, dd_1, rr_2, rd_2 = spread(sums[1:2])
    dd_2, rr_3, rd_3, dd_3 = spread(sums[2:3])
    r1 = rr + rr_1
    r2 = rr + 2.0 * rr_1 + rr_2
    r3 = rr + 3.0 * (rr_1 + rr_2) + rr_3
    y1 = rd + rd_1
    y2 = rd + 2.0 * rd_1 + rd_2
    y3 = rd + 3.0 * (rd_1 + rd_2) + rd_3
    d1 = dd + dd_1
    d2 = dd + 2.0 * dd_1 + dd_2
    d3 = dd + 3.0 * (dd_1 + dd_2) + dd_3
    beta1 = rr / rr1
    p1 = r1 + beta1 * (2.0 * y1 + beta1 * d1)
    p2 = r2 + beta1 * (2.0 * y2 + beta1 * d2)
    p3 = r3 + beta1 * (2.0 * y3 + beta1 * d3)
    rp1 = r1 + beta1 * y1
    rp2 = r2 + beta1 * y2
    alpha2 = rr / p1
    rr3 = rr - alpha2 * (2.0 * rp1 - alpha2 * p2)
    beta2 = rr3 / rr
    q1 = (
        r1 + alpha2 * (alpha2 * p3 - 2.0 * rp2)
        + beta2 * (2.0 * (rp1 - alpha2 * p2) + beta2 * p1)
    )
    alpha3 = rr3 / q1
    kappa = alpha2 + alpha3 * beta2
    mu = alpha2 * alpha3
    xp0 = kappa - mu
    xr0, xr1 = xp0 + alpha3, -mu
    xd0, xd1 = beta1 * xp0, -beta1 * mu
    fp0, fp1, fp2 = mu - kappa, 2.0 * mu - kappa, mu
    fr0, fr1, fr2 = 1.0 + fp0 - alpha3, fp1 - alpha3, fp2
    fd0, fd1, fd2 = beta1 * fp0, beta1 * fp1, beta1 * fp2
    cx = rows(x0, x1, xr0, xr1, xd0, xd1)
    cr = rows(fr0, fr1, fr2, fd0, fd1, fd2)

    for block in range(4):
        xs, rs = [], []
        for k in range(4):
            i = 4 * block + k
            here = inner(i)
            r = [g_buf[n, here, :] for n in range(3)]
            d = [g_buf[3, here, :], g_buf[4, here, :], tu2[here, :]]
            parts = (field[0, i], field[1, i], r[0], r[1], d[0], d[1])
            xs.append(functools.reduce(lambda s, t: s + t, [c * t for c, t in zip(cx, parts)]))
            rs.append(functools.reduce(lambda s, t: s + t, [c * t for c, t in zip(cr, r + d)]))
        for values, out in ((xs, x_out), (rs, r_out)):
            t = jnp.transpose(jnp.concatenate(exchange_groups(values), axis=0))
            for k in range(4):
                out[pl.ds(4 * block + k, MEMB, stride=TY), :] = t[32 * k : 32 * k + 32]

    for copy in sent + [tv_copy, tu_copy]:
        copy.wait_send()
    fan_wait(a1, PLANE - 1, ar_send.at[0, 0])
    fan_wait(b1, DEPTH - 1, ar_send.at[0, 1])
    fan_wait(a2, PLANE - 1, ar_send.at[1, 0])
    fan_wait(b2, DEPTH - 1, ar_send.at[1, 1])


def on_device(zonal, meridional, fraction, thickness, land, codes):
    vmem = pl.BlockSpec(memory_space=pltpu.VMEM)
    smem = pl.BlockSpec(memory_space=pltpu.SMEM)
    hbm = pl.BlockSpec(memory_space=pl.ANY)
    flat = jax.ShapeDtypeStruct((MEMB * TY, TX), F32)
    padded = (TY + 2) * PITCH
    x, r = pl.pallas_call(
        kernel,
        out_shape=(flat, flat),
        in_specs=[hbm, hbm, vmem, smem, vmem, smem],
        out_specs=(vmem, vmem),
        scratch_shapes=[
            pltpu.VMEM((MEMB, LEV, TY, TX), jnp.bfloat16),
            pltpu.VMEM((MEMB, LEV, TY, TX), jnp.bfloat16),
            pltpu.VMEM((MEMB * TY, TX), F32),
            pltpu.VMEM((MEMB * TY, TX), F32),
            pltpu.VMEM((LEV, TY, TX), F32),
            pltpu.VMEM((padded, 128), F32),
            pltpu.VMEM(((TY + 1) * 32, 128), F32),
            pltpu.VMEM((5, TY, 32, 128), F32),
            pltpu.VMEM((5, padded, 128), F32),
            pltpu.VMEM((TY, 32, 128), F32),
            pltpu.VMEM((TY, 32, 128), F32),
            pltpu.VMEM((TY, TX), F32),
            pltpu.VMEM((5, 4, 32, 128), F32),
            pltpu.VMEM((5, 2, TY, 128), F32),
            pltpu.VMEM((TY, 128), F32),
            pltpu.VMEM((TY, 128), F32),
            pltpu.VMEM((32, 128), F32),
            pltpu.VMEM((32, 128), F32),
            pltpu.VMEM((PLANE, 1, 128), F32),
            pltpu.VMEM((DEPTH, 1, 128), F32),
            pltpu.VMEM((PLANE, 4, 128), F32),
            pltpu.VMEM((DEPTH, 4, 128), F32),
            pltpu.SemaphoreType.DMA((2, CHUNKS)),
            pltpu.SemaphoreType.DMA((6, 4)),
            pltpu.SemaphoreType.DMA((6, 4)),
            pltpu.SemaphoreType.DMA((2, 2)),
            pltpu.SemaphoreType.DMA((2, 2)),
        ],
        compiler_params=pltpu.CompilerParams(
            collective_id=0, has_side_effects=True, vmem_limit_bytes=40 << 20
        ),
    )(zonal, meridional, fraction, thickness, land, codes)
    return x.reshape(MEMB, TY, TX), r.reshape(MEMB, TY, TX)


def solution(mesh):
    in_specs = (
        P(None, None, "tile", None),
        P(None, None, "tile", None),
        P(None, "tile", None),
        P(),
        P("tile", None),
        P("tile", None),
    )
    out_specs = (P(None, "tile", None), P(None, "tile", None))
    return jax.shard_map(
        on_device, mesh=mesh, in_specs=in_specs, out_specs=out_specs, check_vma=False
    )
```

```python
import functools

import jax
import jax.numpy as jnp
from jax import lax
from jax.experimental import pallas as pl
from jax.experimental.pallas import tpu as pltpu
from jax.sharding import PartitionSpec as P

MESH = pl.DeviceIdType.MESH
F32 = jnp.float32
MEMB, LEV, TY, TX = 32, 8, 16, 128
NTX = 16
PLANE, DEPTH = 32, 8
N_TILE = PLANE * DEPTH
PITCH = 48
UNROLL = 4
CHUNKS = 4


def lanes(shape):
    return lax.broadcasted_iota(jnp.int32, shape, len(shape) - 1)


def roll_lanes(x, shift):
    return pltpu.roll(x, shift % 128, axis=x.ndim - 1)


def exchange_groups(a):
    lane = lanes(a[0].shape)
    low = lane < 64
    even = (lane // 32) % 2 == 0
    b0 = jnp.where(low, a[0], roll_lanes(a[2], 64))
    b2 = jnp.where(low, roll_lanes(a[0], 64), a[2])
    b1 = jnp.where(low, a[1], roll_lanes(a[3], 64))
    b3 = jnp.where(low, roll_lanes(a[1], 64), a[3])
    return (
        jnp.where(even, b0, roll_lanes(b1, 32)),
        jnp.where(even, roll_lanes(b0, 96), b1),
        jnp.where(even, b2, roll_lanes(b3, 32)),
        jnp.where(even, roll_lanes(b2, 96), b3),
    )


def reverse8(x):
    place = lax.broadcasted_iota(jnp.int32, x.shape, 0)
    x = pltpu.roll(x, 4, axis=0)
    x = jnp.where(place % 4 < 2, pltpu.roll(x, 6, axis=0), pltpu.roll(x, 2, axis=0))
    return jnp.where(place % 2 < 1, pltpu.roll(x, 7, axis=0), pltpu.roll(x, 1, axis=0))


def reverse_rows(x):
    blocks = x.shape[0] // 8
    return jnp.concatenate(
        [reverse8(x[8 * k : 8 * k + 8]) for k in range(blocks - 1, -1, -1)], axis=0
    )


def reverse_columns(x):
    even = (lanes(x.shape) // 32) % 2 == 0
    return reverse_rows(jnp.where(even, roll_lanes(x, 32), roll_lanes(x, 96)))


def pack_sums(p):
    p = [x[0:8] + x[8:16] + (x[16:24] + x[24:32]) for x in p]
    lane = lanes(p[0].shape)
    low = lane < 64
    even = (lane // 32) % 2 == 0
    x = jnp.where(low, p[0] + roll_lanes(p[0], 64), p[2] + roll_lanes(p[2], 64))
    y = jnp.where(low, p[1] + roll_lanes(p[1], 64), p[3] + roll_lanes(p[3], 64))
    z = jnp.where(even, x + roll_lanes(x, 96), y + roll_lanes(y, 32))
    return jnp.sum(z, axis=0, keepdims=True)


def spread(row):
    lane = lanes(row.shape)
    out = []
    for k in range(4):
        x = jnp.where(lane // 32 == k, row, 0.0)
        x = x + roll_lanes(x, 64)
        out.append(x + roll_lanes(x, 32))
    return out


def kernel(
    u_hbm, v_hbm, fraction_hbm, thickness_hbm, land_hbm, codes_hbm, field, images, factors,
    u_buf, v_buf, fraction, thickness, land, codes, tu1, tv1, weight, tu2, tv2, g_buf, q_buf, qsum, stage,
    edge_send, edge_recv, tu_send, tu_recv, tv_send, a1, b1, a2, b2,
    load_sem, small_sem, send_sem, recv_sem, ar_send, ar_recv,
):
    me = lax.axis_index("tile")
    east, west = lax.rem(me + 1, N_TILE), lax.rem(me + N_TILE - 1, N_TILE)
    north, south = lax.rem(me + NTX, N_TILE), lax.rem(me + N_TILE - NTX, N_TILE)
    level, place = me // PLANE, lax.rem(me, PLANE)
    plane_peers = [level * PLANE + lax.rem(place + d, PLANE) for d in range(1, PLANE)]
    level_peers = [lax.rem(level + d, DEPTH) * PLANE + place for d in range(1, DEPTH)]

    small_loads = []
    pairs = ((thickness_hbm, thickness), (codes_hbm, codes), (fraction_hbm, fraction), (land_hbm, land))
    for n, (src, dst) in enumerate(pairs):
        copy = pltpu.make_async_copy(src, dst, small_sem.at[n])
        copy.start()
        small_loads.append(copy)
    part = MEMB // CHUNKS
    loads = []
    for c in range(CHUNKS):
        for n, (src, dst) in enumerate(((u_hbm, u_buf), (v_hbm, v_buf))):
            at = pl.ds(c * part, part)
            copy = pltpu.make_async_copy(src.at[at], dst.at[at], load_sem.at[n, c])
            copy.start()
            loads.append(copy)

    barrier = pltpu.get_barrier_semaphore()
    greeted = [east, west, north, south] + plane_peers + level_peers
    for peer in greeted:
        pl.semaphore_signal(barrier, inc=1, device_id=(peer,), device_id_type=MESH)

    for copy in small_loads:
        copy.wait()
    flip = [codes[0, k] == 1 for k in range(4)]

    depth = None
    for k in range(LEV):
        w = thickness[k] * fraction[k].astype(F32)
        weight[k] = w
        depth = w if depth is None else depth + w
    root = 0.5 * jnp.sqrt(land[...].astype(F32) * depth)
    stage[...] = root

    def to_groups(rows_of, store):
        for block in range(4):
            z = jnp.concatenate([rows_of(4 * block + k) for k in range(4)], axis=0)
            t = jnp.transpose(z)
            out = exchange_groups([t[32 * g : 32 * g + 32] for g in range(4)])
            for k in range(4):
                store(4 * block + k, out[k])

    def inner(i):
        start = (i + 1) * PITCH + 8
        if not isinstance(i, int):
            start = pl.multiple_of(start, 8)
        return pl.ds(start, 32)

    def column(s):
        return pl.ds(PITCH + 8 + s, TY, stride=PITCH)

    def store_q(i, value):
        q_buf[i] = value
        g_buf[0, inner(i), :] = value

    to_groups(lambda i: jnp.broadcast_to(stage[pl.ds(i, 1), :], (MEMB, TX)), store_q)

    def column_sums(src, dst, n):
        for c in range(CHUNKS):
            loads[2 * c + n].wait()

            def member(m, carry):
                total = weight[0] * src[m, 0].astype(F32)
                for k in range(1, LEV):
                    total = total + weight[k] * src[m, k].astype(F32)
                dst[pl.ds(pl.multiple_of(m * TY, TY), TY), :] = total
                return carry

            lax.fori_loop(c * part, (c + 1) * part, member, 0, unroll=2)

    def remote(src, dst, index, direction, peer):
        return pltpu.make_async_remote_copy(
            src_ref=src, dst_ref=dst,
            send_sem=send_sem.at[index, direction], recv_sem=recv_sem.at[index, direction],
            device_id=(peer,), device_id_type=MESH,
        )

    def edges(k):
        return [
            remote(edge_send.at[k, 2], g_buf.at[k, pl.ds(17 * PITCH + 8, 32)], k, 2, south),
            remote(edge_send.at[k, 3], g_buf.at[k, pl.ds(8, 32)], k, 3, north),
            remote(edge_send.at[k, 0, pl.ds(0, TY)], edge_recv.at[k, 0], k, 0, west),
            remote(edge_send.at[k, 1, pl.ds(0, TY)], edge_recv.at[k, 1], k, 1, east),
        ]

    def put_rows(k):
        low, high = g_buf[k, inner(0), :], g_buf[k, inner(TY - 1), :]
        edge_send[k, 2] = jnp.where(flip[3], reverse_columns(low), low)
        edge_send[k, 3] = jnp.where(flip[2], reverse_columns(high), high)

    def put_columns(k):
        first, last = g_buf[k, column(0), :], g_buf[k, column(31), :]
        to_west = roll_lanes(first, 96)
        to_east = roll_lanes(last, 32)
        edge_send[k, 0, pl.ds(0, TY)] = jnp.where(flip[1], reverse_rows(to_west), to_west)
        edge_send[k, 1, pl.ds(0, TY)] = jnp.where(flip[0], reverse_rows(to_east), to_east)
        return to_west, to_east

    def take_columns(k, to_west, to_east):
        lane = lanes(to_west.shape)
        g_buf[k, column(32), :] = jnp.where(lane < 96, to_west, edge_recv[k, 0])
        g_buf[k, column(-1), :] = jnp.where(lane >= 32, to_east, edge_recv[k, 1])

    sent = []

    def send_rows(k):
        put_rows(k)
        copies = edges(k)
        copies[0].start()
        copies[1].start()
        sent.extend(copies)
        return copies

    def send_columns(k, copies):
        own = put_columns(k)
        copies[2].start()
        copies[3].start()
        return own

    def around(k, i):
        here = inner(i)
        base = here.start
        return (g_buf[k, pl.ds(base + 1, 32), :] + g_buf[k, pl.ds(base - 1, 32), :]) + (
            g_buf[k, inner(i + 1), :] + g_buf[k, inner(i - 1), :]
        )

    column_sums(u_buf, tu1, 0)
    column_sums(v_buf, tv1, 1)

    def store_tu(i, value):
        tu2[inner(i), :] = value

    def store_tv(i, value):
        tv2[pl.ds(i * 32, 32), :] = value

    to_groups(lambda i: tv1[pl.ds(i, MEMB, stride=TY), :], store_tv)
    to_groups(lambda i: tu1[pl.ds(i, MEMB, stride=TY), :], store_tu)

    row = tv2[pl.ds(0, 32), :]
    tv_send[...] = jnp.where(flip[3], reverse_columns(row), row)
    own_tu = roll_lanes(tu2[column(0), :], 96)
    tu_send[...] = jnp.where(flip[1], reverse_rows(own_tu), own_tu)

    pl.semaphore_wait(barrier, len(greeted))
    tv_copy = remote(tv_send, tv2.at[pl.ds(TY * 32, 32)], 5, 2, south)
    tv_copy.start()
    tu_copy = remote(tu_send, tu_recv, 5, 0, west)
    tu_copy.start()
    copies = send_rows(0)
    own = send_columns(0, copies)
    tu_copy.wait_recv()
    tu2[column(32), :] = jnp.where(lanes(own_tu.shape) < 96, own_tu, tu_recv[...])
    copies[2].wait_recv()
    copies[3].wait_recv()
    take_columns(0, *own)

    zero = jnp.zeros((32, 128), F32)

    def first(i, total):
        q = q_buf[i]
        here = inner(i)
        below = i * 32 if isinstance(i, int) else pl.multiple_of(i * 32, 32)
        value = (
            tu2[here, :] - tu2[pl.ds(here.start + 1, 32), :]
            + tv2[pl.ds(below, 32), :] - tv2[pl.ds(below + 32, 32), :]
        )
        value = jnp.where(q > 0.0, value, 0.0)
        qsum[i] = around(0, i)
        field[0, i] = value
        g_buf[1, here, :] = q * value
        return total + value * value

    def middle(body, start):
        return lax.fori_loop(1, TY - 1, body, start, unroll=UNROLL)

    n0 = middle(first, zero)
    tv_copy.wait_recv()
    copies[0].wait_recv()
    copies[1].wait_recv()
    n0 = first(TY - 1, first(0, n0))
    flight = send_rows(1)
    own = send_columns(1, flight)

    def image(k, copies, own, square):
        def step(i, totals):
            q, old = q_buf[i], field[k - 1, i]
            value = q * (qsum[i] * old - around(k, i))
            field[k, i] = value
            if k < 4:
                g_buf[k + 1, inner(i), :] = q * value
            if square is None:
                return totals
            cross, own_square = totals
            return cross + old * value, own_square + value * value if square else own_square

        copies[2].wait_recv()
        copies[3].wait_recv()
        take_columns(k, *own)
        totals = middle(step, (zero, zero))
        copies[0].wait_recv()
        copies[1].wait_recv()
        totals = step(TY - 1, step(0, totals))
        if k == 4:
            return totals
        ahead = send_rows(k + 1)
        return totals, ahead, send_columns(k + 1, ahead)

    def fan(buf, slot, peers, phase, which):
        def copy_to(peer):
            return pltpu.make_async_remote_copy(
                src_ref=buf.at[slot], dst_ref=buf.at[slot],
                send_sem=ar_send.at[which, phase], recv_sem=ar_recv.at[which, phase],
                device_id=(peer,), device_id_type=MESH,
            )

        for peer in peers:
            copy_to(peer).start()

    def fan_wait(buf, count, sem):
        pltpu.make_async_copy(buf.at[pl.ds(0, count)], buf.at[pl.ds(0, count)], sem).wait()

    def start_level(values, buf, which):
        buf[place] = values
        fan(buf, place, plane_peers, 0, which)

    def cross_levels(buf_a, buf_b, which):
        fan_wait(buf_a, PLANE - 1, ar_recv.at[which, 0])
        buf_b[level] = jnp.sum(buf_a[...], axis=0)
        fan(buf_b, level, level_peers, 1, which)

    def finish(buf_b, which):
        fan_wait(buf_b, DEPTH - 1, ar_recv.at[which, 1])
        return jnp.sum(buf_b[...], axis=0)

    (n1, n2), flight, own = image(1, flight, own, True)
    (n3, _), flight, own = image(2, flight, own, False)
    start_level(pack_sums([n0, n1, n2, n3]), a1, 0)
    _, flight, own = image(3, flight, own, None)
    cross_levels(a1, b1, 0)
    image(4, flight, own, None)
    s0, s1, s2, s3 = spread(finish(b1, 0))

    m0, m1, m2, m3 = s0, s0 + s1, s0 + 2.0 * s1 + s2, s0 + 3.0 * (s1 + s2) + s3
    alpha0 = m0 / m1
    rr1 = m0 - alpha0 * (2.0 * m1 - alpha0 * m2)
    gain = 1.0 + rr1 / m0
    alpha1 = rr1 / (gain * gain * m1 - alpha0 * (2.0 * gain * m2 - alpha0 * m3))
    lead = alpha0 * alpha1
    lin = -(alpha0 + alpha1 * gain)
    c0, c1, c2 = 1.0 + lin + lead, lin + 2.0 * lead, lead
    e0, e1 = gain - alpha0, -alpha0
    x0, x1 = -lin - lead, -lead

    def rows(*values):
        return [jnp.broadcast_to(v, (32, 128)) for v in values]

    c0b, c1b, c2b, e0b, e1b = rows(c0, c1, c2, e0, e1)

    def second(i, totals):
        v = [field[k, i] for k in range(5)]
        r = [c0b * v[k] + c1b * v[k + 1] + c2b * v[k + 2] for k in range(3)]
        d = [e0b * v[k] + e1b * v[k + 1] for k in range(3)]
        for k in range(3):
            images[k, i] = r[k]
            images[3 + k, i] = d[k]
        pairs = (
            (r[0], r[0]), (r[0], d[0]), (d[0], d[0]), (r[0], r[1]),
            (r[0], d[1]), (d[0], d[1]), (r[1], r[1]), (r[1], d[1]),
            (d[1], d[1]), (r[1], r[2]), (r[1], d[2]), (d[1], d[2]),
        )
        out = []
        for t, (x, y) in zip(totals, pairs):
            p = x * y
            out.append(t + (p[0:8] + p[8:16] + (p[16:24] + p[24:32])))
        return tuple(out)

    small = jnp.zeros((8, 128), F32)
    totals = lax.fori_loop(0, TY, second, (small,) * 12, unroll=2)
    wide = [jnp.concatenate([t, jnp.zeros((24, 128), F32)], axis=0) for t in totals]
    packed = [pack_sums(wide[4 * k : 4 * k + 4]) for k in range(3)]
    start_level(jnp.concatenate(packed + [packed[0] * 0.0], axis=0), a2, 1)
    cross_levels(a2, b2, 1)
    sums = finish(b2, 1)
    rr, rd, dd, rr_1 = spread(sums[0:1])
    rd_1, dd_1, rr_2, rd_2 = spread(sums[1:2])
    dd_2, rr_3, rd_3, dd_3 = spread(sums[2:3])
    r1 = rr + rr_1
    r2 = rr + 2.0 * rr_1 + rr_2
    r3 = rr + 3.0 * (rr_1 + rr_2) + rr_3
    y1 = rd + rd_1
    y2 = rd + 2.0 * rd_1 + rd_2
    y3 = rd + 3.0 * (rd_1 + rd_2) + rd_3
    d1 = dd + dd_1
    d2 = dd + 2.0 * dd_1 + dd_2
    d3 = dd + 3.0 * (dd_1 + dd_2) + dd_3
    beta1 = rr / rr1
    p1 = r1 + beta1 * (2.0 * y1 + beta1 * d1)
    p2 = r2 + beta1 * (2.0 * y2 + beta1 * d2)
    p3 = r3 + beta1 * (2.0 * y3 + beta1 * d3)
    rp1 = r1 + beta1 * y1
    rp2 = r2 + beta1 * y2
    alpha2 = rr / p1
    rr3 = rr - alpha2 * (2.0 * rp1 - alpha2 * p2)
    beta2 = rr3 / rr
    q1 = (
        r1 + alpha2 * (alpha2 * p3 - 2.0 * rp2)
        + beta2 * (2.0 * (rp1 - alpha2 * p2) + beta2 * p1)
    )
    alpha3 = rr3 / q1
    kappa = alpha2 + alpha3 * beta2
    mu = alpha2 * alpha3
    xp0 = kappa - mu
    xr0, xr1 = xp0 + alpha3, -mu
    xd0, xd1 = beta1 * xp0, -beta1 * mu
    fp0, fp1, fp2 = mu - kappa, 2.0 * mu - kappa, mu
    fr0, fr1, fr2 = 1.0 + fp0 - alpha3, fp1 - alpha3, fp2
    fd0, fd1, fd2 = beta1 * fp0, beta1 * fp1, beta1 * fp2
    for k, factor in enumerate((x0, x1, xr0, xr1, xd0, xd1, fr0, fr1, fr2, fd0, fd1, fd2)):
        factors[k] = jnp.broadcast_to(factor, (8, 128))

    for copy in sent + [tv_copy, tu_copy]:
        copy.wait_send()
    fan_wait(a1, PLANE - 1, ar_send.at[0, 0])
    fan_wait(b1, DEPTH - 1, ar_send.at[0, 1])
    fan_wait(a2, PLANE - 1, ar_send.at[1, 0])
    fan_wait(b2, DEPTH - 1, ar_send.at[1, 1])


def combine(field, images, factors, x_hbm, r_hbm, x_buf, r_buf, sem):
    c = [jnp.concatenate([factors[k]] * 4, axis=0) for k in range(12)]
    copies = []
    for block in range(4):
        xs, rs = [], []
        for k in range(4):
            i = 4 * block + k
            v = [images[n, i] for n in range(6)]
            parts = (field[0, i], field[1, i], v[0], v[1], v[3], v[4])
            xs.append(functools.reduce(lambda s, t: s + t, [a * t for a, t in zip(c[:6], parts)]))
            rs.append(functools.reduce(lambda s, t: s + t, [a * t for a, t in zip(c[6:], v)]))
        for values, out in ((xs, x_buf), (rs, r_buf)):
            t = jnp.transpose(jnp.concatenate(exchange_groups(values), axis=0))
            for k in range(4):
                out[pl.ds(4 * block + k, MEMB, stride=TY), :] = t[32 * k : 32 * k + 32]
    for n, (src, dst) in enumerate(((x_buf, x_hbm), (r_buf, r_hbm))):
        copy = pltpu.make_async_copy(src, dst, sem.at[n])
        copy.start()
        copies.append(copy)
    for copy in copies:
        copy.wait()


def on_device(zonal, meridional, fraction, thickness, land, codes):
    vmem = pl.BlockSpec(memory_space=pltpu.VMEM)
    hbm = pl.BlockSpec(memory_space=pltpu.HBM)
    arguments = [
        pltpu.with_memory_space_constraint(x, pltpu.HBM)
        for x in (zonal, meridional, fraction, thickness, land, codes)
    ]
    flat = jax.ShapeDtypeStruct((MEMB * TY, TX), F32)
    padded = (TY + 2) * PITCH
    field, images, factors = pl.pallas_call(
        kernel,
        out_shape=(
            jax.ShapeDtypeStruct((5, TY, 32, 128), F32),
            jax.ShapeDtypeStruct((6, TY, 32, 128), F32),
            jax.ShapeDtypeStruct((12, 8, 128), F32),
        ),
        in_specs=[hbm] * 6,
        out_specs=(vmem, vmem, vmem),
        scratch_shapes=[
            pltpu.VMEM((MEMB, LEV, TY, TX), jnp.bfloat16),
            pltpu.VMEM((MEMB, LEV, TY, TX), jnp.bfloat16),
            pltpu.VMEM((LEV, TY, TX), jnp.bfloat16),
            pltpu.SMEM((LEV,), F32),
            pltpu.VMEM((TY, TX), jnp.int32),
            pltpu.SMEM((1, 4), jnp.int32),
            pltpu.VMEM((MEMB * TY, TX), F32),
            pltpu.VMEM((MEMB * TY, TX), F32),
            pltpu.VMEM((LEV, TY, TX), F32),
            pltpu.VMEM((padded, 128), F32),
            pltpu.VMEM(((TY + 1) * 32, 128), F32),
            pltpu.VMEM((5, padded, 128), F32),
            pltpu.VMEM((TY, 32, 128), F32),
            pltpu.VMEM((TY, 32, 128), F32),
            pltpu.VMEM((TY, TX), F32),
            pltpu.VMEM((5, 4, 32, 128), F32),
            pltpu.VMEM((5, 2, TY, 128), F32),
            pltpu.VMEM((TY, 128), F32),
            pltpu.VMEM((TY, 128), F32),
            pltpu.VMEM((32, 128), F32),
            pltpu.VMEM((PLANE, 1, 128), F32),
            pltpu.VMEM((DEPTH, 1, 128), F32),
            pltpu.VMEM((PLANE, 4, 128), F32),
            pltpu.VMEM((DEPTH, 4, 128), F32),
            pltpu.SemaphoreType.DMA((2, CHUNKS)),
            pltpu.SemaphoreType.DMA((4,)),
            pltpu.SemaphoreType.DMA((6, 4)),
            pltpu.SemaphoreType.DMA((6, 4)),
            pltpu.SemaphoreType.DMA((2, 2)),
            pltpu.SemaphoreType.DMA((2, 2)),
        ],
        compiler_params=pltpu.CompilerParams(
            collective_id=0, has_side_effects=True, vmem_limit_bytes=40 << 20
        ),
    )(*arguments)
    x, r = pl.pallas_call(
        combine,
        out_shape=(flat, flat),
        in_specs=[vmem] * 3,
        out_specs=(hbm, hbm),
        scratch_shapes=[
            pltpu.VMEM((MEMB * TY, TX), F32),
            pltpu.VMEM((MEMB * TY, TX), F32),
            pltpu.SemaphoreType.DMA((2,)),
        ],
        compiler_params=pltpu.CompilerParams(vmem_limit_bytes=16 << 20),
    )(field, images, factors)
    return x.reshape(MEMB, TY, TX), r.reshape(MEMB, TY, TX)


def solution(mesh):
    in_specs = (
        P(None, None, "tile", None),
        P(None, None, "tile", None),
        P(None, "tile", None),
        P(),
        P("tile", None),
        P("tile", None),
    )
    out_specs = (P(None, "tile", None), P(None, "tile", None))
    return jax.shard_map(
        on_device, mesh=mesh, in_specs=in_specs, out_specs=out_specs, check_vma=False
    )
```

```python
import functools

import jax
import jax.numpy as jnp
from jax import lax
from jax.experimental import pallas as pl
from jax.experimental.pallas import tpu as pltpu
from jax.sharding import PartitionSpec as P

MESH = pl.DeviceIdType.MESH
F32 = jnp.float32
MEMB, LEV, TY, TX = 32, 8, 16, 128
NTX = 16
PLANE, DEPTH = 32, 8
N_TILE = PLANE * DEPTH
PITCH = 48
UNROLL = 4
CHUNKS = 4


def lanes(shape):
    return lax.broadcasted_iota(jnp.int32, shape, len(shape) - 1)


def roll_lanes(x, shift):
    return pltpu.roll(x, shift % 128, axis=x.ndim - 1)


def exchange_groups(a):
    lane = lanes(a[0].shape)
    low = lane < 64
    even = (lane // 32) % 2 == 0
    b0 = jnp.where(low, a[0], roll_lanes(a[2], 64))
    b2 = jnp.where(low, roll_lanes(a[0], 64), a[2])
    b1 = jnp.where(low, a[1], roll_lanes(a[3], 64))
    b3 = jnp.where(low, roll_lanes(a[1], 64), a[3])
    return (
        jnp.where(even, b0, roll_lanes(b1, 32)),
        jnp.where(even, roll_lanes(b0, 96), b1),
        jnp.where(even, b2, roll_lanes(b3, 32)),
        jnp.where(even, roll_lanes(b2, 96), b3),
    )


def reverse8(x):
    place = lax.broadcasted_iota(jnp.int32, x.shape, 0)
    x = pltpu.roll(x, 4, axis=0)
    x = jnp.where(place % 4 < 2, pltpu.roll(x, 6, axis=0), pltpu.roll(x, 2, axis=0))
    return jnp.where(place % 2 < 1, pltpu.roll(x, 7, axis=0), pltpu.roll(x, 1, axis=0))


def reverse_rows(x):
    blocks = x.shape[0] // 8
    return jnp.concatenate(
        [reverse8(x[8 * k : 8 * k + 8]) for k in range(blocks - 1, -1, -1)], axis=0
    )


def reverse_columns(x):
    even = (lanes(x.shape) // 32) % 2 == 0
    return reverse_rows(jnp.where(even, roll_lanes(x, 32), roll_lanes(x, 96)))


def pack_sums(p):
    p = [x[0:8] + x[8:16] + (x[16:24] + x[24:32]) for x in p]
    lane = lanes(p[0].shape)
    low = lane < 64
    even = (lane // 32) % 2 == 0
    x = jnp.where(low, p[0] + roll_lanes(p[0], 64), p[2] + roll_lanes(p[2], 64))
    y = jnp.where(low, p[1] + roll_lanes(p[1], 64), p[3] + roll_lanes(p[3], 64))
    z = jnp.where(even, x + roll_lanes(x, 96), y + roll_lanes(y, 32))
    return jnp.sum(z, axis=0, keepdims=True)


def spread(row):
    lane = lanes(row.shape)
    out = []
    for k in range(4):
        x = jnp.where(lane // 32 == k, row, 0.0)
        x = x + roll_lanes(x, 64)
        out.append(x + roll_lanes(x, 32))
    return out


def pick(row, group):
    row = jnp.where(lanes(row.shape) // 32 == group, row, 0.0)
    row = row + roll_lanes(row, 64)
    return row + roll_lanes(row, 32)


def kernel(
    u_hbm, v_hbm, fraction_hbm, thickness_hbm, land_hbm, codes_hbm, field, images, factors,
    u_buf, v_buf, fraction, thickness, land, codes, tu1, tv1, weight, tu2, tv2, g_buf, q_buf, qsum, stage,
    edge_send, edge_recv, tu_send, tu_recv, tv_send, tv_recv, d_recv,
    corner_send, corner_recv, a1, b1, a2, b2,
    load_sem, small_sem, send_sem, recv_sem, ar_send, ar_recv,
):
    me = lax.axis_index("tile")
    east, west = lax.rem(me + 1, N_TILE), lax.rem(me + N_TILE - 1, N_TILE)
    north, south = lax.rem(me + NTX, N_TILE), lax.rem(me + N_TILE - NTX, N_TILE)
    diagonal = {n: lax.rem(me + N_TILE + n, N_TILE) for n in (-17, -15, 15, 17)}
    level, place = me // PLANE, lax.rem(me, PLANE)
    plane_peers = [level * PLANE + lax.rem(place + d, PLANE) for d in range(1, PLANE)]
    level_peers = [lax.rem(level + d, DEPTH) * PLANE + place for d in range(1, DEPTH)]

    small_loads = []
    pairs = ((thickness_hbm, thickness), (codes_hbm, codes), (fraction_hbm, fraction), (land_hbm, land))
    for n, (src, dst) in enumerate(pairs):
        copy = pltpu.make_async_copy(src, dst, small_sem.at[n])
        copy.start()
        small_loads.append(copy)
    part = MEMB // CHUNKS
    loads = []
    for c in range(CHUNKS):
        for n, (src, dst) in enumerate(((u_hbm, u_buf), (v_hbm, v_buf))):
            at = pl.ds(c * part, part)
            copy = pltpu.make_async_copy(src.at[at], dst.at[at], load_sem.at[n, c])
            copy.start()
            loads.append(copy)

    barrier = pltpu.get_barrier_semaphore()
    greeted = [east, west, north, south] + list(diagonal.values()) + plane_peers + level_peers
    for peer in greeted:
        pl.semaphore_signal(barrier, inc=1, device_id=(peer,), device_id_type=MESH)

    for copy in small_loads:
        copy.wait()
    flip = [codes[0, k] == 1 for k in range(4)]

    depth = None
    for k in range(LEV):
        w = thickness[k] * fraction[k].astype(F32)
        weight[k] = w
        depth = w if depth is None else depth + w
    root = 0.5 * jnp.sqrt(land[...].astype(F32) * depth)
    stage[...] = root

    def to_groups(rows_of, store):
        for block in range(4):
            z = jnp.concatenate([rows_of(4 * block + k) for k in range(4)], axis=0)
            t = jnp.transpose(z)
            out = exchange_groups([t[32 * g : 32 * g + 32] for g in range(4)])
            for k in range(4):
                store(4 * block + k, out[k])

    def inner(i):
        start = (i + 1) * PITCH + 8
        if not isinstance(i, int):
            start = pl.multiple_of(start, 8)
        return pl.ds(start, 32)

    def column(s):
        return pl.ds(PITCH + 8 + s, TY, stride=PITCH)

    def store_q(i, value):
        q_buf[i] = value
        g_buf[0, inner(i), :] = value

    to_groups(lambda i: jnp.broadcast_to(stage[pl.ds(i, 1), :], (MEMB, TX)), store_q)

    def column_sums(src, dst, n):
        for c in range(CHUNKS):
            loads[2 * c + n].wait()

            def member(m, carry):
                total = weight[0] * src[m, 0].astype(F32)
                for k in range(1, LEV):
                    total = total + weight[k] * src[m, k].astype(F32)
                dst[pl.ds(pl.multiple_of(m * TY, TY), TY), :] = total
                return carry

            lax.fori_loop(c * part, (c + 1) * part, member, 0, unroll=2)

    def remote(src, dst, index, direction, peer):
        return pltpu.make_async_remote_copy(
            src_ref=src, dst_ref=dst,
            send_sem=send_sem.at[index, direction], recv_sem=recv_sem.at[index, direction],
            device_id=(peer,), device_id_type=MESH,
        )

    def edges(k):
        from_north, from_south = g_buf.at[k, pl.ds(17 * PITCH + 8, 32)], g_buf.at[k, pl.ds(8, 32)]
        if k == 1:
            from_north, from_south = d_recv.at[0], d_recv.at[1]
        return [
            remote(edge_send.at[k, 2], from_north, k, 2, south),
            remote(edge_send.at[k, 3], from_south, k, 3, north),
            remote(edge_send.at[k, 0, pl.ds(0, TY)], edge_recv.at[k, 0], k, 0, west),
            remote(edge_send.at[k, 1, pl.ds(0, TY)], edge_recv.at[k, 1], k, 1, east),
        ]

    def put_rows(k, low=None, high=None):
        if low is None:
            low, high = g_buf[k, inner(0), :], g_buf[k, inner(TY - 1), :]
        edge_send[k, 2] = jnp.where(flip[3], reverse_columns(low), low)
        edge_send[k, 3] = jnp.where(flip[2], reverse_columns(high), high)

    def put_columns(k, first=None, last=None):
        if first is None:
            first, last = g_buf[k, column(0), :], g_buf[k, column(31), :]
        to_west = roll_lanes(first, 96)
        to_east = roll_lanes(last, 32)
        edge_send[k, 0, pl.ds(0, TY)] = jnp.where(flip[1], reverse_rows(to_west), to_west)
        edge_send[k, 1, pl.ds(0, TY)] = jnp.where(flip[0], reverse_rows(to_east), to_east)
        return to_west, to_east

    def take_columns(k, to_west, to_east):
        lane = lanes(to_west.shape)
        g_buf[k, column(32), :] = jnp.where(lane < 96, to_west, edge_recv[k, 0])
        g_buf[k, column(-1), :] = jnp.where(lane >= 32, to_east, edge_recv[k, 1])

    sent = []

    def send_rows(k, *values):
        put_rows(k, *values)
        copies = edges(k)
        copies[0].start()
        copies[1].start()
        sent.extend(copies)
        return copies

    def send_columns(k, copies, *values):
        own = put_columns(k, *values)
        copies[2].start()
        copies[3].start()
        return own

    def around(k, i):
        here = inner(i)
        base = here.start
        return (g_buf[k, pl.ds(base + 1, 32), :] + g_buf[k, pl.ds(base - 1, 32), :]) + (
            g_buf[k, inner(i + 1), :] + g_buf[k, inner(i - 1), :]
        )

    column_sums(u_buf, tu1, 0)
    column_sums(v_buf, tv1, 1)

    def store_tu(i, value):
        tu2[inner(i), :] = value

    def store_tv(i, value):
        tv2[pl.ds(i * 32, 32), :] = value

    to_groups(lambda i: tv1[pl.ds(i, MEMB, stride=TY), :], store_tv)
    to_groups(lambda i: tu1[pl.ds(i, MEMB, stride=TY), :], store_tu)

    tv_row = tv2[pl.ds(0, 32), :]
    tv_send[...] = jnp.where(flip[3], reverse_columns(tv_row), tv_row)
    tu_column = tu2[column(0), :]
    own_tu = roll_lanes(tu_column, 96)
    tu_send[...] = jnp.where(flip[1], reverse_rows(own_tu), own_tu)
    last_lanes = lanes(own_tu.shape) >= 96
    tu2[column(32), :] = jnp.where(last_lanes, 0.0, own_tu)
    tv2[pl.ds(TY * 32, 32), :] = jnp.zeros((32, 128), F32)

    def part_row(i):
        here, below = inner(i), i * 32
        return (
            tu2[here, :] - tu2[pl.ds(here.start + 1, 32), :]
            + tv2[pl.ds(below, 32), :] - tv2[pl.ds(below + 32, 32), :]
        )

    def part_column(n):
        return (
            tu2[column(n), :] - tu2[column(n + 1), :]
            + tv2[pl.ds(n, TY, stride=32), :] - tv2[pl.ds(n + 32, TY, stride=32), :]
        )

    low, high = tu2[pl.ds(PITCH + 8, 1), :], tu2[pl.ds(TY * PITCH + 8, 1), :]
    left, right = pick(tv2[pl.ds(0, 1), :], 0), pick(tv2[pl.ds(31, 1), :], 3)
    corner_send[0] = pick(jnp.where(flip[1], high, low), 0)
    corner_send[1] = jnp.where(flip[3], right, left)
    corner_send[2] = pick(jnp.where(flip[1], low, high), 0)
    corner_send[3] = jnp.where(flip[3], left, right)

    def corner(start, size, direction, peer):
        at = pl.ds(start, size)
        return remote(corner_send.at[at], corner_recv.at[at], 6, direction, peer)

    pl.semaphore_wait(barrier, len(greeted))
    corners = [
        corner(0, 2, 0, diagonal[-17]), corner(2, 1, 1, diagonal[15]), corner(3, 1, 2, diagonal[-15]),
    ]
    for copy in corners:
        copy.start()
    tv_copy = remote(tv_send, tv_recv, 5, 2, south)
    tv_copy.start()
    tu_copy = remote(tu_send, tu_recv, 5, 0, west)
    tu_copy.start()
    parts = send_rows(1, part_row(0), part_row(TY - 1))
    send_columns(1, parts, part_column(0), part_column(31))
    copies = send_rows(0)
    own = send_columns(0, copies)
    tu_copy.wait_recv()
    tu2[column(32), :] = jnp.where(last_lanes, tu_recv[...], own_tu)
    copies[2].wait_recv()
    copies[3].wait_recv()
    take_columns(0, *own)

    zero = jnp.zeros((32, 128), F32)

    def first(i, total):
        q = q_buf[i]
        here = inner(i)
        below = i * 32 if isinstance(i, int) else pl.multiple_of(i * 32, 32)
        value = (
            tu2[here, :] - tu2[pl.ds(here.start + 1, 32), :]
            + tv2[pl.ds(below, 32), :] - tv2[pl.ds(below + 32, 32), :]
        )
        value = jnp.where(q > 0.0, value, 0.0)
        qsum[i] = around(0, i)
        field[0, i] = value
        g_buf[1, here, :] = q * value
        return total + value * value

    def middle(body, start):
        return lax.fori_loop(1, TY - 1, body, start, unroll=UNROLL)

    n0 = middle(first, zero)
    tv_copy.wait_recv()
    tv2[pl.ds(TY * 32, 32), :] = tv_recv[...]
    copies[0].wait_recv()
    copies[1].wait_recv()
    n0 = first(TY - 1, first(0, n0))
    for copy in parts + corners:
        copy.wait_recv()
    row_shape = (32, 128)
    position = lanes(row_shape) // 32 * 32 + lax.broadcasted_iota(jnp.int32, row_shape, 0)

    def at_end(shape_position, flipped, last, value):
        return jnp.where(shape_position == jnp.where(flipped, 0, last), value, 0.0)

    north_ghost, south_ghost = pl.ds(17 * PITCH + 8, 32), pl.ds(8, 32)
    g_buf[1, north_ghost, :] = g_buf[0, north_ghost, :] * (
        d_recv[0] - at_end(position, flip[2], TX - 1, corner_recv[0])
    )
    g_buf[1, south_ghost, :] = g_buf[0, south_ghost, :] * (
        d_recv[1] - tv_row - at_end(position, flip[3], TX - 1, corner_recv[2])
    )
    index = lax.broadcasted_iota(jnp.int32, (TY, 128), 0)
    lane = lanes((TY, 128))
    from_east = edge_recv[1, 0] - at_end(index, flip[0], TY - 1, corner_recv[1])
    from_west = edge_recv[1, 1] - tu_column - at_end(index, flip[1], TY - 1, corner_recv[3])
    g_buf[1, column(32), :] = jnp.where(
        lane < 96, roll_lanes(g_buf[1, column(0), :], 96), g_buf[0, column(32), :] * from_east
    )
    g_buf[1, column(-1), :] = jnp.where(
        lane >= 32, roll_lanes(g_buf[1, column(31), :], 32), g_buf[0, column(-1), :] * from_west
    )

    def image(k, copies, own, square):
        def step(i, totals):
            q, old = q_buf[i], field[k - 1, i]
            value = q * (qsum[i] * old - around(k, i))
            field[k, i] = value
            if k < 4:
                g_buf[k + 1, inner(i), :] = q * value
            if square is None:
                return totals
            cross, own_square = totals
            return cross + old * value, own_square + value * value if square else own_square

        if k == 1:
            totals = step(TY - 1, step(0, (zero, zero)))
            ahead = send_rows(2)
            totals = middle(step, totals)
            return totals, ahead, send_columns(2, ahead)
        copies[2].wait_recv()
        copies[3].wait_recv()
        take_columns(k, *own)
        totals = middle(step, (zero, zero))
        copies[0].wait_recv()
        copies[1].wait_recv()
        totals = step(TY - 1, step(0, totals))
        if k == 4:
            return totals
        ahead = send_rows(k + 1)
        return totals, ahead, send_columns(k + 1, ahead)

    def fan(buf, slot, peers, phase, which):
        def copy_to(peer):
            return pltpu.make_async_remote_copy(
                src_ref=buf.at[slot], dst_ref=buf.at[slot],
                send_sem=ar_send.at[which, phase], recv_sem=ar_recv.at[which, phase],
                device_id=(peer,), device_id_type=MESH,
            )

        for peer in peers:
            copy_to(peer).start()

    def fan_wait(buf, count, sem):
        pltpu.make_async_copy(buf.at[pl.ds(0, count)], buf.at[pl.ds(0, count)], sem).wait()

    def start_level(values, buf, which):
        buf[place] = values
        fan(buf, place, plane_peers, 0, which)

    def cross_levels(buf_a, buf_b, which):
        fan_wait(buf_a, PLANE - 1, ar_recv.at[which, 0])
        buf_b[level] = jnp.sum(buf_a[...], axis=0)
        fan(buf_b, level, level_peers, 1, which)

    def finish(buf_b, which):
        fan_wait(buf_b, DEPTH - 1, ar_recv.at[which, 1])
        return jnp.sum(buf_b[...], axis=0)

    (n1, n2), flight, own = image(1, None, None, True)
    (n3, _), flight, own = image(2, flight, own, False)
    start_level(pack_sums([n0, n1, n2, n3]), a1, 0)
    _, flight, own = image(3, flight, own, None)
    cross_levels(a1, b1, 0)
    image(4, flight, own, None)
    s0, s1, s2, s3 = spread(finish(b1, 0))

    m0, m1, m2, m3 = s0, s0 + s1, s0 + 2.0 * s1 + s2, s0 + 3.0 * (s1 + s2) + s3
    alpha0 = m0 / m1
    rr1 = m0 - alpha0 * (2.0 * m1 - alpha0 * m2)
    gain = 1.0 + rr1 / m0
    alpha1 = rr1 / (gain * gain * m1 - alpha0 * (2.0 * gain * m2 - alpha0 * m3))
    lead = alpha0 * alpha1
    lin = -(alpha0 + alpha1 * gain)
    c0, c1, c2 = 1.0 + lin + lead, lin + 2.0 * lead, lead
    e0, e1 = gain - alpha0, -alpha0
    x0, x1 = -lin - lead, -lead

    def rows(*values):
        return [jnp.broadcast_to(v, (32, 128)) for v in values]

    c0b, c1b, c2b, e0b, e1b = rows(c0, c1, c2, e0, e1)

    def second(i, totals):
        v = [field[k, i] for k in range(5)]
        r = [c0b * v[k] + c1b * v[k + 1] + c2b * v[k + 2] for k in range(3)]
        d = [e0b * v[k] + e1b * v[k + 1] for k in range(3)]
        for k in range(3):
            images[k, i] = r[k]
            images[3 + k, i] = d[k]
        pairs = (
            (r[0], r[0]), (r[0], d[0]), (d[0], d[0]), (r[0], r[1]),
            (r[0], d[1]), (d[0], d[1]), (r[1], r[1]), (r[1], d[1]),
            (d[1], d[1]), (r[1], r[2]), (r[1], d[2]), (d[1], d[2]),
        )
        out = []
        for t, (x, y) in zip(totals, pairs):
            p = x * y
            out.append(t + (p[0:8] + p[8:16] + (p[16:24] + p[24:32])))
        return tuple(out)

    small = jnp.zeros((8, 128), F32)
    totals = lax.fori_loop(0, TY, second, (small,) * 12, unroll=2)
    wide = [jnp.concatenate([t, jnp.zeros((24, 128), F32)], axis=0) for t in totals]
    packed = [pack_sums(wide[4 * k : 4 * k + 4]) for k in range(3)]
    start_level(jnp.concatenate(packed + [packed[0] * 0.0], axis=0), a2, 1)
    cross_levels(a2, b2, 1)
    sums = finish(b2, 1)
    rr, rd, dd, rr_1 = spread(sums[0:1])
    rd_1, dd_1, rr_2, rd_2 = spread(sums[1:2])
    dd_2, rr_3, rd_3, dd_3 = spread(sums[2:3])
    r1 = rr + rr_1
    r2 = rr + 2.0 * rr_1 + rr_2
    r3 = rr + 3.0 * (rr_1 + rr_2) + rr_3
    y1 = rd + rd_1
    y2 = rd + 2.0 * rd_1 + rd_2
    y3 = rd + 3.0 * (rd_1 + rd_2) + rd_3
    d1 = dd + dd_1
    d2 = dd + 2.0 * dd_1 + dd_2
    d3 = dd + 3.0 * (dd_1 + dd_2) + dd_3
    beta1 = rr / rr1
    p1 = r1 + beta1 * (2.0 * y1 + beta1 * d1)
    p2 = r2 + beta1 * (2.0 * y2 + beta1 * d2)
    p3 = r3 + beta1 * (2.0 * y3 + beta1 * d3)
    rp1 = r1 + beta1 * y1
    rp2 = r2 + beta1 * y2
    alpha2 = rr / p1
    rr3 = rr - alpha2 * (2.0 * rp1 - alpha2 * p2)
    beta2 = rr3 / rr
    q1 = (
        r1 + alpha2 * (alpha2 * p3 - 2.0 * rp2)
        + beta2 * (2.0 * (rp1 - alpha2 * p2) + beta2 * p1)
    )
    alpha3 = rr3 / q1
    kappa = alpha2 + alpha3 * beta2
    mu = alpha2 * alpha3
    xp0 = kappa - mu
    xr0, xr1 = xp0 + alpha3, -mu
    xd0, xd1 = beta1 * xp0, -beta1 * mu
    fp0, fp1, fp2 = mu - kappa, 2.0 * mu - kappa, mu
    fr0, fr1, fr2 = 1.0 + fp0 - alpha3, fp1 - alpha3, fp2
    fd0, fd1, fd2 = beta1 * fp0, beta1 * fp1, beta1 * fp2
    for k, factor in enumerate((x0, x1, xr0, xr1, xd0, xd1, fr0, fr1, fr2, fd0, fd1, fd2)):
        factors[k] = jnp.broadcast_to(factor, (8, 128))

    for copy in sent + corners + [tv_copy, tu_copy]:
        copy.wait_send()
    fan_wait(a1, PLANE - 1, ar_send.at[0, 0])
    fan_wait(b1, DEPTH - 1, ar_send.at[0, 1])
    fan_wait(a2, PLANE - 1, ar_send.at[1, 0])
    fan_wait(b2, DEPTH - 1, ar_send.at[1, 1])


def combine(field, images, factors, x_hbm, r_hbm, x_buf, r_buf, sem):
    c = [jnp.concatenate([factors[k]] * 4, axis=0) for k in range(12)]
    parts = (
        [functools.partial(lambda ref, n, i: ref[n, i], field, n) for n in (0, 1)]
        + [functools.partial(lambda ref, n, i: ref[n, i], images, n) for n in (0, 1, 3, 4)],
        [functools.partial(lambda ref, n, i: ref[n, i], images, n) for n in range(6)],
    )
    copies = []
    for half in range(2):
        for which, (buf, hbm) in enumerate(((x_buf, x_hbm), (r_buf, r_hbm))):
            for block in (2 * half, 2 * half + 1):
                values = []
                for i in range(4 * block, 4 * block + 4):
                    terms = [f * part(i) for f, part in zip(c[6 * which : 6 * which + 6], parts[which])]
                    values.append(functools.reduce(lambda s, t: s + t, terms))
                t = jnp.transpose(jnp.concatenate(exchange_groups(values), axis=0))
                for k in range(4):
                    at = pl.ds(4 * (block % 2) + k, MEMB, stride=8)
                    buf[half, at, :] = t[32 * k : 32 * k + 32]
            copy = pltpu.make_async_copy(
                buf.at[half].reshape(MEMB, 8, TX), hbm.at[:, pl.ds(8 * half, 8)], sem.at[half, which]
            )
            copy.start()
            copies.append(copy)
    for copy in copies:
        copy.wait()


def on_device(zonal, meridional, fraction, thickness, land, codes):
    vmem = pl.BlockSpec(memory_space=pltpu.VMEM)
    hbm = pl.BlockSpec(memory_space=pltpu.HBM)
    arguments = [
        pltpu.with_memory_space_constraint(x, pltpu.HBM)
        for x in (zonal, meridional, fraction, thickness, land, codes)
    ]
    whole = jax.ShapeDtypeStruct((MEMB, TY, TX), F32)
    padded = (TY + 2) * PITCH
    field, images, factors = pl.pallas_call(
        kernel,
        out_shape=(
            jax.ShapeDtypeStruct((5, TY, 32, 128), F32),
            jax.ShapeDtypeStruct((6, TY, 32, 128), F32),
            jax.ShapeDtypeStruct((12, 8, 128), F32),
        ),
        in_specs=[hbm] * 6,
        out_specs=(vmem, vmem, vmem),
        scratch_shapes=[
            pltpu.VMEM((MEMB, LEV, TY, TX), jnp.bfloat16),
            pltpu.VMEM((MEMB, LEV, TY, TX), jnp.bfloat16),
            pltpu.VMEM((LEV, TY, TX), jnp.bfloat16),
            pltpu.SMEM((LEV,), F32),
            pltpu.VMEM((TY, TX), jnp.int32),
            pltpu.SMEM((1, 4), jnp.int32),
            pltpu.VMEM((MEMB * TY, TX), F32),
            pltpu.VMEM((MEMB * TY, TX), F32),
            pltpu.VMEM((LEV, TY, TX), F32),
            pltpu.VMEM((padded, 128), F32),
            pltpu.VMEM(((TY + 1) * 32, 128), F32),
            pltpu.VMEM((5, padded, 128), F32),
            pltpu.VMEM((TY, 32, 128), F32),
            pltpu.VMEM((TY, 32, 128), F32),
            pltpu.VMEM((TY, TX), F32),
            pltpu.VMEM((5, 4, 32, 128), F32),
            pltpu.VMEM((5, 2, TY, 128), F32),
            pltpu.VMEM((TY, 128), F32),
            pltpu.VMEM((TY, 128), F32),
            pltpu.VMEM((32, 128), F32),
            pltpu.VMEM((32, 128), F32),
            pltpu.VMEM((2, 32, 128), F32),
            pltpu.VMEM((4, 1, 128), F32),
            pltpu.VMEM((4, 1, 128), F32),
            pltpu.VMEM((PLANE, 1, 128), F32),
            pltpu.VMEM((DEPTH, 1, 128), F32),
            pltpu.VMEM((PLANE, 4, 128), F32),
            pltpu.VMEM((DEPTH, 4, 128), F32),
            pltpu.SemaphoreType.DMA((2, CHUNKS)),
            pltpu.SemaphoreType.DMA((4,)),
            pltpu.SemaphoreType.DMA((7, 4)),
            pltpu.SemaphoreType.DMA((7, 4)),
            pltpu.SemaphoreType.DMA((2, 2)),
            pltpu.SemaphoreType.DMA((2, 2)),
        ],
        compiler_params=pltpu.CompilerParams(
            collective_id=0, has_side_effects=True, vmem_limit_bytes=40 << 20
        ),
    )(*arguments)
    return pl.pallas_call(
        combine,
        out_shape=(whole, whole),
        in_specs=[vmem] * 3,
        out_specs=(hbm, hbm),
        scratch_shapes=[
            pltpu.VMEM((2, MEMB * 8, TX), F32),
            pltpu.VMEM((2, MEMB * 8, TX), F32),
            pltpu.SemaphoreType.DMA((2, 2)),
        ],
        compiler_params=pltpu.CompilerParams(vmem_limit_bytes=16 << 20),
    )(field, images, factors)


def solution(mesh):
    in_specs = (
        P(None, None, "tile", None),
        P(None, None, "tile", None),
        P(None, "tile", None),
        P(),
        P("tile", None),
        P("tile", None),
    )
    out_specs = (P(None, "tile", None), P(None, "tile", None))
    return jax.shard_map(
        on_device, mesh=mesh, in_specs=in_specs, out_specs=out_specs, check_vma=False
    )
```

```python
import functools

import jax
import jax.numpy as jnp
from jax import lax
from jax.experimental import pallas as pl
from jax.experimental.pallas import tpu as pltpu
from jax.sharding import PartitionSpec as P

MESH = pl.DeviceIdType.MESH
F32 = jnp.float32
MEMB, LEV, TY, TX = 32, 8, 16, 128
NTX = 16
PLANE, DEPTH = 32, 8
N_TILE = PLANE * DEPTH
PITCH = 48
UNROLL = 4
CHUNKS = 4


def lanes(shape):
    return lax.broadcasted_iota(jnp.int32, shape, len(shape) - 1)


def roll_lanes(x, shift):
    return pltpu.roll(x, shift % 128, axis=x.ndim - 1)


def exchange_groups(a):
    lane = lanes(a[0].shape)
    low = lane < 64
    even = (lane // 32) % 2 == 0
    b0 = jnp.where(low, a[0], roll_lanes(a[2], 64))
    b2 = jnp.where(low, roll_lanes(a[0], 64), a[2])
    b1 = jnp.where(low, a[1], roll_lanes(a[3], 64))
    b3 = jnp.where(low, roll_lanes(a[1], 64), a[3])
    return (
        jnp.where(even, b0, roll_lanes(b1, 32)),
        jnp.where(even, roll_lanes(b0, 96), b1),
        jnp.where(even, b2, roll_lanes(b3, 32)),
        jnp.where(even, roll_lanes(b2, 96), b3),
    )


def reverse8(x):
    place = lax.broadcasted_iota(jnp.int32, x.shape, 0)
    x = pltpu.roll(x, 4, axis=0)
    x = jnp.where(place % 4 < 2, pltpu.roll(x, 6, axis=0), pltpu.roll(x, 2, axis=0))
    return jnp.where(place % 2 < 1, pltpu.roll(x, 7, axis=0), pltpu.roll(x, 1, axis=0))


def reverse_rows(x):
    blocks = x.shape[0] // 8
    return jnp.concatenate(
        [reverse8(x[8 * k : 8 * k + 8]) for k in range(blocks - 1, -1, -1)], axis=0
    )


def reverse_columns(x):
    even = (lanes(x.shape) // 32) % 2 == 0
    return reverse_rows(jnp.where(even, roll_lanes(x, 32), roll_lanes(x, 96)))


def pack_sums(p):
    return fold([x[0:8] + x[8:16] + (x[16:24] + x[24:32]) for x in p])


def fold(p):
    lane = lanes(p[0].shape)
    low = lane < 64
    even = (lane // 32) % 2 == 0
    x = jnp.where(low, p[0] + roll_lanes(p[0], 64), p[2] + roll_lanes(p[2], 64))
    y = jnp.where(low, p[1] + roll_lanes(p[1], 64), p[3] + roll_lanes(p[3], 64))
    z = jnp.where(even, x + roll_lanes(x, 96), y + roll_lanes(y, 32))
    return jnp.sum(z, axis=0, keepdims=True)


def spread(row):
    lane = lanes(row.shape)
    out = []
    for k in range(4):
        x = jnp.where(lane // 32 == k, row, 0.0)
        x = x + roll_lanes(x, 64)
        out.append(x + roll_lanes(x, 32))
    return out


def pick(row, group):
    row = jnp.where(lanes(row.shape) // 32 == group, row, 0.0)
    row = row + roll_lanes(row, 64)
    return row + roll_lanes(row, 32)


def kernel(
    u_hbm, v_hbm, fraction_hbm, thickness_hbm, land_hbm, codes_hbm, field, factors,
    u_buf, v_buf, fraction, thickness, land, codes, tu1, tv1, weight, tu2, tv2, g_buf, q_buf, qsum, stage,
    edge_send, edge_recv, tu_send, tu_recv, tv_send, tv_recv, row_recv,
    corner_send, corner_recv, a1, b1, a2, b2,
    load_sem, small_sem, send_sem, recv_sem, ar_send, ar_recv,
):
    me = lax.axis_index("tile")
    east, west = lax.rem(me + 1, N_TILE), lax.rem(me + N_TILE - 1, N_TILE)
    north, south = lax.rem(me + NTX, N_TILE), lax.rem(me + N_TILE - NTX, N_TILE)
    diagonal = {n: lax.rem(me + N_TILE + n, N_TILE) for n in (-17, -15, 15, 17)}
    level, place = me // PLANE, lax.rem(me, PLANE)
    plane_peers = [level * PLANE + lax.rem(place + d, PLANE) for d in range(1, PLANE)]
    level_peers = [lax.rem(level + d, DEPTH) * PLANE + place for d in range(1, DEPTH)]

    small_loads = []
    pairs = ((thickness_hbm, thickness), (codes_hbm, codes), (fraction_hbm, fraction), (land_hbm, land))
    for n, (src, dst) in enumerate(pairs):
        copy = pltpu.make_async_copy(src, dst, small_sem.at[n])
        copy.start()
        small_loads.append(copy)
    part = MEMB // CHUNKS
    loads = []
    for c in range(CHUNKS):
        for n, (src, dst) in enumerate(((u_hbm, u_buf), (v_hbm, v_buf))):
            at = pl.ds(c * part, part)
            copy = pltpu.make_async_copy(src.at[at], dst.at[at], load_sem.at[n, c])
            copy.start()
            loads.append(copy)

    barrier = pltpu.get_barrier_semaphore()
    greeted = [east, west, north, south] + list(diagonal.values()) + plane_peers + level_peers
    for peer in greeted:
        pl.semaphore_signal(barrier, inc=1, device_id=(peer,), device_id_type=MESH)

    for copy in small_loads:
        copy.wait()
    flip = [codes[0, k] == 1 for k in range(4)]

    total = thickness[0]
    for k in range(1, LEV):
        total = total + thickness[k]
    shift = 1.0 + 0.125 * total

    depth = None
    for k in range(LEV):
        w = thickness[k] * fraction[k].astype(F32)
        weight[k] = w
        depth = w if depth is None else depth + w
    root = 0.5 * jnp.sqrt(land[...].astype(F32) * depth)
    stage[...] = root

    def to_groups(rows_of, store):
        for block in range(4):
            z = jnp.concatenate([rows_of(4 * block + k) for k in range(4)], axis=0)
            t = jnp.transpose(z)
            out = exchange_groups([t[32 * g : 32 * g + 32] for g in range(4)])
            for k in range(4):
                store(4 * block + k, out[k])

    def inner(i):
        start = (i + 1) * PITCH + 8
        if not isinstance(i, int):
            start = pl.multiple_of(start, 8)
        return pl.ds(start, 32)

    def column(s):
        return pl.ds(PITCH + 8 + s, TY, stride=PITCH)

    def store_q(i, value):
        q_buf[i] = value
        g_buf[0, inner(i), :] = value

    to_groups(lambda i: jnp.broadcast_to(stage[pl.ds(i, 1), :], (MEMB, TX)), store_q)

    def column_sums(src, dst, n):
        for c in range(CHUNKS):
            loads[2 * c + n].wait()

            def member(m, carry):
                total = weight[0] * src[m, 0].astype(F32)
                for k in range(1, LEV):
                    total = total + weight[k] * src[m, k].astype(F32)
                dst[pl.ds(pl.multiple_of(m * TY, TY), TY), :] = total
                return carry

            lax.fori_loop(c * part, (c + 1) * part, member, 0, unroll=2)

    def remote(src, dst, index, direction, peer):
        return pltpu.make_async_remote_copy(
            src_ref=src, dst_ref=dst,
            send_sem=send_sem.at[index, direction], recv_sem=recv_sem.at[index, direction],
            device_id=(peer,), device_id_type=MESH,
        )

    def edges(k):
        if k == 0:
            from_north, from_south = g_buf.at[0, pl.ds(17 * PITCH + 8, 32)], g_buf.at[0, pl.ds(8, 32)]
        else:
            from_north, from_south = row_recv.at[k - 1, 0], row_recv.at[k - 1, 1]
        return [
            remote(edge_send.at[k, 2], from_north, k, 2, south),
            remote(edge_send.at[k, 3], from_south, k, 3, north),
            remote(edge_send.at[k, 0, pl.ds(0, TY)], edge_recv.at[k, 0], k, 0, west),
            remote(edge_send.at[k, 1, pl.ds(0, TY)], edge_recv.at[k, 1], k, 1, east),
        ]

    def put_rows(k, low=None, high=None):
        if low is None:
            low, high = g_buf[k, inner(0), :], g_buf[k, inner(TY - 1), :]
        edge_send[k, 2] = jnp.where(flip[3], reverse_columns(low), low)
        edge_send[k, 3] = jnp.where(flip[2], reverse_columns(high), high)

    def put_columns(k, first=None, last=None):
        if first is None:
            first, last = g_buf[k, column(0), :], g_buf[k, column(31), :]
        to_west = roll_lanes(first, 96)
        to_east = roll_lanes(last, 32)
        edge_send[k, 0, pl.ds(0, TY)] = jnp.where(flip[1], reverse_rows(to_west), to_west)
        edge_send[k, 1, pl.ds(0, TY)] = jnp.where(flip[0], reverse_rows(to_east), to_east)
        return to_west, to_east

    def take_columns(k, to_west, to_east):
        lane = lanes(to_west.shape)
        g_buf[k, column(32), :] = jnp.where(lane < 96, to_west, edge_recv[k, 0])
        g_buf[k, column(-1), :] = jnp.where(lane >= 32, to_east, edge_recv[k, 1])

    sent = []
    blank = jnp.zeros((32, 128), F32)
    for k in range(2, 5):
        if k != 3:
            g_buf[k, pl.ds(8, 32), :] = blank
            g_buf[k, pl.ds(17 * PITCH + 8, 32), :] = blank

    def send_rows(k, *values):
        put_rows(k, *values)
        copies = edges(k)
        copies[0].start()
        copies[1].start()
        sent.extend(copies)
        return copies

    def send_columns(k, copies, *values):
        own = put_columns(k, *values)
        copies[2].start()
        copies[3].start()
        return own

    def around(k, i):
        here = inner(i)
        base = here.start
        return (g_buf[k, pl.ds(base + 1, 32), :] + g_buf[k, pl.ds(base - 1, 32), :]) + (
            g_buf[k, inner(i + 1), :] + g_buf[k, inner(i - 1), :]
        )

    column_sums(u_buf, tu1, 0)
    column_sums(v_buf, tv1, 1)

    def store_tu(i, value):
        tu2[inner(i), :] = value

    def store_tv(i, value):
        tv2[pl.ds(i * 32, 32), :] = value

    to_groups(lambda i: tv1[pl.ds(i, MEMB, stride=TY), :], store_tv)
    to_groups(lambda i: tu1[pl.ds(i, MEMB, stride=TY), :], store_tu)

    tv_row = tv2[pl.ds(0, 32), :]
    tv_send[...] = jnp.where(flip[3], reverse_columns(tv_row), tv_row)
    tu_column = tu2[column(0), :]
    own_tu = roll_lanes(tu_column, 96)
    tu_send[...] = jnp.where(flip[1], reverse_rows(own_tu), own_tu)
    last_lanes = lanes(own_tu.shape) >= 96
    tu2[column(32), :] = jnp.where(last_lanes, 0.0, own_tu)
    tv2[pl.ds(TY * 32, 32), :] = jnp.zeros((32, 128), F32)

    def part_row(i):
        here, below = inner(i), i * 32
        return (
            tu2[here, :] - tu2[pl.ds(here.start + 1, 32), :]
            + tv2[pl.ds(below, 32), :] - tv2[pl.ds(below + 32, 32), :]
        )

    def part_column(n):
        return (
            tu2[column(n), :] - tu2[column(n + 1), :]
            + tv2[pl.ds(n, TY, stride=32), :] - tv2[pl.ds(n + 32, TY, stride=32), :]
        )

    low, high = tu2[pl.ds(PITCH + 8, 1), :], tu2[pl.ds(TY * PITCH + 8, 1), :]
    left, right = pick(tv2[pl.ds(0, 1), :], 0), pick(tv2[pl.ds(31, 1), :], 3)
    corner_send[0] = pick(jnp.where(flip[1], high, low), 0)
    corner_send[1] = jnp.where(flip[3], right, left)
    corner_send[2] = pick(jnp.where(flip[1], low, high), 0)
    corner_send[3] = jnp.where(flip[3], left, right)

    def corner(start, size, index, direction, peer):
        at = pl.ds(start, size)
        return remote(corner_send.at[at], corner_recv.at[at], index, direction, peer)

    pl.semaphore_wait(barrier, len(greeted))
    corners = [
        corner(0, 2, 6, 0, diagonal[-17]), corner(2, 1, 6, 1, diagonal[15]), corner(3, 1, 6, 2, diagonal[-15]),
    ]
    for copy in corners:
        copy.start()
    tv_copy = remote(tv_send, tv_recv, 5, 2, south)
    tv_copy.start()
    tu_copy = remote(tu_send, tu_recv, 5, 0, west)
    tu_copy.start()
    parts = send_rows(1, part_row(0), part_row(TY - 1))
    send_columns(1, parts, part_column(0), part_column(31))
    copies = send_rows(0)
    own = send_columns(0, copies)
    tu_copy.wait_recv()
    tu2[column(32), :] = jnp.where(last_lanes, tu_recv[...], own_tu)
    copies[2].wait_recv()
    copies[3].wait_recv()
    take_columns(0, *own)

    zero = jnp.zeros((32, 128), F32)

    def first(i, total):
        q = q_buf[i]
        here = inner(i)
        below = i * 32 if isinstance(i, int) else pl.multiple_of(i * 32, 32)
        value = (
            tu2[here, :] - tu2[pl.ds(here.start + 1, 32), :]
            + tv2[pl.ds(below, 32), :] - tv2[pl.ds(below + 32, 32), :]
        )
        value = jnp.where(q > 0.0, value, 0.0)
        qsum[pl.ds(below, 32), :] = q * around(0, i) + (1.0 - shift)
        field[0, i] = value
        g_buf[1, here, :] = q * value
        return total + value * value

    def middle(body, start):
        return lax.fori_loop(1, TY - 1, body, start, unroll=UNROLL)

    n0 = middle(first, zero)
    tv_copy.wait_recv()
    tv2[pl.ds(TY * 32, 32), :] = tv_recv[...]
    copies[0].wait_recv()
    copies[1].wait_recv()
    n0 = first(TY - 1, first(0, n0))
    for copy in parts + corners:
        copy.wait_recv()
    row_shape = (32, 128)
    position = lanes(row_shape) // 32 * 32 + lax.broadcasted_iota(jnp.int32, row_shape, 0)

    def at_end(shape_position, flipped, last, value):
        return jnp.where(shape_position == jnp.where(flipped, 0, last), value, 0.0)

    north_ghost, south_ghost = pl.ds(17 * PITCH + 8, 32), pl.ds(8, 32)
    g_buf[1, north_ghost, :] = g_buf[0, north_ghost, :] * (
        row_recv[0, 0] - at_end(position, flip[2], TX - 1, corner_recv[0])
    )
    g_buf[1, south_ghost, :] = g_buf[0, south_ghost, :] * (
        row_recv[0, 1] - tv_row - at_end(position, flip[3], TX - 1, corner_recv[2])
    )
    index = lax.broadcasted_iota(jnp.int32, (TY, 128), 0)
    lane = lanes((TY, 128))
    from_east = edge_recv[1, 0] - at_end(index, flip[0], TY - 1, corner_recv[1])
    from_west = edge_recv[1, 1] - tu_column - at_end(index, flip[1], TY - 1, corner_recv[3])
    g_buf[1, column(32), :] = jnp.where(
        lane < 96, roll_lanes(g_buf[1, column(0), :], 96), g_buf[0, column(32), :] * from_east
    )
    g_buf[1, column(-1), :] = jnp.where(
        lane >= 32, roll_lanes(g_buf[1, column(31), :], 32), g_buf[0, column(-1), :] * from_west
    )

    def level_of(i):
        return pl.ds(i * 32 if isinstance(i, int) else pl.multiple_of(i * 32, 32), 32)

    def step_of(k):
        def step(i, totals):
            q, old = q_buf[i], field[k - 1, i]
            value = qsum[level_of(i), :] * old - q * around(k, i)
            field[k, i] = value
            if k < 4:
                g_buf[k + 1, inner(i), :] = q * value
            return (totals[0] + old * value, totals[1] + value * value) if k == 1 else totals

        return step

    def flat(k):
        return field.at[k].reshape(TY * 32, 128)

    def field_column(k, n):
        return flat(k)[pl.ds(n, TY, stride=32), :]

    def inside_columns(k):
        first_column, last_column = g_buf[k, column(0), :], g_buf[k, column(31), :]
        g_buf[k, column(32), :] = jnp.where(lane < 96, roll_lanes(first_column, 96), 0.0)
        g_buf[k, column(-1), :] = jnp.where(lane >= 32, roll_lanes(last_column, 32), 0.0)
        return first_column, last_column

    def add_ghosts(k, rows, columns):
        north_row = field[k, TY - 1] - q_buf[TY - 1] * rows[0]
        south_row = field[k, 0] - q_buf[0] * rows[1]
        field[k, TY - 1] = north_row
        field[k, 0] = south_row
        east_column = field_column(k, 31) - jnp.where(lane >= 96, g_buf[0, column(31), :] * columns[0], 0.0)
        west_column = field_column(k, 0) - jnp.where(lane < 32, g_buf[0, column(0), :] * columns[1], 0.0)
        flat(k)[pl.ds(31, TY, stride=32), :] = east_column
        flat(k)[pl.ds(0, TY, stride=32), :] = west_column
        if k < 4:
            g_buf[k + 1, inner(0), :] = q_buf[0] * south_row
            g_buf[k + 1, inner(TY - 1), :] = q_buf[TY - 1] * north_row
            g_buf[k + 1, column(31), :] = g_buf[0, column(31), :] * east_column
            g_buf[k + 1, column(0), :] = g_buf[0, column(0), :] * west_column

    def fan(buf, slot, peers, phase, which):
        def copy_to(peer):
            return pltpu.make_async_remote_copy(
                src_ref=buf.at[slot], dst_ref=buf.at[slot],
                send_sem=ar_send.at[which, phase], recv_sem=ar_recv.at[which, phase],
                device_id=(peer,), device_id_type=MESH,
            )

        for peer in peers:
            copy_to(peer).start()

    def fan_wait(buf, count, sem):
        pltpu.make_async_copy(buf.at[pl.ds(0, count)], buf.at[pl.ds(0, count)], sem).wait()

    def start_level(values, buf, which):
        buf[place] = values
        fan(buf, place, plane_peers, 0, which)

    def cross_levels(buf_a, buf_b, which):
        fan_wait(buf_a, PLANE - 1, ar_recv.at[which, 0])
        buf_b[level] = jnp.sum(buf_a[...], axis=0)
        fan(buf_b, level, level_peers, 1, which)

    def finish(buf_b, which):
        fan_wait(buf_b, DEPTH - 1, ar_recv.at[which, 1])
        return jnp.sum(buf_b[...], axis=0)

    step = step_of(1)
    totals = step(TY - 1, step(0, (zero, zero)))
    flight = send_rows(2)
    n1, n2 = middle(step, totals)
    first_column, last_column = inside_columns(2)
    send_columns(2, flight, first_column, last_column)
    start, end = pl.ds(PITCH + 8, 1), pl.ds(TY * PITCH + 8, 1)
    start_last, end_last = pl.ds(PITCH + 39, 1), pl.ds(TY * PITCH + 39, 1)
    p00, p10 = pick(g_buf[2, start, :], 0), pick(g_buf[2, end, :], 0)
    p01, p11 = pick(g_buf[2, start_last, :], 3), pick(g_buf[2, end_last, :], 3)
    corner_send[4] = jnp.where(flip[1], p10, p00)
    corner_send[5] = jnp.where(flip[3], p01, p00)
    corner_send[6] = jnp.where(flip[0], p11, p01)
    corner_send[7] = jnp.where(flip[3], p00, p01)
    corner_send[8] = jnp.where(flip[1], p00, p10)
    corner_send[9] = jnp.where(flip[2], p11, p10)
    corner_send[10] = jnp.where(flip[0], p01, p11)
    corner_send[11] = jnp.where(flip[2], p10, p11)
    more_corners = [
        corner(4 + 2 * n, 2, 7, n, diagonal[d]) for n, d in enumerate((-17, -15, 15, 17))
    ]
    for copy in more_corners:
        copy.start()
    step = step_of(2)
    step(TY - 1, step(0, ()))
    seconds = send_rows(3, field[2, 0], field[2, TY - 1])
    middle(step, ())
    send_columns(3, seconds, field_column(2, 0), field_column(2, 31))
    start_level(pack_sums([n0, n1, n2, zero]), a1, 0)

    own_rows = g_buf[2, inner(TY - 1), :], g_buf[2, inner(0), :]
    for copy in flight:
        copy.wait_recv()
    add_ghosts(2, (row_recv[1, 0], row_recv[1, 1]), (edge_recv[2, 0], edge_recv[2, 1]))
    for copy in seconds + more_corners:
        copy.wait_recv()

    def ends(shape_position, flipped, last, at_last, at_first):
        return at_end(shape_position, flipped, last, corner_recv[at_last]) + jnp.where(
            shape_position == jnp.where(flipped, last, 0), corner_recv[at_first], 0.0
        )

    for side, ghost, flipped, corner_slots in (
        (0, north_ghost, flip[2], (4, 6)),
        (1, south_ghost, flip[3], (8, 10)),
    ):
        q = g_buf[0, ghost, :]
        missing = own_rows[side] + ends(position, flipped, TX - 1, *corner_slots)
        g_buf[3, ghost, :] = q * (row_recv[2, side] - q * missing)
    q = g_buf[0, column(32), :]
    missing = last_column + ends(index, flip[0], TY - 1, 5, 9)
    g_buf[3, column(32), :] = jnp.where(
        lane < 96, roll_lanes(g_buf[3, column(0), :], 96), q * (edge_recv[3, 0] - q * missing)
    )
    q = g_buf[0, column(-1), :]
    missing = first_column + ends(index, flip[1], TY - 1, 7, 11)
    g_buf[3, column(-1), :] = jnp.where(
        lane >= 32, roll_lanes(g_buf[3, column(31), :], 32), q * (edge_recv[3, 1] - q * missing)
    )

    step = step_of(3)
    step(TY - 1, step(0, ()))
    flight = send_rows(4)
    middle(step, ())
    send_columns(4, flight, *inside_columns(4))
    cross_levels(a1, b1, 0)
    step = step_of(4)
    middle(step, step(TY - 1, step(0, ())))
    for copy in flight:
        copy.wait_recv()
    add_ghosts(4, (row_recv[3, 0], row_recv[3, 1]), (edge_recv[4, 0], edge_recv[4, 1]))
    s0, s1, s2, _ = spread(finish(b1, 0))

    c = shift
    m1 = c * s0 + s1
    m2 = c * (c * s0 + 2.0 * s1) + s2
    alpha0 = s0 / m1
    rr1 = s0 - alpha0 * (2.0 * m1 - alpha0 * m2)
    beta0 = rr1 / s0
    e = (1.0 - alpha0 * c, -alpha0)
    f = (e[0] + beta0, -alpha0)
    wide_e = [jnp.broadcast_to(x, (32, 128)) for x in e]
    wide_f = [jnp.broadcast_to(x, (32, 128)) for x in f]

    def second(i, totals):
        v = [field[k, i] for k in range(5)]
        r = [wide_e[0] * v[k] + wide_e[1] * v[k + 1] for k in range(3)]
        d = [wide_f[0] * v[k] + wide_f[1] * v[k + 1] for k in range(4)]
        pairs = (
            (r[0], r[0]), (r[0], r[1]), (r[1], r[1]), (r[1], r[2]),
            (r[0], d[0]), (r[0], d[1]), (r[1], d[1]), (r[1], d[2]), (r[2], d[2]),
            (d[0], d[0]), (d[0], d[1]), (d[1], d[1]), (d[1], d[2]), (d[2], d[2]), (d[2], d[3]),
        )
        out = []
        for t, (x, y) in zip(totals, pairs):
            p = x * y
            out.append(t + (p[0:8] + p[8:16] + (p[16:24] + p[24:32])))
        return tuple(out)

    small = jnp.zeros((8, 128), F32)
    totals = lax.fori_loop(0, TY, second, (small,) * 15, unroll=2) + (small,)
    start_level(jnp.concatenate([fold(totals[4 * k : 4 * k + 4]) for k in range(4)], axis=0), a2, 1)
    cross_levels(a2, b2, 1)
    sums = finish(b2, 1)
    sums = [x for k in range(4) for x in spread(sums[k : k + 1])]
    rho, sigma, delta = sums[:4], sums[4:9], sums[9:15]

    def dot(a, b):
        terms = []
        for one, other, table in ((a[0], b[0], rho), (a[0], b[1], sigma), (a[1], b[0], sigma), (a[1], b[1], delta)):
            for i, x in enumerate(one):
                inner_sum = functools.reduce(lambda p, n: p + n, [y * table[i + j] for j, y in enumerate(other)], 0.0)
                terms.append(x * inner_sum)
        return functools.reduce(lambda p, n: p + n, terms)

    def operate(a):
        def one(p):
            if not p:
                return []
            return [c * p[0]] + [p[i - 1] + c * p[i] for i in range(1, len(p))] + [p[-1]]

        return one(a[0]), one(a[1])

    def add(a, b, scale):
        def one(p, n):
            out = []
            for i in range(max(len(p), len(n))):
                terms = ([p[i]] if i < len(p) else []) + ([scale * n[i]] if i < len(n) else [])
                out.append(functools.reduce(lambda x, y: x + y, terms))
            return out

        return one(a[0], b[0]), one(a[1], b[1])

    unit = jnp.ones((1, 128), F32)
    residual, direction, answer = ([unit], []), ([], [unit]), ([], [])
    norm = rho[0]
    for k in range(3):
        image = operate(direction)
        alpha = norm / dot(direction, image)
        answer = add(answer, direction, alpha)
        residual = add(residual, image, -alpha)
        if k < 2:
            after = dot(residual, residual)
            direction = add(residual, direction, after / norm)
            norm = after

    def over_field(a, start, size):
        out = [start] + [None] * (size - 1)
        for values, (low_factor, high_factor) in zip(a, (e, f)):
            for k, x in enumerate(values):
                for n, term in ((k, x * low_factor), (k + 1, x * high_factor)):
                    out[n] = term if out[n] is None else out[n] + term
        return out

    for k, factor in enumerate(over_field(answer, alpha0, 4) + over_field(residual, None, 5)):
        factors[k] = jnp.broadcast_to(factor, (8, 128))

    for copy in sent + corners + more_corners + [tv_copy, tu_copy]:
        copy.wait_send()
    fan_wait(a1, PLANE - 1, ar_send.at[0, 0])
    fan_wait(b1, DEPTH - 1, ar_send.at[0, 1])
    fan_wait(a2, PLANE - 1, ar_send.at[1, 0])
    fan_wait(b2, DEPTH - 1, ar_send.at[1, 1])


def combine(field, factors, x_hbm, r_hbm, x_buf, r_buf, sem):
    c = [jnp.concatenate([factors[k]] * 4, axis=0) for k in range(9)]
    copies = []
    for half in range(2):
        for which, (buf, hbm) in enumerate(((x_buf, x_hbm), (r_buf, r_hbm))):
            for block in (2 * half, 2 * half + 1):
                values = []
                for i in range(4 * block, 4 * block + 4):
                    terms = [f * field[n, i] for n, f in enumerate(c[4:] if which else c[:4])]
                    values.append(functools.reduce(lambda s, t: s + t, terms))
                t = jnp.transpose(jnp.concatenate(exchange_groups(values), axis=0))
                for k in range(4):
                    at = pl.ds(4 * (block % 2) + k, MEMB, stride=8)
                    buf[half, at, :] = t[32 * k : 32 * k + 32]
            copy = pltpu.make_async_copy(
                buf.at[half].reshape(MEMB, 8, TX), hbm.at[:, pl.ds(8 * half, 8)], sem.at[half, which]
            )
            copy.start()
            copies.append(copy)
    for copy in copies:
        copy.wait()


def on_device(zonal, meridional, fraction, thickness, land, codes):
    vmem = pl.BlockSpec(memory_space=pltpu.VMEM)
    hbm = pl.BlockSpec(memory_space=pltpu.HBM)
    arguments = [
        pltpu.with_memory_space_constraint(x, pltpu.HBM)
        for x in (zonal, meridional, fraction, thickness, land, codes)
    ]
    whole = jax.ShapeDtypeStruct((MEMB, TY, TX), F32)
    padded = (TY + 2) * PITCH
    field, factors = pl.pallas_call(
        kernel,
        out_shape=(
            jax.ShapeDtypeStruct((5, TY, 32, 128), F32),
            jax.ShapeDtypeStruct((9, 8, 128), F32),
        ),
        in_specs=[hbm] * 6,
        out_specs=(vmem, vmem),
        scratch_shapes=[
            pltpu.VMEM((MEMB, LEV, TY, TX), jnp.bfloat16),
            pltpu.VMEM((MEMB, LEV, TY, TX), jnp.bfloat16),
            pltpu.VMEM((LEV, TY, TX), jnp.bfloat16),
            pltpu.SMEM((LEV,), F32),
            pltpu.VMEM((TY, TX), jnp.int32),
            pltpu.SMEM((1, 4), jnp.int32),
            pltpu.VMEM((MEMB * TY, TX), F32),
            pltpu.VMEM((MEMB * TY, TX), F32),
            pltpu.VMEM((LEV, TY, TX), F32),
            pltpu.VMEM((padded, 128), F32),
            pltpu.VMEM(((TY + 1) * 32, 128), F32),
            pltpu.VMEM((5, padded, 128), F32),
            pltpu.VMEM((TY, 32, 128), F32),
            pltpu.VMEM((TY * 32, 128), F32),
            pltpu.VMEM((TY, TX), F32),
            pltpu.VMEM((5, 4, 32, 128), F32),
            pltpu.VMEM((5, 2, TY, 128), F32),
            pltpu.VMEM((TY, 128), F32),
            pltpu.VMEM((TY, 128), F32),
            pltpu.VMEM((32, 128), F32),
            pltpu.VMEM((32, 128), F32),
            pltpu.VMEM((4, 2, 32, 128), F32),
            pltpu.VMEM((12, 1, 128), F32),
            pltpu.VMEM((12, 1, 128), F32),
            pltpu.VMEM((PLANE, 1, 128), F32),
            pltpu.VMEM((DEPTH, 1, 128), F32),
            pltpu.VMEM((PLANE, 4, 128), F32),
            pltpu.VMEM((DEPTH, 4, 128), F32),
            pltpu.SemaphoreType.DMA((2, CHUNKS)),
            pltpu.SemaphoreType.DMA((4,)),
            pltpu.SemaphoreType.DMA((8, 4)),
            pltpu.SemaphoreType.DMA((8, 4)),
            pltpu.SemaphoreType.DMA((2, 2)),
            pltpu.SemaphoreType.DMA((2, 2)),
        ],
        compiler_params=pltpu.CompilerParams(
            collective_id=0, has_side_effects=True, vmem_limit_bytes=40 << 20
        ),
    )(*arguments)
    return pl.pallas_call(
        combine,
        out_shape=(whole, whole),
        in_specs=[vmem] * 2,
        out_specs=(hbm, hbm),
        scratch_shapes=[
            pltpu.VMEM((2, MEMB * 8, TX), F32),
            pltpu.VMEM((2, MEMB * 8, TX), F32),
            pltpu.SemaphoreType.DMA((2, 2)),
        ],
        compiler_params=pltpu.CompilerParams(vmem_limit_bytes=16 << 20),
    )(field, factors)


def solution(mesh):
    in_specs = (
        P(None, None, "tile", None),
        P(None, None, "tile", None),
        P(None, "tile", None),
        P(),
        P("tile", None),
        P("tile", None),
    )
    out_specs = (P(None, "tile", None), P(None, "tile", None))
    return jax.shard_map(
        on_device, mesh=mesh, in_specs=in_specs, out_specs=out_specs, check_vma=False
    )
```

```python
import functools

import jax
import jax.numpy as jnp
from jax import lax
from jax.experimental import pallas as pl
from jax.experimental.pallas import tpu as pltpu
from jax.sharding import PartitionSpec as P

MESH = pl.DeviceIdType.MESH
F32 = jnp.float32
MEMB, LEV, TY, TX = 32, 8, 16, 128
NTX = 16
PLANE, DEPTH = 32, 8
N_TILE = PLANE * DEPTH
PITCH = 48
UNROLL = 4
CHUNKS = 4


def lanes(shape):
    return lax.broadcasted_iota(jnp.int32, shape, len(shape) - 1)


def roll_lanes(x, shift):
    return pltpu.roll(x, shift % 128, axis=x.ndim - 1)


def exchange_groups(a):
    lane = lanes(a[0].shape)
    low = lane < 64
    even = (lane // 32) % 2 == 0
    b0 = jnp.where(low, a[0], roll_lanes(a[2], 64))
    b2 = jnp.where(low, roll_lanes(a[0], 64), a[2])
    b1 = jnp.where(low, a[1], roll_lanes(a[3], 64))
    b3 = jnp.where(low, roll_lanes(a[1], 64), a[3])
    return (
        jnp.where(even, b0, roll_lanes(b1, 32)),
        jnp.where(even, roll_lanes(b0, 96), b1),
        jnp.where(even, b2, roll_lanes(b3, 32)),
        jnp.where(even, roll_lanes(b2, 96), b3),
    )


def reverse8(x):
    place = lax.broadcasted_iota(jnp.int32, x.shape, 0)
    x = pltpu.roll(x, 4, axis=0)
    x = jnp.where(place % 4 < 2, pltpu.roll(x, 6, axis=0), pltpu.roll(x, 2, axis=0))
    return jnp.where(place % 2 < 1, pltpu.roll(x, 7, axis=0), pltpu.roll(x, 1, axis=0))


def reverse_rows(x):
    blocks = x.shape[0] // 8
    return jnp.concatenate(
        [reverse8(x[8 * k : 8 * k + 8]) for k in range(blocks - 1, -1, -1)], axis=0
    )


def reverse_columns(x):
    even = (lanes(x.shape) // 32) % 2 == 0
    return reverse_rows(jnp.where(even, roll_lanes(x, 32), roll_lanes(x, 96)))


def pack_sums(p):
    return fold([x[0:8] + x[8:16] + (x[16:24] + x[24:32]) for x in p])


def fold(p):
    lane = lanes(p[0].shape)
    low = lane < 64
    even = (lane // 32) % 2 == 0
    x = jnp.where(low, p[0] + roll_lanes(p[0], 64), p[2] + roll_lanes(p[2], 64))
    y = jnp.where(low, p[1] + roll_lanes(p[1], 64), p[3] + roll_lanes(p[3], 64))
    z = jnp.where(even, x + roll_lanes(x, 96), y + roll_lanes(y, 32))
    return jnp.sum(z, axis=0, keepdims=True)


def spread(row):
    lane = lanes(row.shape)
    out = []
    for k in range(4):
        x = jnp.where(lane // 32 == k, row, 0.0)
        x = x + roll_lanes(x, 64)
        out.append(x + roll_lanes(x, 32))
    return out


def pick(row, group):
    row = jnp.where(lanes(row.shape) // 32 == group, row, 0.0)
    row = row + roll_lanes(row, 64)
    return row + roll_lanes(row, 32)


def kernel(
    u_hbm, v_hbm, fraction_hbm, thickness_hbm, land_hbm, codes_hbm, turned, factors,
    u_buf, v_buf, fraction, thickness, land, codes, tu1, tv1, weight, tu2, tv2, field, g_buf, q_buf, qsum, stage,
    edge_send, edge_recv, tu_send, tu_recv, tv_send, tv_recv, row_recv,
    corner_send, corner_recv, a1, b1, a2, b2,
    load_sem, small_sem, send_sem, recv_sem, ar_send, ar_recv,
):
    me = lax.axis_index("tile")
    east, west = lax.rem(me + 1, N_TILE), lax.rem(me + N_TILE - 1, N_TILE)
    north, south = lax.rem(me + NTX, N_TILE), lax.rem(me + N_TILE - NTX, N_TILE)
    diagonal = {n: lax.rem(me + N_TILE + n, N_TILE) for n in (-17, -15, 15, 17)}
    level, place = me // PLANE, lax.rem(me, PLANE)
    ys = [level * PLANE + 8 * lax.rem(place // 8 + d, 4) for d in range(4)]
    xs = [2 * lax.rem(place // 2 + d, 4) for d in range(4)]
    cores = [lax.rem(place + d, 2) for d in range(2)]
    offsets = sorted(
        ((y, x, c) for y in range(4) for x in range(4) for c in range(2) if (y, x, c) != (0, 0, 0)),
        key=lambda o: -(min(o[0], 4 - o[0]) + min(o[1], 4 - o[1])),
    )
    plane_peers = [ys[y] + xs[x] + cores[c] for y, x, c in offsets]
    level_peers = [lax.rem(level + d, DEPTH) * PLANE + place for d in (4, 3, 5, 2, 6, 1, 7)]

    small_loads = []
    pairs = ((thickness_hbm, thickness), (codes_hbm, codes), (fraction_hbm, fraction), (land_hbm, land))
    for n, (src, dst) in enumerate(pairs):
        copy = pltpu.make_async_copy(src, dst, small_sem.at[n])
        copy.start()
        small_loads.append(copy)
    part = MEMB // CHUNKS
    loads = []
    for c in range(CHUNKS):
        for n, (src, dst) in enumerate(((u_hbm, u_buf), (v_hbm, v_buf))):
            at = pl.ds(c * part, part)
            copy = pltpu.make_async_copy(src.at[at], dst.at[at], load_sem.at[n, c])
            copy.start()
            loads.append(copy)

    barrier = pltpu.get_barrier_semaphore()
    greeted = [east, west, north, south] + list(diagonal.values()) + plane_peers + level_peers
    for peer in greeted:
        pl.semaphore_signal(barrier, inc=1, device_id=(peer,), device_id_type=MESH)

    for copy in small_loads:
        copy.wait()
    flip = [codes[0, k] == 1 for k in range(4)]

    total = thickness[0]
    for k in range(1, LEV):
        total = total + thickness[k]
    shift = 1.0 + 0.125 * total

    depth = None
    for k in range(LEV):
        w = thickness[k] * fraction[k].astype(F32)
        weight[k] = w
        depth = w if depth is None else depth + w
    root = 0.5 * jnp.sqrt(land[...].astype(F32) * depth)
    stage[...] = root

    def to_groups(rows_of, store):
        for block in range(4):
            z = jnp.concatenate([rows_of(4 * block + k) for k in range(4)], axis=0)
            t = jnp.transpose(z)
            out = exchange_groups([t[32 * g : 32 * g + 32] for g in range(4)])
            for k in range(4):
                store(4 * block + k, out[k])

    def inner(i):
        start = (i + 1) * PITCH + 8
        if not isinstance(i, int):
            start = pl.multiple_of(start, 8)
        return pl.ds(start, 32)

    def column(s):
        return pl.ds(PITCH + 8 + s, TY, stride=PITCH)

    def store_q(i, value):
        q_buf[i] = value
        g_buf[0, inner(i), :] = value

    to_groups(lambda i: jnp.broadcast_to(stage[pl.ds(i, 1), :], (MEMB, TX)), store_q)

    def column_sums(src, dst, n):
        for c in range(CHUNKS):
            loads[2 * c + n].wait()

            def member(m, carry):
                total = weight[0] * src[m, 0].astype(F32)
                for k in range(1, LEV):
                    total = total + weight[k] * src[m, k].astype(F32)
                dst[pl.ds(pl.multiple_of(m * TY, TY), TY), :] = total
                return carry

            lax.fori_loop(c * part, (c + 1) * part, member, 0, unroll=2)

    def remote(src, dst, index, direction, peer):
        return pltpu.make_async_remote_copy(
            src_ref=src, dst_ref=dst,
            send_sem=send_sem.at[index, direction], recv_sem=recv_sem.at[index, direction],
            device_id=(peer,), device_id_type=MESH,
        )

    def edges(k):
        if k == 0:
            from_north, from_south = g_buf.at[0, pl.ds(17 * PITCH + 8, 32)], g_buf.at[0, pl.ds(8, 32)]
        else:
            from_north, from_south = row_recv.at[k - 1, 0], row_recv.at[k - 1, 1]
        return [
            remote(edge_send.at[k, 2], from_north, k, 2, south),
            remote(edge_send.at[k, 3], from_south, k, 3, north),
            remote(edge_send.at[k, 0, pl.ds(0, TY)], edge_recv.at[k, 0], k, 0, west),
            remote(edge_send.at[k, 1, pl.ds(0, TY)], edge_recv.at[k, 1], k, 1, east),
        ]

    def put_rows(k, low=None, high=None):
        if low is None:
            low, high = g_buf[k, inner(0), :], g_buf[k, inner(TY - 1), :]
        edge_send[k, 2] = jnp.where(flip[3], reverse_columns(low), low)
        edge_send[k, 3] = jnp.where(flip[2], reverse_columns(high), high)

    def put_columns(k, first=None, last=None):
        if first is None:
            first, last = g_buf[k, column(0), :], g_buf[k, column(31), :]
        to_west = roll_lanes(first, 96)
        to_east = roll_lanes(last, 32)
        edge_send[k, 0, pl.ds(0, TY)] = jnp.where(flip[1], reverse_rows(to_west), to_west)
        edge_send[k, 1, pl.ds(0, TY)] = jnp.where(flip[0], reverse_rows(to_east), to_east)
        return to_west, to_east

    def take_columns(k, to_west, to_east):
        lane = lanes(to_west.shape)
        g_buf[k, column(32), :] = jnp.where(lane < 96, to_west, edge_recv[k, 0])
        g_buf[k, column(-1), :] = jnp.where(lane >= 32, to_east, edge_recv[k, 1])

    sent = []
    blank = jnp.zeros((32, 128), F32)
    for k in range(2, 5):
        if k != 3:
            g_buf[k, pl.ds(8, 32), :] = blank
            g_buf[k, pl.ds(17 * PITCH + 8, 32), :] = blank

    def send_rows(k, *values, put=True):
        if put:
            put_rows(k, *values)
        copies = edges(k)
        copies[0].start()
        copies[1].start()
        sent.extend(copies)
        return copies

    def send_columns(k, copies, *values, put=True):
        own = put_columns(k, *values) if put else None
        copies[2].start()
        copies[3].start()
        return own

    def around(k, i):
        here = inner(i)
        base = here.start
        return (g_buf[k, pl.ds(base + 1, 32), :] + g_buf[k, pl.ds(base - 1, 32), :]) + (
            g_buf[k, inner(i + 1), :] + g_buf[k, inner(i - 1), :]
        )

    put_rows(0)
    own = put_columns(0)
    column_sums(u_buf, tu1, 0)
    column_sums(v_buf, tv1, 1)

    def store_tu(i, value):
        tu2[inner(i), :] = value

    def store_tv(i, value):
        tv2[pl.ds(i * 32, 32), :] = value

    to_groups(lambda i: tv1[pl.ds(i, MEMB, stride=TY), :], store_tv)
    to_groups(lambda i: tu1[pl.ds(i, MEMB, stride=TY), :], store_tu)

    tv_row = tv2[pl.ds(0, 32), :]
    tv_send[...] = jnp.where(flip[3], reverse_columns(tv_row), tv_row)
    tu_column = tu2[column(0), :]
    own_tu = roll_lanes(tu_column, 96)
    tu_send[...] = jnp.where(flip[1], reverse_rows(own_tu), own_tu)
    last_lanes = lanes(own_tu.shape) >= 96
    tu2[column(32), :] = jnp.where(last_lanes, 0.0, own_tu)
    tv2[pl.ds(TY * 32, 32), :] = jnp.zeros((32, 128), F32)

    def part_row(i):
        here, below = inner(i), i * 32
        return (
            tu2[here, :] - tu2[pl.ds(here.start + 1, 32), :]
            + tv2[pl.ds(below, 32), :] - tv2[pl.ds(below + 32, 32), :]
        )

    def part_column(n):
        return (
            tu2[column(n), :] - tu2[column(n + 1), :]
            + tv2[pl.ds(n, TY, stride=32), :] - tv2[pl.ds(n + 32, TY, stride=32), :]
        )

    low, high = tu2[pl.ds(PITCH + 8, 1), :], tu2[pl.ds(TY * PITCH + 8, 1), :]
    left, right = pick(tv2[pl.ds(0, 1), :], 0), pick(tv2[pl.ds(31, 1), :], 3)
    corner_send[0] = pick(jnp.where(flip[1], high, low), 0)
    corner_send[1] = jnp.where(flip[3], right, left)
    corner_send[2] = pick(jnp.where(flip[1], low, high), 0)
    corner_send[3] = jnp.where(flip[3], left, right)

    def corner(start, size, index, direction, peer):
        at = pl.ds(start, size)
        return remote(corner_send.at[at], corner_recv.at[at], index, direction, peer)

    put_rows(1, part_row(0), part_row(TY - 1))
    put_columns(1, part_column(0), part_column(31))
    pl.semaphore_wait(barrier, len(greeted))
    corners = [
        corner(0, 2, 6, 0, diagonal[-17]), corner(2, 1, 6, 1, diagonal[15]), corner(3, 1, 6, 2, diagonal[-15]),
    ]
    for copy in corners:
        copy.start()
    tv_copy = remote(tv_send, tv_recv, 5, 2, south)
    tv_copy.start()
    tu_copy = remote(tu_send, tu_recv, 5, 0, west)
    tu_copy.start()
    parts = send_rows(1, put=False)
    send_columns(1, parts, put=False)
    copies = send_rows(0, put=False)
    send_columns(0, copies, put=False)
    tu_copy.wait_recv()
    tu2[column(32), :] = jnp.where(last_lanes, tu_recv[...], own_tu)
    copies[2].wait_recv()
    copies[3].wait_recv()
    take_columns(0, *own)

    zero = jnp.zeros((32, 128), F32)

    def first(i, total):
        q = q_buf[i]
        here = inner(i)
        below = i * 32 if isinstance(i, int) else pl.multiple_of(i * 32, 32)
        value = (
            tu2[here, :] - tu2[pl.ds(here.start + 1, 32), :]
            + tv2[pl.ds(below, 32), :] - tv2[pl.ds(below + 32, 32), :]
        )
        value = jnp.where(q > 0.0, value, 0.0)
        qsum[pl.ds(below, 32), :] = q * around(0, i) + (1.0 - shift)
        field[0, i] = value
        g_buf[1, here, :] = q * value
        return total + value * value

    def middle(body, start):
        return lax.fori_loop(1, TY - 1, body, start, unroll=UNROLL)

    n0 = middle(first, zero)
    tv_copy.wait_recv()
    tv2[pl.ds(TY * 32, 32), :] = tv_recv[...]
    copies[0].wait_recv()
    copies[1].wait_recv()
    n0 = first(TY - 1, first(0, n0))
    for copy in parts + corners:
        copy.wait_recv()
    row_shape = (32, 128)
    position = lanes(row_shape) // 32 * 32 + lax.broadcasted_iota(jnp.int32, row_shape, 0)

    def at_end(shape_position, flipped, last, value):
        return jnp.where(shape_position == jnp.where(flipped, 0, last), value, 0.0)

    north_ghost, south_ghost = pl.ds(17 * PITCH + 8, 32), pl.ds(8, 32)
    g_buf[1, north_ghost, :] = g_buf[0, north_ghost, :] * (
        row_recv[0, 0] - at_end(position, flip[2], TX - 1, corner_recv[0])
    )
    g_buf[1, south_ghost, :] = g_buf[0, south_ghost, :] * (
        row_recv[0, 1] - tv_row - at_end(position, flip[3], TX - 1, corner_recv[2])
    )
    index = lax.broadcasted_iota(jnp.int32, (TY, 128), 0)
    lane = lanes((TY, 128))
    from_east = edge_recv[1, 0] - at_end(index, flip[0], TY - 1, corner_recv[1])
    from_west = edge_recv[1, 1] - tu_column - at_end(index, flip[1], TY - 1, corner_recv[3])
    g_buf[1, column(32), :] = jnp.where(
        lane < 96, roll_lanes(g_buf[1, column(0), :], 96), g_buf[0, column(32), :] * from_east
    )
    g_buf[1, column(-1), :] = jnp.where(
        lane >= 32, roll_lanes(g_buf[1, column(31), :], 32), g_buf[0, column(-1), :] * from_west
    )

    def level_of(i):
        return pl.ds(i * 32 if isinstance(i, int) else pl.multiple_of(i * 32, 32), 32)

    def step_of(k):
        def step(i, totals):
            q, old = q_buf[i], field[k - 1, i]
            value = qsum[level_of(i), :] * old - q * around(k, i)
            field[k, i] = value
            if k < 4:
                g_buf[k + 1, inner(i), :] = q * value
            return (totals[0] + old * value, totals[1] + value * value) if k == 1 else totals

        return step

    def flat(k):
        return field.at[k].reshape(TY * 32, 128)

    def field_column(k, n):
        return flat(k)[pl.ds(n, TY, stride=32), :]

    def inside_columns(k):
        first_column, last_column = g_buf[k, column(0), :], g_buf[k, column(31), :]
        g_buf[k, column(32), :] = jnp.where(lane < 96, roll_lanes(first_column, 96), 0.0)
        g_buf[k, column(-1), :] = jnp.where(lane >= 32, roll_lanes(last_column, 32), 0.0)
        return first_column, last_column

    def add_ghosts(k, rows, columns):
        north_row = field[k, TY - 1] - q_buf[TY - 1] * rows[0]
        south_row = field[k, 0] - q_buf[0] * rows[1]
        field[k, TY - 1] = north_row
        field[k, 0] = south_row
        east_column = field_column(k, 31) - jnp.where(lane >= 96, g_buf[0, column(31), :] * columns[0], 0.0)
        west_column = field_column(k, 0) - jnp.where(lane < 32, g_buf[0, column(0), :] * columns[1], 0.0)
        flat(k)[pl.ds(31, TY, stride=32), :] = east_column
        flat(k)[pl.ds(0, TY, stride=32), :] = west_column
        if k < 4:
            g_buf[k + 1, inner(0), :] = q_buf[0] * south_row
            g_buf[k + 1, inner(TY - 1), :] = q_buf[TY - 1] * north_row
            g_buf[k + 1, column(31), :] = g_buf[0, column(31), :] * east_column
            g_buf[k + 1, column(0), :] = g_buf[0, column(0), :] * west_column

    def fan(buf, slot, peers, phase, which):
        def copy_to(peer):
            return pltpu.make_async_remote_copy(
                src_ref=buf.at[slot], dst_ref=buf.at[slot],
                send_sem=ar_send.at[which, phase], recv_sem=ar_recv.at[which, phase],
                device_id=(peer,), device_id_type=MESH,
            )

        for peer in peers:
            copy_to(peer).start()

    def fan_wait(buf, count, sem):
        pltpu.make_async_copy(buf.at[pl.ds(0, count)], buf.at[pl.ds(0, count)], sem).wait()

    def start_level(values, buf, which):
        buf[place] = values
        fan(buf, place, plane_peers, 0, which)

    def cross_levels(buf_a, buf_b, which):
        fan_wait(buf_a, PLANE - 1, ar_recv.at[which, 0])
        buf_b[level] = jnp.sum(buf_a[...], axis=0)
        fan(buf_b, level, level_peers, 1, which)

    def finish(buf_b, which):
        fan_wait(buf_b, DEPTH - 1, ar_recv.at[which, 1])
        return jnp.sum(buf_b[...], axis=0)

    step = step_of(1)
    totals = step(TY - 1, step(0, (zero, zero)))
    flight = send_rows(2)
    n1, n2 = middle(step, totals)
    first_column, last_column = inside_columns(2)
    send_columns(2, flight, first_column, last_column)
    start, end = pl.ds(PITCH + 8, 1), pl.ds(TY * PITCH + 8, 1)
    start_last, end_last = pl.ds(PITCH + 39, 1), pl.ds(TY * PITCH + 39, 1)
    p00, p10 = pick(g_buf[2, start, :], 0), pick(g_buf[2, end, :], 0)
    p01, p11 = pick(g_buf[2, start_last, :], 3), pick(g_buf[2, end_last, :], 3)
    corner_send[4] = jnp.where(flip[1], p10, p00)
    corner_send[5] = jnp.where(flip[3], p01, p00)
    corner_send[6] = jnp.where(flip[0], p11, p01)
    corner_send[7] = jnp.where(flip[3], p00, p01)
    corner_send[8] = jnp.where(flip[1], p00, p10)
    corner_send[9] = jnp.where(flip[2], p11, p10)
    corner_send[10] = jnp.where(flip[0], p01, p11)
    corner_send[11] = jnp.where(flip[2], p10, p11)
    more_corners = [
        corner(4 + 2 * n, 2, 7, n, diagonal[d]) for n, d in enumerate((-17, -15, 15, 17))
    ]
    for copy in more_corners:
        copy.start()
    step = step_of(2)
    step(TY - 1, step(0, ()))
    seconds = send_rows(3, field[2, 0], field[2, TY - 1])
    middle(step, ())
    send_columns(3, seconds, field_column(2, 0), field_column(2, 31))
    start_level(pack_sums([n0, n1, n2, zero]), a1, 0)

    own_rows = g_buf[2, inner(TY - 1), :], g_buf[2, inner(0), :]
    for copy in flight:
        copy.wait_recv()
    add_ghosts(2, (row_recv[1, 0], row_recv[1, 1]), (edge_recv[2, 0], edge_recv[2, 1]))
    for copy in seconds + more_corners:
        copy.wait_recv()

    def ends(shape_position, flipped, last, at_last, at_first):
        return at_end(shape_position, flipped, last, corner_recv[at_last]) + jnp.where(
            shape_position == jnp.where(flipped, last, 0), corner_recv[at_first], 0.0
        )

    for side, ghost, flipped, corner_slots in (
        (0, north_ghost, flip[2], (4, 6)),
        (1, south_ghost, flip[3], (8, 10)),
    ):
        q = g_buf[0, ghost, :]
        missing = own_rows[side] + ends(position, flipped, TX - 1, *corner_slots)
        g_buf[3, ghost, :] = q * (row_recv[2, side] - q * missing)
    q = g_buf[0, column(32), :]
    missing = last_column + ends(index, flip[0], TY - 1, 5, 9)
    g_buf[3, column(32), :] = jnp.where(
        lane < 96, roll_lanes(g_buf[3, column(0), :], 96), q * (edge_recv[3, 0] - q * missing)
    )
    q = g_buf[0, column(-1), :]
    missing = first_column + ends(index, flip[1], TY - 1, 7, 11)
    g_buf[3, column(-1), :] = jnp.where(
        lane >= 32, roll_lanes(g_buf[3, column(31), :], 32), q * (edge_recv[3, 1] - q * missing)
    )

    step = step_of(3)
    step(TY - 1, step(0, ()))
    flight = send_rows(4)
    middle(step, ())
    send_columns(4, flight, *inside_columns(4))
    cross_levels(a1, b1, 0)
    step = step_of(4)
    middle(step, step(TY - 1, step(0, ())))
    for copy in flight:
        copy.wait_recv()
    add_ghosts(4, (row_recv[3, 0], row_recv[3, 1]), (edge_recv[4, 0], edge_recv[4, 1]))
    s0, s1, s2, _ = spread(finish(b1, 0))

    c = shift
    m1 = c * s0 + s1
    m2 = c * (c * s0 + 2.0 * s1) + s2
    alpha0 = s0 / m1
    rr1 = s0 - alpha0 * (2.0 * m1 - alpha0 * m2)
    beta0 = rr1 / s0
    e = (1.0 - alpha0 * c, -alpha0)
    f = (e[0] + beta0, -alpha0)
    wide_e = [jnp.broadcast_to(x, (32, 128)) for x in e]
    wide_f = [jnp.broadcast_to(x, (32, 128)) for x in f]

    def second(i, totals):
        v = [field[k, i] for k in range(5)]
        r = [wide_e[0] * v[k] + wide_e[1] * v[k + 1] for k in range(3)]
        d = [wide_f[0] * v[k] + wide_f[1] * v[k + 1] for k in range(4)]
        pairs = (
            (r[0], r[0]), (r[0], r[1]), (r[1], r[1]), (r[1], r[2]),
            (r[0], d[0]), (r[0], d[1]), (r[1], d[1]), (r[1], d[2]), (r[2], d[2]),
            (d[0], d[0]), (d[0], d[1]), (d[1], d[1]), (d[1], d[2]), (d[2], d[2]), (d[2], d[3]),
        )
        out = []
        for t, (x, y) in zip(totals, pairs):
            p = x * y
            out.append(t + (p[0:8] + p[8:16] + (p[16:24] + p[24:32])))
        return tuple(out)

    small = jnp.zeros((8, 128), F32)
    totals = lax.fori_loop(0, TY, second, (small,) * 15, unroll=2) + (small,)
    start_level(jnp.concatenate([fold(totals[4 * k : 4 * k + 4]) for k in range(4)], axis=0), a2, 1)

    def turn(n, carry):
        k, block = n // 4, lax.rem(n, 4)
        values = [field[k, 4 * block + i] for i in range(4)]
        t = jnp.transpose(jnp.concatenate(exchange_groups(values), axis=0))
        for i in range(4):
            turned[k, 4 * block + i] = t[32 * i : 32 * i + 32]
        return carry

    lax.fori_loop(0, 20, turn, 0, unroll=2)
    cross_levels(a2, b2, 1)
    sums = finish(b2, 1)
    sums = [x for k in range(4) for x in spread(sums[k : k + 1])]
    rho, sigma, delta = sums[:4], sums[4:9], sums[9:15]

    def dot(a, b):
        terms = []
        for one, other, table in ((a[0], b[0], rho), (a[0], b[1], sigma), (a[1], b[0], sigma), (a[1], b[1], delta)):
            for i, x in enumerate(one):
                inner_sum = functools.reduce(lambda p, n: p + n, [y * table[i + j] for j, y in enumerate(other)], 0.0)
                terms.append(x * inner_sum)
        return functools.reduce(lambda p, n: p + n, terms)

    def operate(a):
        def one(p):
            if not p:
                return []
            return [c * p[0]] + [p[i - 1] + c * p[i] for i in range(1, len(p))] + [p[-1]]

        return one(a[0]), one(a[1])

    def add(a, b, scale):
        def one(p, n):
            out = []
            for i in range(max(len(p), len(n))):
                terms = ([p[i]] if i < len(p) else []) + ([scale * n[i]] if i < len(n) else [])
                out.append(functools.reduce(lambda x, y: x + y, terms))
            return out

        return one(a[0], b[0]), one(a[1], b[1])

    unit = jnp.ones((1, 128), F32)
    residual, direction, answer = ([unit], []), ([], [unit]), ([], [])
    norm = rho[0]
    for k in range(3):
        image = operate(direction)
        alpha = norm / dot(direction, image)
        answer = add(answer, direction, alpha)
        residual = add(residual, image, -alpha)
        if k < 2:
            after = dot(residual, residual)
            direction = add(residual, direction, after / norm)
            norm = after

    def over_field(a, start, size):
        out = [start] + [None] * (size - 1)
        for values, (low_factor, high_factor) in zip(a, (e, f)):
            for k, x in enumerate(values):
                for n, term in ((k, x * low_factor), (k + 1, x * high_factor)):
                    out[n] = term if out[n] is None else out[n] + term
        return out

    rows = over_field(answer, alpha0, 4) + over_field(residual, None, 5)
    columns = jnp.transpose(jnp.concatenate(rows + [jnp.zeros((119, 128), F32)], axis=0))
    for k in range(9):
        factors[k] = jnp.broadcast_to(columns[0:MEMB, k : k + 1], (MEMB, TX))

    for copy in sent + corners + more_corners + [tv_copy, tu_copy]:
        copy.wait_send()
    fan_wait(a1, PLANE - 1, ar_send.at[0, 0])
    fan_wait(b1, DEPTH - 1, ar_send.at[0, 1])
    fan_wait(a2, PLANE - 1, ar_send.at[1, 0])
    fan_wait(b2, DEPTH - 1, ar_send.at[1, 1])


def combine(turned, factors, x_hbm, r_hbm, x_buf, r_buf, sem):
    copies = []
    for half in range(2):
        for which, (buf, hbm) in enumerate(((x_buf, x_hbm), (r_buf, r_hbm))):
            c = [factors[k] for k in range(9)][4 * which : 4 + 5 * which]
            for i in range(8):
                terms = [f * turned[k, 8 * half + i] for k, f in enumerate(c)]
                buf[half, pl.ds(i, MEMB, stride=8), :] = functools.reduce(lambda s, t: s + t, terms)
            copy = pltpu.make_async_copy(
                buf.at[half].reshape(MEMB, 8, TX), hbm.at[:, pl.ds(8 * half, 8)], sem.at[half, which]
            )
            copy.start()
            copies.append(copy)
    for copy in copies:
        copy.wait()


def on_device(zonal, meridional, fraction, thickness, land, codes):
    vmem = pl.BlockSpec(memory_space=pltpu.VMEM)
    hbm = pl.BlockSpec(memory_space=pltpu.HBM)
    arguments = [
        pltpu.with_memory_space_constraint(x, pltpu.HBM)
        for x in (zonal, meridional, fraction, thickness, land, codes)
    ]
    whole = jax.ShapeDtypeStruct((MEMB, TY, TX), F32)
    padded = (TY + 2) * PITCH
    turned, factors = pl.pallas_call(
        kernel,
        out_shape=(
            jax.ShapeDtypeStruct((5, TY, 32, 128), F32),
            jax.ShapeDtypeStruct((9, MEMB, TX), F32),
        ),
        in_specs=[hbm] * 6,
        out_specs=(vmem, vmem),
        scratch_shapes=[
            pltpu.VMEM((MEMB, LEV, TY, TX), jnp.bfloat16),
            pltpu.VMEM((MEMB, LEV, TY, TX), jnp.bfloat16),
            pltpu.VMEM((LEV, TY, TX), jnp.bfloat16),
            pltpu.SMEM((LEV,), F32),
            pltpu.VMEM((TY, TX), jnp.int32),
            pltpu.SMEM((1, 4), jnp.int32),
            pltpu.VMEM((MEMB * TY, TX), F32),
            pltpu.VMEM((MEMB * TY, TX), F32),
            pltpu.VMEM((LEV, TY, TX), F32),
            pltpu.VMEM((padded, 128), F32),
            pltpu.VMEM(((TY + 1) * 32, 128), F32),
            pltpu.VMEM((5, TY, 32, 128), F32),
            pltpu.VMEM((5, padded, 128), F32),
            pltpu.VMEM((TY, 32, 128), F32),
            pltpu.VMEM((TY * 32, 128), F32),
            pltpu.VMEM((TY, TX), F32),
            pltpu.VMEM((5, 4, 32, 128), F32),
            pltpu.VMEM((5, 2, TY, 128), F32),
            pltpu.VMEM((TY, 128), F32),
            pltpu.VMEM((TY, 128), F32),
            pltpu.VMEM((32, 128), F32),
            pltpu.VMEM((32, 128), F32),
            pltpu.VMEM((4, 2, 32, 128), F32),
            pltpu.VMEM((12, 1, 128), F32),
            pltpu.VMEM((12, 1, 128), F32),
            pltpu.VMEM((PLANE, 1, 128), F32),
            pltpu.VMEM((DEPTH, 1, 128), F32),
            pltpu.VMEM((PLANE, 4, 128), F32),
            pltpu.VMEM((DEPTH, 4, 128), F32),
            pltpu.SemaphoreType.DMA((2, CHUNKS)),
            pltpu.SemaphoreType.DMA((4,)),
            pltpu.SemaphoreType.DMA((8, 4)),
            pltpu.SemaphoreType.DMA((8, 4)),
            pltpu.SemaphoreType.DMA((2, 2)),
            pltpu.SemaphoreType.DMA((2, 2)),
        ],
        compiler_params=pltpu.CompilerParams(
            collective_id=0, has_side_effects=True, vmem_limit_bytes=40 << 20
        ),
    )(*arguments)
    return pl.pallas_call(
        combine,
        out_shape=(whole, whole),
        in_specs=[vmem] * 2,
        out_specs=(hbm, hbm),
        scratch_shapes=[
            pltpu.VMEM((2, MEMB * 8, TX), F32),
            pltpu.VMEM((2, MEMB * 8, TX), F32),
            pltpu.SemaphoreType.DMA((2, 2)),
        ],
        compiler_params=pltpu.CompilerParams(vmem_limit_bytes=16 << 20),
    )(turned, factors)


def solution(mesh):
    in_specs = (
        P(None, None, "tile", None),
        P(None, None, "tile", None),
        P(None, "tile", None),
        P(),
        P("tile", None),
        P("tile", None),
    )
    out_specs = (P(None, "tile", None), P(None, "tile", None))
    return jax.shard_map(
        on_device, mesh=mesh, in_specs=in_specs, out_specs=out_specs, check_vma=False
    )
```

```python
import functools

import jax
import jax.numpy as jnp
from jax import lax
from jax.experimental import pallas as pl
from jax.experimental.pallas import tpu as pltpu
from jax.sharding import PartitionSpec as P

MESH = pl.DeviceIdType.MESH
F32 = jnp.float32
MEMB, LEV, TY, TX = 32, 8, 16, 128
NTX = 16
PLANE, DEPTH = 32, 8
N_TILE = PLANE * DEPTH
PITCH = 48
UNROLL = 4
CHUNKS = 4


def lanes(shape):
    return lax.broadcasted_iota(jnp.int32, shape, len(shape) - 1)


def roll_lanes(x, shift):
    return pltpu.roll(x, shift % 128, axis=x.ndim - 1)


def exchange_groups(a):
    lane = lanes(a[0].shape)
    low = lane < 64
    even = (lane // 32) % 2 == 0
    b0 = jnp.where(low, a[0], roll_lanes(a[2], 64))
    b2 = jnp.where(low, roll_lanes(a[0], 64), a[2])
    b1 = jnp.where(low, a[1], roll_lanes(a[3], 64))
    b3 = jnp.where(low, roll_lanes(a[1], 64), a[3])
    return (
        jnp.where(even, b0, roll_lanes(b1, 32)),
        jnp.where(even, roll_lanes(b0, 96), b1),
        jnp.where(even, b2, roll_lanes(b3, 32)),
        jnp.where(even, roll_lanes(b2, 96), b3),
    )


def reverse8(x):
    place = lax.broadcasted_iota(jnp.int32, x.shape, 0)
    x = pltpu.roll(x, 4, axis=0)
    x = jnp.where(place % 4 < 2, pltpu.roll(x, 6, axis=0), pltpu.roll(x, 2, axis=0))
    return jnp.where(place % 2 < 1, pltpu.roll(x, 7, axis=0), pltpu.roll(x, 1, axis=0))


def reverse_rows(x):
    blocks = x.shape[0] // 8
    return jnp.concatenate(
        [reverse8(x[8 * k : 8 * k + 8]) for k in range(blocks - 1, -1, -1)], axis=0
    )


def reverse_columns(x):
    even = (lanes(x.shape) // 32) % 2 == 0
    return reverse_rows(jnp.where(even, roll_lanes(x, 32), roll_lanes(x, 96)))


def pack_sums(p):
    return fold([x[0:8] + x[8:16] + (x[16:24] + x[24:32]) for x in p])


def fold(p):
    lane = lanes(p[0].shape)
    low = lane < 64
    even = (lane // 32) % 2 == 0
    x = jnp.where(low, p[0] + roll_lanes(p[0], 64), p[2] + roll_lanes(p[2], 64))
    y = jnp.where(low, p[1] + roll_lanes(p[1], 64), p[3] + roll_lanes(p[3], 64))
    z = jnp.where(even, x + roll_lanes(x, 96), y + roll_lanes(y, 32))
    return jnp.sum(z, axis=0, keepdims=True)


def spread(row):
    lane = lanes(row.shape)
    out = []
    for k in range(4):
        x = jnp.where(lane // 32 == k, row, 0.0)
        x = x + roll_lanes(x, 64)
        out.append(x + roll_lanes(x, 32))
    return out


def pick(row, group):
    row = jnp.where(lanes(row.shape) // 32 == group, row, 0.0)
    row = row + roll_lanes(row, 64)
    return row + roll_lanes(row, 32)


def kernel(
    u_hbm, v_hbm, fraction_hbm, thickness_hbm, land_hbm, codes_hbm, turned, factors,
    u_buf, v_buf, fraction, thickness, land, codes, tu1, tv1, weight, tu2, tv2, field, g_buf, q_buf, qsum, stage,
    edge_send, edge_recv, tu_send, tu_recv, tv_send, tv_recv, row_recv,
    corner_send, corner_recv, a1, b1, a2, b2,
    load_sem, small_sem, send_sem, recv_sem, ar_send, ar_recv,
):
    me = lax.axis_index("tile")
    east, west = lax.rem(me + 1, N_TILE), lax.rem(me + N_TILE - 1, N_TILE)
    north, south = lax.rem(me + NTX, N_TILE), lax.rem(me + N_TILE - NTX, N_TILE)
    diagonal = {n: lax.rem(me + N_TILE + n, N_TILE) for n in (-17, -15, 15, 17)}
    level, place = me // PLANE, lax.rem(me, PLANE)
    ys = [level * PLANE + 8 * lax.rem(place // 8 + d, 4) for d in range(4)]
    xs = [2 * lax.rem(place // 2 + d, 4) for d in range(4)]
    cores = [lax.rem(place + d, 2) for d in range(2)]
    offsets = sorted(
        ((y, x, c) for y in range(4) for x in range(4) for c in range(2) if (y, x, c) != (0, 0, 0)),
        key=lambda o: -(min(o[0], 4 - o[0]) + min(o[1], 4 - o[1])),
    )
    plane_peers = [ys[y] + xs[x] + cores[c] for y, x, c in offsets]
    level_peers = [lax.rem(level + d, DEPTH) * PLANE + place for d in (4, 3, 5, 2, 6, 1, 7)]

    small_loads = []
    pairs = ((thickness_hbm, thickness), (codes_hbm, codes), (fraction_hbm, fraction), (land_hbm, land))
    for n, (src, dst) in enumerate(pairs):
        copy = pltpu.make_async_copy(src, dst, small_sem.at[n])
        copy.start()
        small_loads.append(copy)
    part = MEMB // CHUNKS
    loads = []
    for c in range(CHUNKS):
        for n, (src, dst) in enumerate(((u_hbm, u_buf), (v_hbm, v_buf))):
            at = pl.ds(c * part, part)
            copy = pltpu.make_async_copy(src.at[at], dst.at[at], load_sem.at[n, c])
            copy.start()
            loads.append(copy)

    barrier = pltpu.get_barrier_semaphore()
    greeted = [east, west, north, south] + list(diagonal.values()) + plane_peers + level_peers
    for peer in greeted:
        pl.semaphore_signal(barrier, inc=1, device_id=(peer,), device_id_type=MESH)

    for copy in small_loads:
        copy.wait()
    flip = [codes[0, k] == 1 for k in range(4)]

    total = thickness[0]
    for k in range(1, LEV):
        total = total + thickness[k]
    shift = 1.0 + 0.125 * total

    depth = None
    for k in range(LEV):
        w = thickness[k] * fraction[k].astype(F32)
        weight[k] = w
        depth = w if depth is None else depth + w
    root = 0.5 * jnp.sqrt(land[...].astype(F32) * depth)
    stage[...] = root

    def to_groups(rows_of, store):
        for block in range(4):
            z = jnp.concatenate([rows_of(4 * block + k) for k in range(4)], axis=0)
            t = jnp.transpose(z)
            out = exchange_groups([t[32 * g : 32 * g + 32] for g in range(4)])
            for k in range(4):
                store(4 * block + k, out[k])

    def inner(i):
        start = (i + 1) * PITCH + 8
        if not isinstance(i, int):
            start = pl.multiple_of(start, 8)
        return pl.ds(start, 32)

    def column(s):
        return pl.ds(PITCH + 8 + s, TY, stride=PITCH)

    def store_q(i, value):
        q_buf[i] = value
        g_buf[0, inner(i), :] = value

    to_groups(lambda i: jnp.broadcast_to(stage[pl.ds(i, 1), :], (MEMB, TX)), store_q)

    def column_sums(src, dst, n, c):
        loads[2 * c + n].wait()

        def member(m, carry):
            total = weight[0] * src[m, 0].astype(F32)
            for k in range(1, LEV):
                total = total + weight[k] * src[m, k].astype(F32)
            dst[pl.ds(pl.multiple_of(m * TY, TY), TY), :] = total
            return carry

        lax.fori_loop(c * part, (c + 1) * part, member, 0, unroll=2)

    def remote(src, dst, index, direction, peer):
        return pltpu.make_async_remote_copy(
            src_ref=src, dst_ref=dst,
            send_sem=send_sem.at[index, direction], recv_sem=recv_sem.at[index, direction],
            device_id=(peer,), device_id_type=MESH,
        )

    def edges(k):
        if k == 0:
            from_north, from_south = g_buf.at[0, pl.ds(17 * PITCH + 8, 32)], g_buf.at[0, pl.ds(8, 32)]
        else:
            from_north, from_south = row_recv.at[k - 1, 0], row_recv.at[k - 1, 1]
        return [
            remote(edge_send.at[k, 2], from_north, k, 2, south),
            remote(edge_send.at[k, 3], from_south, k, 3, north),
            remote(edge_send.at[k, 0, pl.ds(0, TY)], edge_recv.at[k, 0], k, 0, west),
            remote(edge_send.at[k, 1, pl.ds(0, TY)], edge_recv.at[k, 1], k, 1, east),
        ]

    def put_rows(k, low=None, high=None):
        if low is None:
            low, high = g_buf[k, inner(0), :], g_buf[k, inner(TY - 1), :]
        edge_send[k, 2] = jnp.where(flip[3], reverse_columns(low), low)
        edge_send[k, 3] = jnp.where(flip[2], reverse_columns(high), high)

    def put_columns(k, first=None, last=None):
        if first is None:
            first, last = g_buf[k, column(0), :], g_buf[k, column(31), :]
        to_west = roll_lanes(first, 96)
        to_east = roll_lanes(last, 32)
        edge_send[k, 0, pl.ds(0, TY)] = jnp.where(flip[1], reverse_rows(to_west), to_west)
        edge_send[k, 1, pl.ds(0, TY)] = jnp.where(flip[0], reverse_rows(to_east), to_east)
        return to_west, to_east

    def take_columns(k, to_west, to_east):
        lane = lanes(to_west.shape)
        g_buf[k, column(32), :] = jnp.where(lane < 96, to_west, edge_recv[k, 0])
        g_buf[k, column(-1), :] = jnp.where(lane >= 32, to_east, edge_recv[k, 1])

    sent = []
    blank = jnp.zeros((32, 128), F32)
    for k in range(2, 5):
        if k != 3:
            g_buf[k, pl.ds(8, 32), :] = blank
            g_buf[k, pl.ds(17 * PITCH + 8, 32), :] = blank

    def send_rows(k, *values, put=True):
        if put:
            put_rows(k, *values)
        copies = edges(k)
        copies[0].start()
        copies[1].start()
        sent.extend(copies)
        return copies

    def send_columns(k, copies, *values, put=True):
        own = put_columns(k, *values) if put else None
        copies[2].start()
        copies[3].start()
        return own

    def around(k, i):
        here = inner(i)
        base = here.start
        return (g_buf[k, pl.ds(base + 1, 32), :] + g_buf[k, pl.ds(base - 1, 32), :]) + (
            g_buf[k, inner(i + 1), :] + g_buf[k, inner(i - 1), :]
        )

    put_rows(0)
    own = put_columns(0)
    for c in range(CHUNKS):
        column_sums(u_buf, tu1, 0, c)
        column_sums(v_buf, tv1, 1, c)

    def store_tu(i, value):
        tu2[inner(i), :] = value

    def store_tv(i, value):
        tv2[pl.ds(i * 32, 32), :] = value

    to_groups(lambda i: tv1[pl.ds(i, MEMB, stride=TY), :], store_tv)
    to_groups(lambda i: tu1[pl.ds(i, MEMB, stride=TY), :], store_tu)

    tv_row = tv2[pl.ds(0, 32), :]
    tv_send[...] = jnp.where(flip[3], reverse_columns(tv_row), tv_row)
    tu_column = tu2[column(0), :]
    own_tu = roll_lanes(tu_column, 96)
    tu_send[...] = jnp.where(flip[1], reverse_rows(own_tu), own_tu)
    last_lanes = lanes(own_tu.shape) >= 96
    tu2[column(32), :] = jnp.where(last_lanes, 0.0, own_tu)
    tv2[pl.ds(TY * 32, 32), :] = jnp.zeros((32, 128), F32)

    def part_row(i):
        here, below = inner(i), i * 32
        return (
            tu2[here, :] - tu2[pl.ds(here.start + 1, 32), :]
            + tv2[pl.ds(below, 32), :] - tv2[pl.ds(below + 32, 32), :]
        )

    def part_column(n):
        return (
            tu2[column(n), :] - tu2[column(n + 1), :]
            + tv2[pl.ds(n, TY, stride=32), :] - tv2[pl.ds(n + 32, TY, stride=32), :]
        )

    low, high = tu2[pl.ds(PITCH + 8, 1), :], tu2[pl.ds(TY * PITCH + 8, 1), :]
    left, right = pick(tv2[pl.ds(0, 1), :], 0), pick(tv2[pl.ds(31, 1), :], 3)
    corner_send[0] = pick(jnp.where(flip[1], high, low), 0)
    corner_send[1] = jnp.where(flip[3], right, left)
    corner_send[2] = pick(jnp.where(flip[1], low, high), 0)
    corner_send[3] = jnp.where(flip[3], left, right)

    def corner(start, size, index, direction, peer):
        at = pl.ds(start, size)
        return remote(corner_send.at[at], corner_recv.at[at], index, direction, peer)

    put_rows(1, part_row(0), part_row(TY - 1))
    put_columns(1, part_column(0), part_column(31))
    pl.semaphore_wait(barrier, len(greeted))
    corners = [
        corner(0, 2, 6, 0, diagonal[-17]), corner(2, 1, 6, 1, diagonal[15]), corner(3, 1, 6, 2, diagonal[-15]),
    ]
    for copy in corners:
        copy.start()
    tv_copy = remote(tv_send, tv_recv, 5, 2, south)
    tv_copy.start()
    tu_copy = remote(tu_send, tu_recv, 5, 0, west)
    tu_copy.start()
    parts = send_rows(1, put=False)
    send_columns(1, parts, put=False)
    copies = send_rows(0, put=False)
    send_columns(0, copies, put=False)
    tu_copy.wait_recv()
    tu2[column(32), :] = jnp.where(last_lanes, tu_recv[...], own_tu)
    copies[2].wait_recv()
    copies[3].wait_recv()
    take_columns(0, *own)

    zero = jnp.zeros((32, 128), F32)

    def first(i, total):
        q = q_buf[i]
        here = inner(i)
        below = i * 32 if isinstance(i, int) else pl.multiple_of(i * 32, 32)
        value = (
            tu2[here, :] - tu2[pl.ds(here.start + 1, 32), :]
            + tv2[pl.ds(below, 32), :] - tv2[pl.ds(below + 32, 32), :]
        )
        value = jnp.where(q > 0.0, value, 0.0)
        qsum[pl.ds(below, 32), :] = q * around(0, i) + (1.0 - shift)
        field[0, i] = value
        g_buf[1, here, :] = q * value
        return total + value * value

    def middle(body, start):
        return lax.fori_loop(1, TY - 1, body, start, unroll=UNROLL)

    n0 = middle(first, zero)
    tv_copy.wait_recv()
    tv2[pl.ds(TY * 32, 32), :] = tv_recv[...]
    copies[0].wait_recv()
    copies[1].wait_recv()
    n0 = first(TY - 1, first(0, n0))
    for copy in parts + corners:
        copy.wait_recv()
    row_shape = (32, 128)
    position = lanes(row_shape) // 32 * 32 + lax.broadcasted_iota(jnp.int32, row_shape, 0)

    def at_end(shape_position, flipped, last, value):
        return jnp.where(shape_position == jnp.where(flipped, 0, last), value, 0.0)

    north_ghost, south_ghost = pl.ds(17 * PITCH + 8, 32), pl.ds(8, 32)
    g_buf[1, north_ghost, :] = g_buf[0, north_ghost, :] * (
        row_recv[0, 0] - at_end(position, flip[2], TX - 1, corner_recv[0])
    )
    g_buf[1, south_ghost, :] = g_buf[0, south_ghost, :] * (
        row_recv[0, 1] - tv_row - at_end(position, flip[3], TX - 1, corner_recv[2])
    )
    index = lax.broadcasted_iota(jnp.int32, (TY, 128), 0)
    lane = lanes((TY, 128))
    from_east = edge_recv[1, 0] - at_end(index, flip[0], TY - 1, corner_recv[1])
    from_west = edge_recv[1, 1] - tu_column - at_end(index, flip[1], TY - 1, corner_recv[3])
    g_buf[1, column(32), :] = jnp.where(
        lane < 96, roll_lanes(g_buf[1, column(0), :], 96), g_buf[0, column(32), :] * from_east
    )
    g_buf[1, column(-1), :] = jnp.where(
        lane >= 32, roll_lanes(g_buf[1, column(31), :], 32), g_buf[0, column(-1), :] * from_west
    )

    def level_of(i):
        return pl.ds(i * 32 if isinstance(i, int) else pl.multiple_of(i * 32, 32), 32)

    def step_of(k):
        def step(i, totals):
            q, old = q_buf[i], field[k - 1, i]
            value = qsum[level_of(i), :] * old - q * around(k, i)
            field[k, i] = value
            if k < 4:
                g_buf[k + 1, inner(i), :] = q * value
            return (totals[0] + old * value, totals[1] + value * value) if k == 1 else totals

        return step

    def flat(k):
        return field.at[k].reshape(TY * 32, 128)

    def field_column(k, n):
        return flat(k)[pl.ds(n, TY, stride=32), :]

    def inside_columns(k):
        first_column, last_column = g_buf[k, column(0), :], g_buf[k, column(31), :]
        g_buf[k, column(32), :] = jnp.where(lane < 96, roll_lanes(first_column, 96), 0.0)
        g_buf[k, column(-1), :] = jnp.where(lane >= 32, roll_lanes(last_column, 32), 0.0)
        return first_column, last_column

    def add_ghosts(k, rows, columns):
        parts = (
            q_buf[TY - 1] * rows[0],
            q_buf[0] * rows[1],
            jnp.where(lane >= 96, g_buf[0, column(31), :] * columns[0], 0.0),
            jnp.where(lane < 32, g_buf[0, column(0), :] * columns[1], 0.0),
        )
        north_row = field[k, TY - 1] - parts[0]
        south_row = field[k, 0] - parts[1]
        field[k, TY - 1] = north_row
        field[k, 0] = south_row
        east_column = field_column(k, 31) - parts[2]
        west_column = field_column(k, 0) - parts[3]
        flat(k)[pl.ds(31, TY, stride=32), :] = east_column
        flat(k)[pl.ds(0, TY, stride=32), :] = west_column
        if k < 4:
            g_buf[k + 1, inner(0), :] = q_buf[0] * south_row
            g_buf[k + 1, inner(TY - 1), :] = q_buf[TY - 1] * north_row
            g_buf[k + 1, column(31), :] = g_buf[0, column(31), :] * east_column
            g_buf[k + 1, column(0), :] = g_buf[0, column(0), :] * west_column
        return parts

    def fan(buf, slot, peers, phase, which):
        def copy_to(peer):
            return pltpu.make_async_remote_copy(
                src_ref=buf.at[slot], dst_ref=buf.at[slot],
                send_sem=ar_send.at[which, phase], recv_sem=ar_recv.at[which, phase],
                device_id=(peer,), device_id_type=MESH,
            )

        for peer in peers:
            copy_to(peer).start()

    def fan_wait(buf, count, sem):
        pltpu.make_async_copy(buf.at[pl.ds(0, count)], buf.at[pl.ds(0, count)], sem).wait()

    def start_level(values, buf, which):
        buf[place] = values
        fan(buf, place, plane_peers, 0, which)

    def cross_levels(buf_a, buf_b, which):
        fan_wait(buf_a, PLANE - 1, ar_recv.at[which, 0])
        buf_b[level] = jnp.sum(buf_a[...], axis=0)
        fan(buf_b, level, level_peers, 1, which)

    def finish(buf_b, which):
        fan_wait(buf_b, DEPTH - 1, ar_recv.at[which, 1])
        return jnp.sum(buf_b[...], axis=0)

    step = step_of(1)
    totals = step(TY - 1, step(0, (zero, zero)))
    flight = send_rows(2)
    n1, n2 = middle(step, totals)
    first_column, last_column = inside_columns(2)
    send_columns(2, flight, first_column, last_column)
    start, end = pl.ds(PITCH + 8, 1), pl.ds(TY * PITCH + 8, 1)
    start_last, end_last = pl.ds(PITCH + 39, 1), pl.ds(TY * PITCH + 39, 1)
    p00, p10 = pick(g_buf[2, start, :], 0), pick(g_buf[2, end, :], 0)
    p01, p11 = pick(g_buf[2, start_last, :], 3), pick(g_buf[2, end_last, :], 3)
    corner_send[4] = jnp.where(flip[1], p10, p00)
    corner_send[5] = jnp.where(flip[3], p01, p00)
    corner_send[6] = jnp.where(flip[0], p11, p01)
    corner_send[7] = jnp.where(flip[3], p00, p01)
    corner_send[8] = jnp.where(flip[1], p00, p10)
    corner_send[9] = jnp.where(flip[2], p11, p10)
    corner_send[10] = jnp.where(flip[0], p01, p11)
    corner_send[11] = jnp.where(flip[2], p10, p11)
    more_corners = [
        corner(4 + 2 * n, 2, 7, n, diagonal[d]) for n, d in enumerate((-17, -15, 15, 17))
    ]
    for copy in more_corners:
        copy.start()
    start_level(pack_sums([n0, n1, n2, zero]), a1, 0)
    step = step_of(2)
    step(TY - 1, step(0, ()))
    seconds = send_rows(3, field[2, 0], field[2, TY - 1])
    middle(step, ())
    send_columns(3, seconds, field_column(2, 0), field_column(2, 31))

    own_rows = g_buf[2, inner(TY - 1), :], g_buf[2, inner(0), :]
    for copy in flight:
        copy.wait_recv()
    add_ghosts(2, (row_recv[1, 0], row_recv[1, 1]), (edge_recv[2, 0], edge_recv[2, 1]))
    for copy in seconds + more_corners:
        copy.wait_recv()

    def ends(shape_position, flipped, last, at_last, at_first):
        return at_end(shape_position, flipped, last, corner_recv[at_last]) + jnp.where(
            shape_position == jnp.where(flipped, last, 0), corner_recv[at_first], 0.0
        )

    for side, ghost, flipped, corner_slots in (
        (0, north_ghost, flip[2], (4, 6)),
        (1, south_ghost, flip[3], (8, 10)),
    ):
        q = g_buf[0, ghost, :]
        missing = own_rows[side] + ends(position, flipped, TX - 1, *corner_slots)
        g_buf[3, ghost, :] = q * (row_recv[2, side] - q * missing)
    q = g_buf[0, column(32), :]
    missing = last_column + ends(index, flip[0], TY - 1, 5, 9)
    g_buf[3, column(32), :] = jnp.where(
        lane < 96, roll_lanes(g_buf[3, column(0), :], 96), q * (edge_recv[3, 0] - q * missing)
    )
    q = g_buf[0, column(-1), :]
    missing = first_column + ends(index, flip[1], TY - 1, 7, 11)
    g_buf[3, column(-1), :] = jnp.where(
        lane >= 32, roll_lanes(g_buf[3, column(31), :], 32), q * (edge_recv[3, 1] - q * missing)
    )

    step = step_of(3)
    step(TY - 1, step(0, ()))
    flight = send_rows(4)
    cross_levels(a1, b1, 0)
    middle(step, ())
    send_columns(4, flight, *inside_columns(4))
    step = step_of(4)
    middle(step, step(TY - 1, step(0, ())))
    s0, s1, s2, _ = spread(finish(b1, 0))

    c = shift
    m1 = c * s0 + s1
    m2 = c * (c * s0 + 2.0 * s1) + s2
    alpha0 = s0 / m1
    rr1 = s0 - alpha0 * (2.0 * m1 - alpha0 * m2)
    beta0 = rr1 / s0
    e = (1.0 - alpha0 * c, -alpha0)
    f = (e[0] + beta0, -alpha0)
    wide_e = [jnp.broadcast_to(x, (32, 128)) for x in e]
    wide_f = [jnp.broadcast_to(x, (32, 128)) for x in f]

    def second(i, totals):
        v = [field[k, i] for k in range(5)]
        r = [wide_e[0] * v[k] + wide_e[1] * v[k + 1] for k in range(3)]
        d = [wide_f[0] * v[k] + wide_f[1] * v[k + 1] for k in range(4)]
        pairs = (
            (r[0], r[0]), (r[0], r[1]), (r[1], r[1]), (r[1], r[2]),
            (r[0], d[0]), (r[0], d[1]), (r[1], d[1]), (r[1], d[2]), (r[2], d[2]),
            (d[0], d[0]), (d[0], d[1]), (d[1], d[1]), (d[1], d[2]), (d[2], d[2]), (d[2], d[3]),
        )
        out = []
        for t, (x, y) in zip(totals, pairs):
            p = x * y
            out.append(t + (p[0:8] + p[8:16] + (p[16:24] + p[24:32])))
        return tuple(out)

    small = jnp.zeros((8, 128), F32)
    totals = lax.fori_loop(0, TY, second, (small,) * 15, unroll=2)
    for copy in flight:
        copy.wait_recv()
    north_part, south_part, east_part, west_part = add_ghosts(
        4, (row_recv[3, 0], row_recv[3, 1]), (edge_recv[4, 0], edge_recv[4, 1])
    )

    def second_image(low, high):
        n = low.shape[0]
        return wide_f[0][0:n] * low + wide_f[1][0:n] * high

    late_rows = north_part * second_image(field[2, TY - 1], field[3, TY - 1])
    late_rows = late_rows + south_part * second_image(field[2, 0], field[3, 0])
    late_columns = east_part * second_image(field_column(2, 31), field_column(3, 31))
    late_columns = late_columns + west_part * second_image(field_column(2, 0), field_column(3, 0))
    late = late_rows[0:16] + late_rows[16:32] + late_columns
    totals = totals[:14] + (totals[14] - wide_f[1][0:8] * (late[0:8] + late[8:16]), small)
    start_level(jnp.concatenate([fold(totals[4 * k : 4 * k + 4]) for k in range(4)], axis=0), a2, 1)

    def turn(n, carry):
        k, block = n // 4, lax.rem(n, 4)
        values = [field[k, 4 * block + i] for i in range(4)]
        t = jnp.transpose(jnp.concatenate(exchange_groups(values), axis=0))
        for i in range(4):
            turned[k, 4 * block + i] = t[32 * i : 32 * i + 32]
        return carry

    lax.fori_loop(0, 20, turn, 0, unroll=2)
    cross_levels(a2, b2, 1)
    sums = finish(b2, 1)
    sums = [x for k in range(4) for x in spread(sums[k : k + 1])]
    rho, sigma, delta = sums[:4], sums[4:9], sums[9:15]

    def dot(a, b):
        terms = []
        for one, other, table in ((a[0], b[0], rho), (a[0], b[1], sigma), (a[1], b[0], sigma), (a[1], b[1], delta)):
            for i, x in enumerate(one):
                inner_sum = functools.reduce(lambda p, n: p + n, [y * table[i + j] for j, y in enumerate(other)], 0.0)
                terms.append(x * inner_sum)
        return functools.reduce(lambda p, n: p + n, terms)

    def operate(a):
        def one(p):
            if not p:
                return []
            return [c * p[0]] + [p[i - 1] + c * p[i] for i in range(1, len(p))] + [p[-1]]

        return one(a[0]), one(a[1])

    def add(a, b, scale):
        def one(p, n):
            out = []
            for i in range(max(len(p), len(n))):
                terms = ([p[i]] if i < len(p) else []) + ([scale * n[i]] if i < len(n) else [])
                out.append(functools.reduce(lambda x, y: x + y, terms))
            return out

        return one(a[0], b[0]), one(a[1], b[1])

    unit = jnp.ones((1, 128), F32)
    residual, direction, answer = ([unit], []), ([], [unit]), ([], [])
    norm = rho[0]
    for k in range(3):
        image = operate(direction)
        alpha = norm / dot(direction, image)
        answer = add(answer, direction, alpha)
        residual = add(residual, image, -alpha)
        if k < 2:
            after = dot(residual, residual)
            direction = add(residual, direction, after / norm)
            norm = after

    def over_field(a, start, size):
        out = [start] + [None] * (size - 1)
        for values, (low_factor, high_factor) in zip(a, (e, f)):
            for k, x in enumerate(values):
                for n, term in ((k, x * low_factor), (k + 1, x * high_factor)):
                    out[n] = term if out[n] is None else out[n] + term
        return out

    rows = over_field(answer, alpha0, 4) + over_field(residual, None, 5)
    columns = jnp.transpose(jnp.concatenate(rows + [jnp.zeros((119, 128), F32)], axis=0))
    for k in range(9):
        factors[k] = jnp.broadcast_to(columns[0:MEMB, k : k + 1], (MEMB, TX))

    for copy in sent + corners + more_corners + [tv_copy, tu_copy]:
        copy.wait_send()
    fan_wait(a1, PLANE - 1, ar_send.at[0, 0])
    fan_wait(b1, DEPTH - 1, ar_send.at[0, 1])
    fan_wait(a2, PLANE - 1, ar_send.at[1, 0])
    fan_wait(b2, DEPTH - 1, ar_send.at[1, 1])


def combine(turned, factors, x_hbm, r_hbm, x_buf, r_buf, sem):
    copies = []
    for half in range(2):
        for which, (buf, hbm) in enumerate(((x_buf, x_hbm), (r_buf, r_hbm))):
            c = [factors[k] for k in range(9)][4 * which : 4 + 5 * which]
            for i in range(8):
                terms = [f * turned[k, 8 * half + i] for k, f in enumerate(c)]
                buf[half, pl.ds(i, MEMB, stride=8), :] = functools.reduce(lambda s, t: s + t, terms)
            copy = pltpu.make_async_copy(
                buf.at[half].reshape(MEMB, 8, TX), hbm.at[:, pl.ds(8 * half, 8)], sem.at[half, which]
            )
            copy.start()
            copies.append(copy)
    for copy in copies:
        copy.wait()


def on_device(zonal, meridional, fraction, thickness, land, codes):
    vmem = pl.BlockSpec(memory_space=pltpu.VMEM)
    hbm = pl.BlockSpec(memory_space=pltpu.HBM)
    arguments = [
        pltpu.with_memory_space_constraint(x, pltpu.HBM)
        for x in (zonal, meridional, fraction, thickness, land, codes)
    ]
    whole = jax.ShapeDtypeStruct((MEMB, TY, TX), F32)
    padded = (TY + 2) * PITCH
    turned, factors = pl.pallas_call(
        kernel,
        out_shape=(
            jax.ShapeDtypeStruct((5, TY, 32, 128), F32),
            jax.ShapeDtypeStruct((9, MEMB, TX), F32),
        ),
        in_specs=[hbm] * 6,
        out_specs=(vmem, vmem),
        scratch_shapes=[
            pltpu.VMEM((MEMB, LEV, TY, TX), jnp.bfloat16),
            pltpu.VMEM((MEMB, LEV, TY, TX), jnp.bfloat16),
            pltpu.VMEM((LEV, TY, TX), jnp.bfloat16),
            pltpu.SMEM((LEV,), F32),
            pltpu.VMEM((TY, TX), jnp.int32),
            pltpu.SMEM((1, 4), jnp.int32),
            pltpu.VMEM((MEMB * TY, TX), F32),
            pltpu.VMEM((MEMB * TY, TX), F32),
            pltpu.VMEM((LEV, TY, TX), F32),
            pltpu.VMEM((padded, 128), F32),
            pltpu.VMEM(((TY + 1) * 32, 128), F32),
            pltpu.VMEM((5, TY, 32, 128), F32),
            pltpu.VMEM((5, padded, 128), F32),
            pltpu.VMEM((TY, 32, 128), F32),
            pltpu.VMEM((TY * 32, 128), F32),
            pltpu.VMEM((TY, TX), F32),
            pltpu.VMEM((5, 4, 32, 128), F32),
            pltpu.VMEM((5, 2, TY, 128), F32),
            pltpu.VMEM((TY, 128), F32),
            pltpu.VMEM((TY, 128), F32),
            pltpu.VMEM((32, 128), F32),
            pltpu.VMEM((32, 128), F32),
            pltpu.VMEM((4, 2, 32, 128), F32),
            pltpu.VMEM((12, 1, 128), F32),
            pltpu.VMEM((12, 1, 128), F32),
            pltpu.VMEM((PLANE, 1, 128), F32),
            pltpu.VMEM((DEPTH, 1, 128), F32),
            pltpu.VMEM((PLANE, 4, 128), F32),
            pltpu.VMEM((DEPTH, 4, 128), F32),
            pltpu.SemaphoreType.DMA((2, CHUNKS)),
            pltpu.SemaphoreType.DMA((4,)),
            pltpu.SemaphoreType.DMA((8, 4)),
            pltpu.SemaphoreType.DMA((8, 4)),
            pltpu.SemaphoreType.DMA((2, 2)),
            pltpu.SemaphoreType.DMA((2, 2)),
        ],
        compiler_params=pltpu.CompilerParams(
            collective_id=0, has_side_effects=True, vmem_limit_bytes=40 << 20
        ),
    )(*arguments)
    return pl.pallas_call(
        combine,
        out_shape=(whole, whole),
        in_specs=[vmem] * 2,
        out_specs=(hbm, hbm),
        scratch_shapes=[
            pltpu.VMEM((2, MEMB * 8, TX), F32),
            pltpu.VMEM((2, MEMB * 8, TX), F32),
            pltpu.SemaphoreType.DMA((2, 2)),
        ],
        compiler_params=pltpu.CompilerParams(vmem_limit_bytes=16 << 20),
    )(turned, factors)


def solution(mesh):
    in_specs = (
        P(None, None, "tile", None),
        P(None, None, "tile", None),
        P(None, "tile", None),
        P(),
        P("tile", None),
        P("tile", None),
    )
    out_specs = (P(None, "tile", None), P(None, "tile", None))
    return jax.shard_map(
        on_device, mesh=mesh, in_specs=in_specs, out_specs=out_specs, check_vma=False
    )
```

```python
import functools

import jax
import jax.numpy as jnp
from jax import lax
from jax.experimental import pallas as pl
from jax.experimental.pallas import tpu as pltpu
from jax.sharding import PartitionSpec as P

MESH = pl.DeviceIdType.MESH
F32 = jnp.float32
MEMB, LEV, TY, TX = 32, 8, 16, 128
NTX = 16
PLANE, DEPTH = 32, 8
N_TILE = PLANE * DEPTH
PITCH = 48
UNROLL = 14
CHUNKS = 2


def lanes(shape):
    return lax.broadcasted_iota(jnp.int32, shape, len(shape) - 1)


def roll_lanes(x, shift):
    return pltpu.roll(x, shift % 128, axis=x.ndim - 1)


def exchange_groups(a):
    lane = lanes(a[0].shape)
    low = lane < 64
    even = (lane // 32) % 2 == 0
    b0 = jnp.where(low, a[0], roll_lanes(a[2], 64))
    b2 = jnp.where(low, roll_lanes(a[0], 64), a[2])
    b1 = jnp.where(low, a[1], roll_lanes(a[3], 64))
    b3 = jnp.where(low, roll_lanes(a[1], 64), a[3])
    return (
        jnp.where(even, b0, roll_lanes(b1, 32)),
        jnp.where(even, roll_lanes(b0, 96), b1),
        jnp.where(even, b2, roll_lanes(b3, 32)),
        jnp.where(even, roll_lanes(b2, 96), b3),
    )


def reverse8(x):
    place = lax.broadcasted_iota(jnp.int32, x.shape, 0)
    x = pltpu.roll(x, 4, axis=0)
    x = jnp.where(place % 4 < 2, pltpu.roll(x, 6, axis=0), pltpu.roll(x, 2, axis=0))
    return jnp.where(place % 2 < 1, pltpu.roll(x, 7, axis=0), pltpu.roll(x, 1, axis=0))


def reverse_rows(x):
    blocks = x.shape[0] // 8
    return jnp.concatenate(
        [reverse8(x[8 * k : 8 * k + 8]) for k in range(blocks - 1, -1, -1)], axis=0
    )


def reverse_columns(x):
    even = (lanes(x.shape) // 32) % 2 == 0
    return reverse_rows(jnp.where(even, roll_lanes(x, 32), roll_lanes(x, 96)))


def pack_sums(p):
    return fold([x[0:8] + x[8:16] + (x[16:24] + x[24:32]) for x in p])


def fold(p):
    lane = lanes(p[0].shape)
    low = lane < 64
    even = (lane // 32) % 2 == 0
    x = jnp.where(low, p[0] + roll_lanes(p[0], 64), p[2] + roll_lanes(p[2], 64))
    y = jnp.where(low, p[1] + roll_lanes(p[1], 64), p[3] + roll_lanes(p[3], 64))
    z = jnp.where(even, x + roll_lanes(x, 96), y + roll_lanes(y, 32))
    return jnp.sum(z, axis=0, keepdims=True)


def spread(row):
    lane = lanes(row.shape)
    out = []
    for k in range(4):
        x = jnp.where(lane // 32 == k, row, 0.0)
        x = x + roll_lanes(x, 64)
        out.append(x + roll_lanes(x, 32))
    return out


def pick(row, group):
    row = jnp.where(lanes(row.shape) // 32 == group, row, 0.0)
    row = row + roll_lanes(row, 64)
    return row + roll_lanes(row, 32)


def kernel(
    u_hbm, v_hbm, fraction_hbm, thickness_hbm, land_hbm, codes_hbm, turned, factors,
    u_buf, v_buf, fraction, thickness, land, codes, tu1, tv1, weight, tu2, tv2, field, g_buf, q_buf, qsum, stage,
    edge_send, edge_recv, tu_send, tu_recv, tv_send, tv_recv, row_recv,
    corner_send, corner_recv, a1, b1, a2, b2,
    load_sem, small_sem, send_sem, recv_sem, ar_send, ar_recv,
):
    me = lax.axis_index("tile")
    east, west = lax.rem(me + 1, N_TILE), lax.rem(me + N_TILE - 1, N_TILE)
    north, south = lax.rem(me + NTX, N_TILE), lax.rem(me + N_TILE - NTX, N_TILE)
    diagonal = {n: lax.rem(me + N_TILE + n, N_TILE) for n in (-17, -15, 15, 17)}
    level, place = me // PLANE, lax.rem(me, PLANE)
    ys = [level * PLANE + 8 * lax.rem(place // 8 + d, 4) for d in range(4)]
    xs = [2 * lax.rem(place // 2 + d, 4) for d in range(4)]
    cores = [lax.rem(place + d, 2) for d in range(2)]
    offsets = sorted(
        ((y, x, c) for y in range(4) for x in range(4) for c in range(2) if (y, x, c) != (0, 0, 0)),
        key=lambda o: -(min(o[0], 4 - o[0]) + min(o[1], 4 - o[1])),
    )
    plane_peers = [ys[y] + xs[x] + cores[c] for y, x, c in offsets]
    level_peers = [lax.rem(level + d, DEPTH) * PLANE + place for d in (4, 3, 5, 2, 6, 1, 7)]

    small_loads = []
    pairs = ((thickness_hbm, thickness), (codes_hbm, codes), (fraction_hbm, fraction), (land_hbm, land))
    for n, (src, dst) in enumerate(pairs):
        copy = pltpu.make_async_copy(src, dst, small_sem.at[n])
        copy.start()
        small_loads.append(copy)
    part = MEMB // CHUNKS
    loads = []
    for c in range(CHUNKS):
        for n, (src, dst) in enumerate(((u_hbm, u_buf), (v_hbm, v_buf))):
            at = pl.ds(c * part, part)
            copy = pltpu.make_async_copy(src.at[at], dst.at[at], load_sem.at[n, c])
            copy.start()
            loads.append(copy)

    barrier = pltpu.get_barrier_semaphore()
    greeted = [east, west, north, south] + list(diagonal.values()) + plane_peers + level_peers
    for peer in greeted:
        pl.semaphore_signal(barrier, inc=1, device_id=(peer,), device_id_type=MESH)

    for copy in small_loads:
        copy.wait()
    flip = [codes[0, k] == 1 for k in range(4)]

    total = thickness[0]
    for k in range(1, LEV):
        total = total + thickness[k]
    shift = 1.0 + 0.125 * total

    depth = None
    for k in range(LEV):
        w = thickness[k] * fraction[k].astype(F32)
        weight[k] = w
        depth = w if depth is None else depth + w
    root = 0.5 * jnp.sqrt(land[...].astype(F32) * depth)
    stage[...] = root

    def to_groups(rows_of, store):
        for block in range(4):
            z = jnp.concatenate([rows_of(4 * block + k) for k in range(4)], axis=0)
            t = jnp.transpose(z)
            out = exchange_groups([t[32 * g : 32 * g + 32] for g in range(4)])
            for k in range(4):
                store(4 * block + k, out[k])

    def inner(i):
        start = (i + 1) * PITCH + 8
        if not isinstance(i, int):
            start = pl.multiple_of(start, 8)
        return pl.ds(start, 32)

    def column(s):
        return pl.ds(PITCH + 8 + s, TY, stride=PITCH)

    def store_q(i, value):
        q_buf[i] = value
        g_buf[0, inner(i), :] = value

    to_groups(lambda i: jnp.broadcast_to(stage[pl.ds(i, 1), :], (MEMB, TX)), store_q)

    def column_sums(src, dst, n, c):
        loads[2 * c + n].wait()

        def member(m, carry):
            total = weight[0] * src[m, 0].astype(F32)
            for k in range(1, LEV):
                total = total + weight[k] * src[m, k].astype(F32)
            dst[pl.ds(pl.multiple_of(m * TY, TY), TY), :] = total
            return carry

        lax.fori_loop(c * part, (c + 1) * part, member, 0, unroll=4)

    def remote(src, dst, index, direction, peer):
        return pltpu.make_async_remote_copy(
            src_ref=src, dst_ref=dst,
            send_sem=send_sem.at[index, direction], recv_sem=recv_sem.at[index, direction],
            device_id=(peer,), device_id_type=MESH,
        )

    def edges(k):
        if k == 0:
            from_north, from_south = g_buf.at[0, pl.ds(17 * PITCH + 8, 32)], g_buf.at[0, pl.ds(8, 32)]
        else:
            from_north, from_south = row_recv.at[k - 1, 0], row_recv.at[k - 1, 1]
        return [
            remote(edge_send.at[k, 2], from_north, k, 2, south),
            remote(edge_send.at[k, 3], from_south, k, 3, north),
            remote(edge_send.at[k, 0, pl.ds(0, TY)], edge_recv.at[k, 0], k, 0, west),
            remote(edge_send.at[k, 1, pl.ds(0, TY)], edge_recv.at[k, 1], k, 1, east),
        ]

    def put_rows(k, low=None, high=None):
        if low is None:
            low, high = g_buf[k, inner(0), :], g_buf[k, inner(TY - 1), :]
        edge_send[k, 2] = jnp.where(flip[3], reverse_columns(low), low)
        edge_send[k, 3] = jnp.where(flip[2], reverse_columns(high), high)

    def put_columns(k, first=None, last=None):
        if first is None:
            first, last = g_buf[k, column(0), :], g_buf[k, column(31), :]
        to_west = roll_lanes(first, 96)
        to_east = roll_lanes(last, 32)
        edge_send[k, 0, pl.ds(0, TY)] = jnp.where(flip[1], reverse_rows(to_west), to_west)
        edge_send[k, 1, pl.ds(0, TY)] = jnp.where(flip[0], reverse_rows(to_east), to_east)
        return to_west, to_east

    def take_columns(k, to_west, to_east):
        lane = lanes(to_west.shape)
        g_buf[k, column(32), :] = jnp.where(lane < 96, to_west, edge_recv[k, 0])
        g_buf[k, column(-1), :] = jnp.where(lane >= 32, to_east, edge_recv[k, 1])

    sent = []
    blank = jnp.zeros((32, 128), F32)
    for k in range(2, 5):
        if k != 3:
            g_buf[k, pl.ds(8, 32), :] = blank
            g_buf[k, pl.ds(17 * PITCH + 8, 32), :] = blank

    def send_rows(k, *values, put=True):
        if put:
            put_rows(k, *values)
        copies = edges(k)
        copies[0].start()
        copies[1].start()
        sent.extend(copies)
        return copies

    def send_columns(k, copies, *values, put=True):
        own = put_columns(k, *values) if put else None
        copies[2].start()
        copies[3].start()
        return own

    def around(k, i):
        here = inner(i)
        base = here.start
        return (g_buf[k, pl.ds(base + 1, 32), :] + g_buf[k, pl.ds(base - 1, 32), :]) + (
            g_buf[k, inner(i + 1), :] + g_buf[k, inner(i - 1), :]
        )

    put_rows(0)
    own = put_columns(0)
    for c in range(CHUNKS):
        column_sums(u_buf, tu1, 0, c)
        column_sums(v_buf, tv1, 1, c)

    def store_tu(i, value):
        tu2[inner(i), :] = value

    def store_tv(i, value):
        tv2[pl.ds(i * 32, 32), :] = value

    to_groups(lambda i: tv1[pl.ds(i, MEMB, stride=TY), :], store_tv)
    to_groups(lambda i: tu1[pl.ds(i, MEMB, stride=TY), :], store_tu)

    tv_row = tv2[pl.ds(0, 32), :]
    tv_send[...] = jnp.where(flip[3], reverse_columns(tv_row), tv_row)
    tu_column = tu2[column(0), :]
    own_tu = roll_lanes(tu_column, 96)
    tu_send[...] = jnp.where(flip[1], reverse_rows(own_tu), own_tu)
    last_lanes = lanes(own_tu.shape) >= 96
    tu2[column(32), :] = jnp.where(last_lanes, 0.0, own_tu)
    tv2[pl.ds(TY * 32, 32), :] = jnp.zeros((32, 128), F32)

    def part_row(i):
        here, below = inner(i), i * 32
        return (
            tu2[here, :] - tu2[pl.ds(here.start + 1, 32), :]
            + tv2[pl.ds(below, 32), :] - tv2[pl.ds(below + 32, 32), :]
        )

    def part_column(n):
        return (
            tu2[column(n), :] - tu2[column(n + 1), :]
            + tv2[pl.ds(n, TY, stride=32), :] - tv2[pl.ds(n + 32, TY, stride=32), :]
        )

    low, high = tu2[pl.ds(PITCH + 8, 1), :], tu2[pl.ds(TY * PITCH + 8, 1), :]
    left, right = pick(tv2[pl.ds(0, 1), :], 0), pick(tv2[pl.ds(31, 1), :], 3)
    corner_send[0] = pick(jnp.where(flip[1], high, low), 0)
    corner_send[1] = jnp.where(flip[3], right, left)
    corner_send[2] = pick(jnp.where(flip[1], low, high), 0)
    corner_send[3] = jnp.where(flip[3], left, right)

    def corner(start, size, index, direction, peer):
        at = pl.ds(start, size)
        return remote(corner_send.at[at], corner_recv.at[at], index, direction, peer)

    put_rows(1, part_row(0), part_row(TY - 1))
    put_columns(1, part_column(0), part_column(31))
    pl.semaphore_wait(barrier, len(greeted))
    corners = [
        corner(0, 2, 6, 0, diagonal[-17]), corner(2, 1, 6, 1, diagonal[15]), corner(3, 1, 6, 2, diagonal[-15]),
    ]
    for copy in corners:
        copy.start()
    tv_copy = remote(tv_send, tv_recv, 5, 2, south)
    tv_copy.start()
    tu_copy = remote(tu_send, tu_recv, 5, 0, west)
    tu_copy.start()
    parts = send_rows(1, put=False)
    send_columns(1, parts, put=False)
    copies = send_rows(0, put=False)
    send_columns(0, copies, put=False)
    tu_copy.wait_recv()
    tu2[column(32), :] = jnp.where(last_lanes, tu_recv[...], own_tu)
    copies[2].wait_recv()
    copies[3].wait_recv()
    take_columns(0, *own)

    zero = jnp.zeros((32, 128), F32)

    def first(i, total):
        q = q_buf[i]
        here = inner(i)
        below = i * 32 if isinstance(i, int) else pl.multiple_of(i * 32, 32)
        value = (
            tu2[here, :] - tu2[pl.ds(here.start + 1, 32), :]
            + tv2[pl.ds(below, 32), :] - tv2[pl.ds(below + 32, 32), :]
        )
        value = jnp.where(q > 0.0, value, 0.0)
        qsum[pl.ds(below, 32), :] = q * around(0, i) + (1.0 - shift)
        field[0, i] = value
        g_buf[1, here, :] = q * value
        return total + value * value

    def middle(body, start):
        return lax.fori_loop(1, TY - 1, body, start, unroll=UNROLL)

    n0 = middle(first, zero)
    tv_copy.wait_recv()
    tv2[pl.ds(TY * 32, 32), :] = tv_recv[...]
    copies[0].wait_recv()
    copies[1].wait_recv()
    n0 = first(TY - 1, first(0, n0))
    for copy in parts + corners:
        copy.wait_recv()
    row_shape = (32, 128)
    position = lanes(row_shape) // 32 * 32 + lax.broadcasted_iota(jnp.int32, row_shape, 0)

    def at_end(shape_position, flipped, last, value):
        return jnp.where(shape_position == jnp.where(flipped, 0, last), value, 0.0)

    north_ghost, south_ghost = pl.ds(17 * PITCH + 8, 32), pl.ds(8, 32)
    g_buf[1, north_ghost, :] = g_buf[0, north_ghost, :] * (
        row_recv[0, 0] - at_end(position, flip[2], TX - 1, corner_recv[0])
    )
    g_buf[1, south_ghost, :] = g_buf[0, south_ghost, :] * (
        row_recv[0, 1] - tv_row - at_end(position, flip[3], TX - 1, corner_recv[2])
    )
    index = lax.broadcasted_iota(jnp.int32, (TY, 128), 0)
    lane = lanes((TY, 128))
    from_east = edge_recv[1, 0] - at_end(index, flip[0], TY - 1, corner_recv[1])
    from_west = edge_recv[1, 1] - tu_column - at_end(index, flip[1], TY - 1, corner_recv[3])
    g_buf[1, column(32), :] = jnp.where(
        lane < 96, roll_lanes(g_buf[1, column(0), :], 96), g_buf[0, column(32), :] * from_east
    )
    g_buf[1, column(-1), :] = jnp.where(
        lane >= 32, roll_lanes(g_buf[1, column(31), :], 32), g_buf[0, column(-1), :] * from_west
    )

    def level_of(i):
        return pl.ds(i * 32 if isinstance(i, int) else pl.multiple_of(i * 32, 32), 32)

    def step_of(k):
        def step(i, totals):
            q, old = q_buf[i], field[k - 1, i]
            value = qsum[level_of(i), :] * old - q * around(k, i)
            field[k, i] = value
            if k < 4:
                g_buf[k + 1, inner(i), :] = q * value
            return (totals[0] + old * value, totals[1] + value * value) if k == 1 else totals

        return step

    def flat(k):
        return field.at[k].reshape(TY * 32, 128)

    def field_column(k, n):
        return flat(k)[pl.ds(n, TY, stride=32), :]

    def inside_columns(k):
        first_column, last_column = g_buf[k, column(0), :], g_buf[k, column(31), :]
        g_buf[k, column(32), :] = jnp.where(lane < 96, roll_lanes(first_column, 96), 0.0)
        g_buf[k, column(-1), :] = jnp.where(lane >= 32, roll_lanes(last_column, 32), 0.0)
        return first_column, last_column

    def add_ghosts(k, rows, columns):
        parts = (
            q_buf[TY - 1] * rows[0],
            q_buf[0] * rows[1],
            jnp.where(lane >= 96, g_buf[0, column(31), :] * columns[0], 0.0),
            jnp.where(lane < 32, g_buf[0, column(0), :] * columns[1], 0.0),
        )
        north_row = field[k, TY - 1] - parts[0]
        south_row = field[k, 0] - parts[1]
        field[k, TY - 1] = north_row
        field[k, 0] = south_row
        east_column = field_column(k, 31) - parts[2]
        west_column = field_column(k, 0) - parts[3]
        flat(k)[pl.ds(31, TY, stride=32), :] = east_column
        flat(k)[pl.ds(0, TY, stride=32), :] = west_column
        if k < 4:
            g_buf[k + 1, inner(0), :] = q_buf[0] * south_row
            g_buf[k + 1, inner(TY - 1), :] = q_buf[TY - 1] * north_row
            g_buf[k + 1, column(31), :] = g_buf[0, column(31), :] * east_column
            g_buf[k + 1, column(0), :] = g_buf[0, column(0), :] * west_column
        return parts

    def fan(buf, slot, peers, phase, which):
        def copy_to(peer):
            return pltpu.make_async_remote_copy(
                src_ref=buf.at[slot], dst_ref=buf.at[slot],
                send_sem=ar_send.at[which, phase], recv_sem=ar_recv.at[which, phase],
                device_id=(peer,), device_id_type=MESH,
            )

        for peer in peers:
            copy_to(peer).start()

    def fan_wait(buf, count, sem):
        pltpu.make_async_copy(buf.at[pl.ds(0, count)], buf.at[pl.ds(0, count)], sem).wait()

    def start_level(values, buf, which):
        buf[place] = values
        fan(buf, place, plane_peers, 0, which)

    def cross_levels(buf_a, buf_b, which):
        fan_wait(buf_a, PLANE - 1, ar_recv.at[which, 0])
        buf_b[level] = jnp.sum(buf_a[...], axis=0)
        fan(buf_b, level, level_peers, 1, which)

    def finish(buf_b, which):
        fan_wait(buf_b, DEPTH - 1, ar_recv.at[which, 1])
        return jnp.sum(buf_b[...], axis=0)

    step = step_of(1)
    totals = step(TY - 1, step(0, (zero, zero)))
    flight = send_rows(2)
    n1, n2 = middle(step, totals)
    first_column, last_column = inside_columns(2)
    send_columns(2, flight, first_column, last_column)
    start, end = pl.ds(PITCH + 8, 1), pl.ds(TY * PITCH + 8, 1)
    start_last, end_last = pl.ds(PITCH + 39, 1), pl.ds(TY * PITCH + 39, 1)
    p00, p10 = pick(g_buf[2, start, :], 0), pick(g_buf[2, end, :], 0)
    p01, p11 = pick(g_buf[2, start_last, :], 3), pick(g_buf[2, end_last, :], 3)
    corner_send[4] = jnp.where(flip[1], p10, p00)
    corner_send[5] = jnp.where(flip[3], p01, p00)
    corner_send[6] = jnp.where(flip[0], p11, p01)
    corner_send[7] = jnp.where(flip[3], p00, p01)
    corner_send[8] = jnp.where(flip[1], p00, p10)
    corner_send[9] = jnp.where(flip[2], p11, p10)
    corner_send[10] = jnp.where(flip[0], p01, p11)
    corner_send[11] = jnp.where(flip[2], p10, p11)
    more_corners = [
        corner(4 + 2 * n, 2, 7, n, diagonal[d]) for n, d in enumerate((-17, -15, 15, 17))
    ]
    for copy in more_corners:
        copy.start()
    start_level(pack_sums([n0, n1, n2, zero]), a1, 0)
    step = step_of(2)
    step(TY - 1, step(0, ()))
    seconds = send_rows(3, field[2, 0], field[2, TY - 1])
    middle(step, ())
    send_columns(3, seconds, field_column(2, 0), field_column(2, 31))

    own_rows = g_buf[2, inner(TY - 1), :], g_buf[2, inner(0), :]
    for copy in flight:
        copy.wait_recv()
    add_ghosts(2, (row_recv[1, 0], row_recv[1, 1]), (edge_recv[2, 0], edge_recv[2, 1]))
    for copy in seconds + more_corners:
        copy.wait_recv()

    def ends(shape_position, flipped, last, at_last, at_first):
        return at_end(shape_position, flipped, last, corner_recv[at_last]) + jnp.where(
            shape_position == jnp.where(flipped, last, 0), corner_recv[at_first], 0.0
        )

    for side, ghost, flipped, corner_slots in (
        (0, north_ghost, flip[2], (4, 6)),
        (1, south_ghost, flip[3], (8, 10)),
    ):
        q = g_buf[0, ghost, :]
        missing = own_rows[side] + ends(position, flipped, TX - 1, *corner_slots)
        g_buf[3, ghost, :] = q * (row_recv[2, side] - q * missing)
    q = g_buf[0, column(32), :]
    missing = last_column + ends(index, flip[0], TY - 1, 5, 9)
    g_buf[3, column(32), :] = jnp.where(
        lane < 96, roll_lanes(g_buf[3, column(0), :], 96), q * (edge_recv[3, 0] - q * missing)
    )
    q = g_buf[0, column(-1), :]
    missing = first_column + ends(index, flip[1], TY - 1, 7, 11)
    g_buf[3, column(-1), :] = jnp.where(
        lane >= 32, roll_lanes(g_buf[3, column(31), :], 32), q * (edge_recv[3, 1] - q * missing)
    )

    step = step_of(3)
    step(TY - 1, step(0, ()))
    flight = send_rows(4)
    cross_levels(a1, b1, 0)
    middle(step, ())
    send_columns(4, flight, *inside_columns(4))
    step = step_of(4)
    middle(step, step(TY - 1, step(0, ())))
    s0, s1, s2, _ = spread(finish(b1, 0))

    c = shift
    m1 = c * s0 + s1
    m2 = c * (c * s0 + 2.0 * s1) + s2
    alpha0 = s0 / m1
    rr1 = s0 - alpha0 * (2.0 * m1 - alpha0 * m2)
    beta0 = rr1 / s0
    e = (1.0 - alpha0 * c, -alpha0)
    f = (e[0] + beta0, -alpha0)
    wide_e = [jnp.broadcast_to(x, (32, 128)) for x in e]
    wide_f = [jnp.broadcast_to(x, (32, 128)) for x in f]

    def second(i, totals):
        v = [field[k, i] for k in range(5)]
        r = [wide_e[0] * v[k] + wide_e[1] * v[k + 1] for k in range(3)]
        d = [wide_f[0] * v[k] + wide_f[1] * v[k + 1] for k in range(4)]
        pairs = (
            (r[0], r[0]), (r[0], r[1]), (r[1], r[1]), (r[1], r[2]),
            (r[0], d[0]), (r[0], d[1]), (r[1], d[1]), (r[1], d[2]), (r[2], d[2]),
            (d[0], d[0]), (d[0], d[1]), (d[1], d[1]), (d[1], d[2]), (d[2], d[2]), (d[2], d[3]),
        )
        out = []
        for t, (x, y) in zip(totals, pairs):
            p = x * y
            out.append(t + (p[0:8] + p[8:16] + (p[16:24] + p[24:32])))
        return tuple(out)

    small = jnp.zeros((8, 128), F32)
    totals = lax.fori_loop(0, TY, second, (small,) * 15, unroll=4)
    for copy in flight:
        copy.wait_recv()
    north_part, south_part, east_part, west_part = add_ghosts(
        4, (row_recv[3, 0], row_recv[3, 1]), (edge_recv[4, 0], edge_recv[4, 1])
    )

    def second_image(low, high):
        n = low.shape[0]
        return wide_f[0][0:n] * low + wide_f[1][0:n] * high

    late_rows = north_part * second_image(field[2, TY - 1], field[3, TY - 1])
    late_rows = late_rows + south_part * second_image(field[2, 0], field[3, 0])
    late_columns = east_part * second_image(field_column(2, 31), field_column(3, 31))
    late_columns = late_columns + west_part * second_image(field_column(2, 0), field_column(3, 0))
    late = late_rows[0:16] + late_rows[16:32] + late_columns
    totals = totals[:14] + (totals[14] - wide_f[1][0:8] * (late[0:8] + late[8:16]), small)
    start_level(jnp.concatenate([fold(totals[4 * k : 4 * k + 4]) for k in range(4)], axis=0), a2, 1)

    def turn(n, carry):
        k, block = n // 4, lax.rem(n, 4)
        values = [field[k, 4 * block + i] for i in range(4)]
        t = jnp.transpose(jnp.concatenate(exchange_groups(values), axis=0))
        for i in range(4):
            turned[k, 4 * block + i] = t[32 * i : 32 * i + 32]
        return carry

    lax.fori_loop(0, 20, turn, 0, unroll=2)
    cross_levels(a2, b2, 1)
    sums = finish(b2, 1)
    sums = [x for k in range(4) for x in spread(sums[k : k + 1])]
    rho, sigma, delta = sums[:4], sums[4:9], sums[9:15]

    def dot(a, b):
        terms = []
        for one, other, table in ((a[0], b[0], rho), (a[0], b[1], sigma), (a[1], b[0], sigma), (a[1], b[1], delta)):
            for i, x in enumerate(one):
                inner_sum = functools.reduce(lambda p, n: p + n, [y * table[i + j] for j, y in enumerate(other)], 0.0)
                terms.append(x * inner_sum)
        return functools.reduce(lambda p, n: p + n, terms)

    def operate(a):
        def one(p):
            if not p:
                return []
            return [c * p[0]] + [p[i - 1] + c * p[i] for i in range(1, len(p))] + [p[-1]]

        return one(a[0]), one(a[1])

    def add(a, b, scale):
        def one(p, n):
            out = []
            for i in range(max(len(p), len(n))):
                terms = ([p[i]] if i < len(p) else []) + ([scale * n[i]] if i < len(n) else [])
                out.append(functools.reduce(lambda x, y: x + y, terms))
            return out

        return one(a[0], b[0]), one(a[1], b[1])

    unit = jnp.ones((1, 128), F32)
    residual, direction, answer = ([unit], []), ([], [unit]), ([], [])
    norm = rho[0]
    for k in range(3):
        image = operate(direction)
        alpha = norm / dot(direction, image)
        answer = add(answer, direction, alpha)
        residual = add(residual, image, -alpha)
        if k < 2:
            after = dot(residual, residual)
            direction = add(residual, direction, after / norm)
            norm = after

    def over_field(a, start, size):
        out = [start] + [None] * (size - 1)
        for values, (low_factor, high_factor) in zip(a, (e, f)):
            for k, x in enumerate(values):
                for n, term in ((k, x * low_factor), (k + 1, x * high_factor)):
                    out[n] = term if out[n] is None else out[n] + term
        return out

    rows = over_field(answer, alpha0, 4) + over_field(residual, None, 5)
    columns = jnp.transpose(jnp.concatenate(rows + [jnp.zeros((119, 128), F32)], axis=0))
    for k in range(9):
        factors[k] = jnp.broadcast_to(columns[0:MEMB, k : k + 1], (MEMB, TX))

    for copy in sent + corners + more_corners + [tv_copy, tu_copy]:
        copy.wait_send()
    fan_wait(a1, PLANE - 1, ar_send.at[0, 0])
    fan_wait(b1, DEPTH - 1, ar_send.at[0, 1])
    fan_wait(a2, PLANE - 1, ar_send.at[1, 0])
    fan_wait(b2, DEPTH - 1, ar_send.at[1, 1])


def combine(turned, factors, x_hbm, r_hbm, x_buf, r_buf, sem):
    copies = []
    for half in range(2):
        for which, (buf, hbm) in enumerate(((x_buf, x_hbm), (r_buf, r_hbm))):
            c = [factors[k] for k in range(9)][4 * which : 4 + 5 * which]
            for i in range(8):
                terms = [f * turned[k, 8 * half + i] for k, f in enumerate(c)]
                buf[half, pl.ds(i, MEMB, stride=8), :] = functools.reduce(lambda s, t: s + t, terms)
            copy = pltpu.make_async_copy(
                buf.at[half].reshape(MEMB, 8, TX), hbm.at[:, pl.ds(8 * half, 8)], sem.at[half, which]
            )
            copy.start()
            copies.append(copy)
    for copy in copies:
        copy.wait()


def on_device(zonal, meridional, fraction, thickness, land, codes):
    vmem = pl.BlockSpec(memory_space=pltpu.VMEM)
    hbm = pl.BlockSpec(memory_space=pltpu.HBM)
    arguments = [
        pltpu.with_memory_space_constraint(x, pltpu.HBM)
        for x in (zonal, meridional, fraction, thickness, land, codes)
    ]
    whole = jax.ShapeDtypeStruct((MEMB, TY, TX), F32)
    padded = (TY + 2) * PITCH
    turned, factors = pl.pallas_call(
        kernel,
        out_shape=(
            jax.ShapeDtypeStruct((5, TY, 32, 128), F32),
            jax.ShapeDtypeStruct((9, MEMB, TX), F32),
        ),
        in_specs=[hbm] * 6,
        out_specs=(vmem, vmem),
        scratch_shapes=[
            pltpu.VMEM((MEMB, LEV, TY, TX), jnp.bfloat16),
            pltpu.VMEM((MEMB, LEV, TY, TX), jnp.bfloat16),
            pltpu.VMEM((LEV, TY, TX), jnp.bfloat16),
            pltpu.SMEM((LEV,), F32),
            pltpu.VMEM((TY, TX), jnp.int32),
            pltpu.SMEM((1, 4), jnp.int32),
            pltpu.VMEM((MEMB * TY, TX), F32),
            pltpu.VMEM((MEMB * TY, TX), F32),
            pltpu.VMEM((LEV, TY, TX), F32),
            pltpu.VMEM((padded, 128), F32),
            pltpu.VMEM(((TY + 1) * 32, 128), F32),
            pltpu.VMEM((5, TY, 32, 128), F32),
            pltpu.VMEM((5, padded, 128), F32),
            pltpu.VMEM((TY, 32, 128), F32),
            pltpu.VMEM((TY * 32, 128), F32),
            pltpu.VMEM((TY, TX), F32),
            pltpu.VMEM((5, 4, 32, 128), F32),
            pltpu.VMEM((5, 2, TY, 128), F32),
            pltpu.VMEM((TY, 128), F32),
            pltpu.VMEM((TY, 128), F32),
            pltpu.VMEM((32, 128), F32),
            pltpu.VMEM((32, 128), F32),
            pltpu.VMEM((4, 2, 32, 128), F32),
            pltpu.VMEM((12, 1, 128), F32),
            pltpu.VMEM((12, 1, 128), F32),
            pltpu.VMEM((PLANE, 1, 128), F32),
            pltpu.VMEM((DEPTH, 1, 128), F32),
            pltpu.VMEM((PLANE, 4, 128), F32),
            pltpu.VMEM((DEPTH, 4, 128), F32),
            pltpu.SemaphoreType.DMA((2, CHUNKS)),
            pltpu.SemaphoreType.DMA((4,)),
            pltpu.SemaphoreType.DMA((8, 4)),
            pltpu.SemaphoreType.DMA((8, 4)),
            pltpu.SemaphoreType.DMA((2, 2)),
            pltpu.SemaphoreType.DMA((2, 2)),
        ],
        compiler_params=pltpu.CompilerParams(
            collective_id=0, has_side_effects=True, vmem_limit_bytes=40 << 20
        ),
    )(*arguments)
    return pl.pallas_call(
        combine,
        out_shape=(whole, whole),
        in_specs=[vmem] * 2,
        out_specs=(hbm, hbm),
        scratch_shapes=[
            pltpu.VMEM((2, MEMB * 8, TX), F32),
            pltpu.VMEM((2, MEMB * 8, TX), F32),
            pltpu.SemaphoreType.DMA((2, 2)),
        ],
        compiler_params=pltpu.CompilerParams(vmem_limit_bytes=16 << 20),
    )(turned, factors)


def solution(mesh):
    in_specs = (
        P(None, None, "tile", None),
        P(None, None, "tile", None),
        P(None, "tile", None),
        P(),
        P("tile", None),
        P("tile", None),
    )
    out_specs = (P(None, "tile", None), P(None, "tile", None))
    return jax.shard_map(
        on_device, mesh=mesh, in_specs=in_specs, out_specs=out_specs, check_vma=False
    )
```
